32 devices in a mesh: ctx: 8 (over z, y), wt: 4 (over x, core).
Axes of the slice: x: 2, y: 2, z: 4, core: 2. Of those that a mesh axis runs over, the one named last changes fastest.
Arguments:
- hidden_in: bfloat16 [2, 4096, 1792], P(None, 'ctx', 'wt'), may hold values from -6 to 6
- lengths: int32 [2], replicated, may hold values from 1024 to 4096, as said below
- gain_attn: bfloat16 [1792], P('wt'), may hold values from 0.5 to 1.5
- gain_ffn: bfloat16 [1792], P('wt'), may hold values from 0.5 to 1.5
- w_query: bfloat16 [1792, 256], P('ctx', 'wt'), may hold values from -0.125 to 0.125
- w_key: bfloat16 [1792, 256], P('ctx', 'wt'), may hold values from -0.125 to 0.125
- w_value: bfloat16 [1792, 1792], P('ctx', 'wt'), may hold values from -0.125 to 0.125
- w_output: bfloat16 [1792, 1792], P('wt', 'ctx'), may hold values from -6 to 6
- w_gate: bfloat16 [1792, 4864], P('ctx', 'wt'), may hold values from -0.125 to 0.125
- w_up: bfloat16 [1792, 4864], P('ctx', 'wt'), may hold values from -0.125 to 0.125
- w_down: bfloat16 [4864, 1792], P('wt', 'ctx'), may hold values from -0.078125 to 0.078125
- cotangent: bfloat16 [2, 4096, 1792], P(None, 'ctx', 'wt'), may hold values from -6 to 6
Outputs:
- layer_out: bfloat16 [2, 4096, 1792], P(None, 'ctx', 'wt')
- grad_input: float32 [2, 4096, 1792], P(None, 'ctx', 'wt')
- grad_gain_attn: float32 [1792], P('wt')
- grad_gain_ffn: float32 [1792], P('wt')
- grad_query: float32 [1792, 256], P('ctx', 'wt')
- grad_key: float32 [1792, 256], P('ctx', 'wt')
- grad_value: float32 [1792, 1792], P('ctx', 'wt')
- grad_output: float32 [1792, 1792], P('wt', 'ctx')
- grad_gate: float32 [1792, 4864], P('ctx', 'wt')
- grad_up: float32 [1792, 4864], P('ctx', 'wt')
- grad_down: float32 [4864, 1792], P('wt', 'ctx')
The draws below stay inside these ranges and needn't reach their ends.
Inputs may be any that keep to these rules, and one draw needn't show every extreme that they name: `lengths`: one sequence, drawn from the seed, has all 4096 positions valid and another a quarter of 4096.
All inputs are finite; a program needn't handle non-finite values.
Results may differ from the reference program's by a relative error of at most 0.024.
Values may be sent and summed in bfloat16 or wider, within the bound.
No kernel may reach another device: no remote copies, remote signals or barrier semaphores. Data moves between devices by JAX's collectives and lax.ppermute only.
A program may use at most 320 MiB of HBM per device.

```python
from functools import partial
import jax
import jax.numpy as jnp
from jax import lax

D = 1792
HEADS = 16
FEAT = 16
FF = 4864
HEAD_DIM = 112
HF = 256
PHI = 273
SEQS = 2
L_DEV = 512
SLOT = 4096


def draw_lengths(key, part):
    first_key, second_key = jax.random.split(jax.random.fold_in(key, 17))
    order = jax.random.permutation(first_key, SEQS)
    others = jax.random.randint(second_key, (SEQS,), SLOT // 4, SLOT + 1)
    chosen = jnp.where(order == 0, SLOT, jnp.where(order == 1, SLOT // 4, others))
    return chosen.astype(jnp.int32)


def level_of(key, extent, shards, smallest, largest):
    gain = 1.0
    for position, blocks in shards:
        heights = jax.random.uniform(jax.random.fold_in(jax.random.fold_in(key, 6), position), (blocks,), jnp.float32, smallest / len(shards), largest / len(shards))
        gain = gain * jnp.repeat(jnp.exp(heights), extent[position] // blocks).reshape((-1,) + (1,) * (len(extent) - 1 - position))
    return gain


def centred(stream_key, dims, spread, reach, cuts=(), kind=jnp.bfloat16):
    values = jax.random.normal(stream_key, dims, jnp.float32) * spread
    if len(cuts) > 0:
        values = level_of(stream_key, dims, cuts, -0.22, 0.18) * values
    return jnp.clip(values, min=-reach, max=reach).astype(kind)


def setup_inputs(seed: int = 0) -> dict:
    keys = jax.random.split(jax.random.key(seed), 13)
    hidden_in = centred(keys[0], (SEQS, SLOT, D), 1.0, 6.0, ((1, 8), (2, 4)))
    lengths = draw_lengths(jax.random.fold_in(keys[12], 71), 0)
    gain_attn = jnp.clip(1.0 + 0.1 * jax.random.normal(keys[2], (D,), jnp.float32), 0.5, 1.5).astype(jnp.bfloat16)
    gain_ffn = jnp.clip(1.0 + 0.1 * jax.random.normal(keys[3], (D,), jnp.float32), 0.5, 1.5).astype(jnp.bfloat16)
    w_query = centred(keys[4], (D, HF), D ** -0.5, 0.125, ((0, 8), (1, 4)))
    w_key = centred(keys[5], (D, HF), D ** -0.5, 0.125, ((0, 8), (1, 4)))
    w_value = centred(keys[6], (D, D), D ** -0.5, 0.125, ((0, 8), (1, 4)))
    w_output = centred(keys[7], (D, D), ((SLOT // 8) ** 0.5 * D ** -0.5), 6.0, ((0, 4), (1, 8)))
    w_gate = centred(keys[8], (D, FF), D ** -0.5, 0.125, ((0, 8), (1, 4)))
    w_up = centred(keys[9], (D, FF), D ** -0.5, 0.125, ((0, 8), (1, 4)))
    w_down = centred(keys[10], (FF, D), FF ** -0.5, 0.078125, ((0, 4), (1, 8)))
    cotangent = centred(keys[11], (SEQS, SLOT, D), 1.0, 6.0, ((1, 8), (2, 4)))
    return dict(hidden_in=hidden_in, lengths=lengths, gain_attn=gain_attn, gain_ffn=gain_ffn, w_query=w_query, w_key=w_key, w_value=w_value, w_output=w_output, w_gate=w_gate, w_up=w_up, w_down=w_down, cotangent=cotangent)


exact_mode = lax.Precision.HIGHEST
epsilon = 1e-05

@jax.custom_vjp
def low(v):
    return lax.optimization_barrier(v.astype(jnp.bfloat16)).astype(jnp.float32)

@jax.custom_vjp
def low_back(v):
    return v

def low_keep(v):
    return (low(v), None)

def low_pass(kept, grad):
    return (grad,)

def back_keep(v):
    return (v, None)

def back_low(kept, grad):
    return (low(grad),)
low.defvjp(low_keep, low_pass)
low_back.defvjp(back_keep, back_low)

def features(vectors):
    feat_dim = vectors.shape[-1]
    outer_prod = (vectors[..., :, None] * vectors[..., None, :]).reshape(vectors.shape[:-1] + (feat_dim * feat_dim,))
    ones_col = jnp.ones(vectors.shape[:-1] + (1,), jnp.float32)
    return jnp.concatenate([ones_col, vectors * feat_dim ** (-0.25), outer_prod * (0.5 / feat_dim) ** 0.5], -1)

def attend(query, key_in, value_in, state_sum, norm_sum, valid_mask):
    feat_dim = query.shape[-1]
    size = query.shape[1]
    mapped = features(query)
    numer = jnp.einsum('slhp,sphe->slhe', mapped, state_sum, precision=exact_mode)
    denom = jnp.einsum('slhp,sph->slh', mapped, norm_sum, precision=exact_mode)
    scores = jnp.einsum('sbhf,schf->shbc', query, key_in, precision=exact_mode) * feat_dim ** (-0.5)
    causal = (jnp.arange(size)[:, None] >= jnp.arange(size)[None, :]).astype(jnp.float32)
    weights = (1.0 + scores + 0.5 * scores * scores) * causal * valid_mask[:, None, None, :]
    numer = numer + jnp.einsum('shbc,sche->sbhe', weights, value_in, precision=exact_mode)
    denom = denom + jnp.einsum('shbc->sbh', weights)
    return numer / denom[..., None]

def block_state(key_in, value_in, valid_mask):
    mapped = features(key_in) * valid_mask[:, :, None, None]
    state_sum = jnp.einsum('slhp,slhe->sphe', mapped, value_in, precision=exact_mode)
    norm_sum = jnp.einsum('slhp->sph', mapped)
    return (state_sum, norm_sum)

def attention(query, key_in, value_in, valid_mask):
    blocks = SLOT // L_DEV

    def to_blocks(array):
        shaped = array.reshape((array.shape[0], blocks, L_DEV) + array.shape[2:])
        return jnp.moveaxis(shaped, 1, 0)

    def advance(carried, pieces):
        block_out = attend(pieces[0], pieces[1], pieces[2], carried[0], carried[1], pieces[3])
        state_add, norm_add = block_state(pieces[1], pieces[2], pieces[3])
        return ((carried[0] + state_add, carried[1] + norm_add), block_out)
    start_state = jnp.zeros((SEQS, PHI, HEADS, HEAD_DIM), jnp.float32)
    start_norm = jnp.zeros((SEQS, PHI, HEADS), jnp.float32)
    inputs = (to_blocks(query), to_blocks(key_in), to_blocks(value_in), to_blocks(valid_mask))
    _, outputs = lax.scan(jax.checkpoint(advance), (start_state, start_norm), inputs)
    return jnp.moveaxis(outputs, 0, 1).reshape(value_in.shape)

def matmul(left, right):
    return jnp.einsum('...d,df->...f', left, right, precision=exact_mode)

def layer(hidden_in, gain_attn, gain_ffn, w_query, w_key, w_value, w_output, w_gate, w_up, w_down, valid_mask):
    inv_one = lax.rsqrt(lax.optimization_barrier(jnp.mean(hidden_in * hidden_in, -1, keepdims=True)) + epsilon)
    normed_one = low(hidden_in * inv_one * gain_attn)
    query = low_back(low(matmul(normed_one, w_query)))
    key_in = low_back(low(matmul(normed_one, w_key)))
    value_in = low_back(low(matmul(normed_one, w_value)))
    attn = attention(query.reshape(SEQS, SLOT, HEADS, FEAT), key_in.reshape(SEQS, SLOT, HEADS, FEAT), value_in.reshape(SEQS, SLOT, HEADS, HEAD_DIM), valid_mask)
    mixed_heads = low(low_back(attn.reshape(SEQS, SLOT, D)))
    residual = hidden_in + low_back(matmul(mixed_heads, w_output))
    inv_two = lax.rsqrt(lax.optimization_barrier(jnp.mean(residual * residual, -1, keepdims=True)) + epsilon)
    normed_two = low(residual * inv_two * gain_ffn)
    gate_pre = low_back(matmul(normed_two, w_gate))
    up_pre = low_back(matmul(normed_two, w_up))
    activation = low(jax.nn.silu(gate_pre) * up_pre)
    return residual + low_back(matmul(activation, w_down))

def reference(hidden_in, lengths, gain_attn, gain_ffn, w_query, w_key, w_value, w_output, w_gate, w_up, w_down, cotangent):
    valid_mask = (jnp.arange(SLOT, dtype=jnp.int32)[None, :] < lengths[:, None]).astype(jnp.float32)
    as_float = [array.astype(jnp.float32) for array in (hidden_in, gain_attn, gain_ffn, w_query, w_key, w_value, w_output, w_gate, w_up, w_down)]
    layer_out, pullback = jax.vjp(partial(layer, valid_mask=valid_mask), *as_float)
    gradients = pullback(cotangent.astype(jnp.float32) * valid_mask[..., None])
    return (layer_out.astype(jnp.bfloat16), gradients[0], gradients[1], gradients[2], gradients[3], gradients[4], gradients[5], gradients[6], gradients[7], gradients[8], gradients[9])
```

```python
from functools import partial

import jax
import jax.numpy as jnp
from jax import lax
from jax.experimental import pallas as pl
from jax.experimental.pallas import tpu as pltpu
from jax.sharding import PartitionSpec as P

D = 1792
FEAT = 16
HEAD_DIM = 112
EXT = 128
PHI = 160
EPS = 1e-05
BF = jnp.bfloat16
F32 = jnp.float32


def mm_nn(left, right):
    return lax.dot_general(left, right, (((1,), (0,)), ((), ())), preferred_element_type=F32)


def mm_tn(left, right):
    return lax.dot_general(left, right, (((0,), (0,)), ((), ())), preferred_element_type=F32)


def mm_nt(left, right):
    return lax.dot_general(left, right, (((1,), (1,)), ((), ())), preferred_element_type=F32)


def swap(value, bit):
    count = lax.axis_size("wt")
    return lax.ppermute(value, "wt", [(i, i ^ bit) for i in range(count)])


def wt_gather(block):
    me = lax.axis_index("wt")
    far = swap(block, 2)
    near = swap(block, 1)
    both = swap(far, 1)
    odd, high = (me & 1) == 1, me >= 2
    first = jnp.where(high, far, block), jnp.where(high, both, near)
    second = jnp.where(high, block, far), jnp.where(high, near, both)
    return jnp.concatenate(
        [
            jnp.where(odd, first[1], first[0]),
            jnp.where(odd, first[0], first[1]),
            jnp.where(odd, second[1], second[0]),
            jnp.where(odd, second[0], second[1]),
        ],
        0,
    )


def wt_scatter(partial_sum):
    me = lax.axis_index("wt")
    core, chip = me & 1, me >> 1
    rows, columns = partial_sum.shape
    shaped = partial_sum.reshape(2, 2, rows // 4, columns)
    sent = lax.dynamic_index_in_dim(shaped, 1 - core, 1, keepdims=False)
    kept = lax.dynamic_index_in_dim(shaped, core, 1, keepdims=False)
    got = swap(sent, 1)
    other = lax.dynamic_index_in_dim(kept, 1 - chip, 0, keepdims=False).astype(
        F32
    ) + lax.dynamic_index_in_dim(got, 1 - chip, 0, keepdims=False).astype(F32)
    mine = lax.dynamic_index_in_dim(kept, chip, 0, keepdims=False).astype(
        F32
    ) + lax.dynamic_index_in_dim(got, chip, 0, keepdims=False).astype(F32)
    return mine + swap(other.astype(BF), 2).astype(F32)


def wt_total(value):
    value = value + swap(value, 1)
    return value + swap(value, 2)


def ring_order(count):
    half = count // 2
    return [2 * r for r in range(half)] + [2 * r + 1 for r in reversed(range(half))]


def ringed():
    return lax.axis_size("ctx") == 8


def hop(value, step):
    order = ring_order(lax.axis_size("ctx"))
    count = len(order)
    pairs = [(order[r], order[(r + step) % count]) for r in range(count)]
    return lax.ppermute(value, "ctx", pairs)


def ring_index(offset):
    order = ring_order(lax.axis_size("ctx"))
    count = len(order)
    place = {device: r for r, device in enumerate(order)}
    table = jnp.array([order[(place[i] + offset) % count] for i in range(count)], jnp.int32)
    return table[lax.axis_index("ctx")]


def ctx_gather(shard):
    if not ringed():
        return lax.all_gather(shard, "ctx", axis=0, tiled=True)
    rows = shard.shape[0]
    half = rows // 2
    pieces = [(shard, 0, 0)]
    right, left = shard, shard
    for step in range(1, 4):
        right, left = hop(right, 1), hop(left, -1)
        pieces += [(right, -step, 0), (left, step, 0)]
    pieces += [(hop(right[:half], 1), 4, 0), (hop(left[half:], -1), 4, half)]
    full = jnp.zeros((rows * 8,) + shard.shape[1:], shard.dtype)
    for piece, offset, start in pieces:
        full = lax.dynamic_update_slice_in_dim(full, piece, ring_index(offset) * rows + start, 0)
    return full


def ctx_scatter(full):
    if not ringed():
        return lax.psum_scatter(full, "ctx", scatter_dimension=0, tiled=True).astype(F32)
    rows = full.shape[0] // 8
    half = rows // 2

    def own(offset):
        return lax.dynamic_slice_in_dim(full, ring_index(offset) * rows, rows, 0)

    opposite = own(4)
    right, left = hop(opposite[:half], 1), hop(opposite[half:], -1)
    zero = jnp.zeros((half, full.shape[1]), full.dtype)
    right, left = jnp.concatenate([right, zero], 0), jnp.concatenate([zero, left], 0)
    for step in (3, 2, 1):
        right = hop((right.astype(F32) + own(step).astype(F32)).astype(BF), 1)
        left = hop((left.astype(F32) + own(-step).astype(F32)).astype(BF), -1)
    return own(0).astype(F32) + right.astype(F32) + left.astype(F32)


def shifted(value, by):
    count = lax.axis_size("ctx")
    pairs = [(i, i + by) for i in range(count) if 0 <= i + by < count]
    return lax.ppermute(value, "ctx", pairs)


def ctx_before(value, sign):
    count, index = lax.axis_size("ctx"), lax.axis_index("ctx")
    if not ringed():
        everything = lax.all_gather(value, "ctx").astype(F32)
        place = jnp.arange(count)
        keep = (place < index) if sign > 0 else (place > index)
        keep = keep.reshape((count,) + (1,) * value.ndim)
        return jnp.sum(jnp.where(keep, everything, 0.0), 0).astype(BF)
    other = lax.ppermute(value, "ctx", [(i, i ^ 1) for i in range(count)])
    behind = (index & 1) == (1 if sign > 0 else 0)
    total = (value.astype(F32) + other.astype(F32)).astype(BF)
    first = shifted(total, 2 * sign)
    two = (total.astype(F32) + first.astype(F32)).astype(BF)
    second = shifted(two, 4 * sign)
    result = first.astype(F32) + second.astype(F32)
    return (result + jnp.where(behind, other.astype(F32), 0.0)).astype(BF)


def ctx_total(value):
    if not ringed():
        return lax.psum(value, "ctx")
    for bit in (1, 2, 4):
        value = value + lax.ppermute(value, "ctx", [(i, i ^ bit) for i in range(8)])
    return value


def turned(rows, by):
    return jnp.concatenate([rows[by:], rows[:by]], 0)


def feature_rows(vectors, square, cross, linear):
    length = vectors.shape[1]
    half = FEAT // 2
    pieces = [vectors * vectors * square]
    pieces += [vectors * turned(vectors, by) * cross for by in range(1, half)]
    pieces += [vectors[:half] * vectors[half:] * cross]
    place = lax.broadcasted_iota(jnp.int32, (half, length), 0)
    pieces += [jnp.where(place == 0, 1.0, 0.0), vectors * linear]
    return jnp.concatenate(pieces, 0).astype(BF)


def feature_pull(grad, vectors, square, cross, linear):
    half = FEAT // 2
    total = 2.0 * square * grad[:FEAT] * vectors
    for by in range(1, half):
        part = grad[FEAT * by : FEAT * (by + 1)] * cross
        total += part * turned(vectors, by) + turned(part * vectors, FEAT - by)
    part = grad[FEAT * half : FEAT * half + half] * cross
    total += jnp.concatenate([part * vectors[half:], part * vectors[:half]], 0)
    return total + grad[PHI - FEAT :] * linear


QUERY_SCALE = (1.0 / 32.0, 1.0 / 16.0, 0.25)
KEY_SCALE = (1.0, 1.0, 1.0)


def extended(value, valid):
    place = lax.broadcasted_iota(jnp.int32, (EXT - HEAD_DIM, value.shape[1]), 0)
    tail = jnp.where(place == 0, jnp.broadcast_to(valid, place.shape), 0.0)
    return jnp.concatenate([(value.astype(F32) * valid).astype(BF), tail.astype(BF)], 0)


def causal_of(length):
    key_place = lax.broadcasted_iota(jnp.int32, (length, length), 0)
    query_place = lax.broadcasted_iota(jnp.int32, (length, length), 1)
    return key_place <= query_place


def state_kernel(key_ref, value_ref, valid_ref, state_ref):
    mapped = feature_rows(key_ref[...].astype(F32), *KEY_SCALE)
    state_ref[0] = mm_nt(mapped, extended(value_ref[...], valid_ref[...])).astype(BF)


def attend_kernel(query_ref, key_ref, value_ref, valid_ref, state_ref, mixed_ref, denom_ref):
    query = query_ref[...]
    scores = mm_tn(key_ref[...], query) * 0.25
    weights = jnp.where(causal_of(query.shape[1]), 1.0 + scores + 0.5 * scores * scores, 0.0)
    total = mm_nn(extended(value_ref[...], valid_ref[...]), weights.astype(BF))
    mapped = feature_rows(query.astype(F32), *QUERY_SCALE)
    total += mm_tn(state_ref[0], mapped)
    denom = total[HEAD_DIM : HEAD_DIM + 1]
    denom_ref[0] = denom
    mixed_ref[...] = (total[:HEAD_DIM] / denom).astype(BF)


def spread_kernel(query_ref, grad_ref, mixed_ref, denom_ref, weighted_ref, state_ref):
    weighted = grad_ref[...].astype(F32) / denom_ref[0]
    shift = jnp.sum(weighted * mixed_ref[...].astype(F32), 0, keepdims=True)
    place = lax.broadcasted_iota(jnp.int32, (EXT - HEAD_DIM, weighted.shape[1]), 0)
    tail = jnp.where(place == 0, -jnp.broadcast_to(shift, place.shape), 0.0)
    whole = jnp.concatenate([weighted, tail], 0).astype(BF)
    weighted_ref[0] = whole
    mapped = feature_rows(query_ref[...].astype(F32), *QUERY_SCALE)
    state_ref[0] = mm_nt(mapped, whole).astype(BF)


def local_kernel(
    query_ref, key_ref, value_ref, valid_ref, state_ref, weighted_ref, dq_ref, dk_ref, dv_ref
):
    query, key_in, weighted = query_ref[...], key_ref[...], weighted_ref[0]
    causal = causal_of(query.shape[1])
    scores = mm_tn(key_in, query) * 0.25
    weights = jnp.where(causal, 1.0 + scores + 0.5 * scores * scores, 0.0).astype(BF)
    dv_ref[...] = mm_nt(weighted[:HEAD_DIM], weights) * valid_ref[...]
    slope = mm_tn(extended(value_ref[...], valid_ref[...]), weighted)
    slope = jnp.where(causal, slope * (1.0 + scores), 0.0).astype(BF)
    mapped = mm_nn(state_ref[0], weighted)
    pulled = feature_pull(mapped, query.astype(F32), *QUERY_SCALE)
    dq_ref[...] = (mm_nn(key_in, slope) * 0.25 + pulled).astype(BF)
    dk_ref[...] = mm_nt(query, slope) * 0.25


def later_kernel(key_ref, value_ref, valid_ref, state_ref, dk_in, dv_in, dk_ref, dv_ref):
    key_in = key_ref[...].astype(F32)
    valid = valid_ref[...]
    mapped = mm_nn(state_ref[0], extended(value_ref[...], valid))
    dk_ref[...] = (dk_in[...] + feature_pull(mapped, key_in, *KEY_SCALE)).astype(BF)
    spread = mm_tn(state_ref[0], feature_rows(key_in, *KEY_SCALE))
    dv_ref[...] = (dv_in[...] + spread[:HEAD_DIM] * valid).astype(BF)


def head_call(kernel, name, heads, length, ins, outs, cost):
    specs = {
        "feat": (pl.BlockSpec((FEAT, length), lambda h: (h, 0)), (heads * FEAT, length)),
        "head": (pl.BlockSpec((HEAD_DIM, length), lambda h: (h, 0)), (heads * HEAD_DIM, length)),
        "valid": (pl.BlockSpec((1, length), lambda h: (0, 0)), (1, length)),
        "state": (pl.BlockSpec((1, PHI, EXT), lambda h: (h, 0, 0)), (heads, PHI, EXT)),
        "row": (pl.BlockSpec((1, 1, length), lambda h: (h, 0, 0)), (heads, 1, length)),
        "ext": (pl.BlockSpec((1, EXT, length), lambda h: (h, 0, 0)), (heads, EXT, length)),
    }
    return pl.pallas_call(
        kernel,
        name=name,
        grid=(heads,),
        in_specs=[specs[i][0] for i in ins],
        out_specs=[specs[o][0] for o, _ in outs],
        out_shape=[jax.ShapeDtypeStruct(specs[o][1], kind) for o, kind in outs],
        compiler_params=pltpu.CompilerParams(vmem_limit_bytes=32 << 20),
        cost_estimate=pl.CostEstimate(flops=cost, bytes_accessed=4 << 20, transcendentals=0),
    )


def body(
    hidden_in,
    lengths,
    gain_attn,
    gain_ffn,
    w_query,
    w_key,
    w_value,
    w_output,
    w_gate,
    w_up,
    w_down,
    cotangent,
):
    seqs, length, width = hidden_in.shape
    heads = w_value.shape[1] // HEAD_DIM
    q_rows = heads * FEAT
    both = range(seqs)
    position = lax.axis_index("ctx") * length + jnp.arange(length, dtype=jnp.int32)
    valid = [(position < lengths[s]).astype(F32)[None, :] for s in both]

    hidden = [hidden_in[s].T for s in both]
    full_in = [wt_gather(hidden[s]) for s in both]
    gains = wt_gather(jnp.stack([gain_attn, gain_ffn], 1)).astype(F32)
    attn_shard = jnp.concatenate([w_query, w_key, w_value, w_output.T], 1)
    w_attn = ctx_gather(attn_shard)
    qkv_columns = 2 * q_rows + heads * HEAD_DIM
    w_qkv, w_out = w_attn[:, :qkv_columns], w_attn[:, qkv_columns:]
    gate_full = ctx_gather(w_gate)
    up_full = ctx_gather(w_up)
    down_full = ctx_gather(w_down.T)
    grad_out = [(cotangent[s].T.astype(F32) * valid[s]).astype(BF) for s in both]
    grad_out_full = [wt_gather(grad_out[s]) for s in both]

    def normed(full, gain):
        value = full.astype(F32)
        inverse = lax.rsqrt(jnp.sum(value * value, 0, keepdims=True) / D + EPS)
        return inverse, (value * inverse * gain[:, None]).astype(BF)

    call = partial(head_call, heads=heads, length=length)
    flops = heads * 2 * length * length * 256

    inv_one, normed_one, query, key_in, value_in, state = [], [], [], [], [], []
    for s in both:
        inverse, normal = normed(full_in[s], gains[:, 0])
        qkv = mm_tn(w_qkv, normal).astype(BF)
        inv_one.append(inverse)
        normed_one.append(normal)
        query.append(qkv[:q_rows])
        key_in.append(qkv[q_rows : 2 * q_rows])
        value_in.append(qkv[2 * q_rows :])
        (own,) = call(
            state_kernel, "state", ins=("feat", "head", "valid"), outs=(("state", BF),), cost=flops // 2
        )(key_in[s], value_in[s], valid[s])
        state.append(ctx_before(own, 1))

    mixed, denom, resid, inv_two, normed_two = [], [], [], [], []
    for s in both:
        mix, den = call(
            attend_kernel,
            "attend",
            ins=("feat", "feat", "head", "valid", "state"),
            outs=(("head", BF), ("row", F32)),
            cost=flops,
        )(query[s], key_in[s], value_in[s], valid[s], state[s])
        mixed.append(mix)
        denom.append(den)
        resid.append(hidden[s].astype(F32) + wt_scatter(mm_nn(w_out, mix).astype(BF)))
        inverse, normal = normed(wt_gather(resid[s].astype(BF)), gains[:, 1])
        inv_two.append(inverse)
        normed_two.append(normal)

    layer_out, grad_gate, grad_up, act, d_norm_two, inner_two = [], [], [], [], [], []
    for s in both:
        gate = mm_tn(gate_full, normed_two[s])
        up = mm_tn(up_full, normed_two[s])
        sig = jax.nn.sigmoid(gate)
        silu = gate * sig
        act.append((silu * up).astype(BF))
        layer_out.append(
            (resid[s] + wt_scatter(mm_nn(down_full, act[s]).astype(BF))).astype(BF)
        )
        d_act = mm_tn(down_full, grad_out_full[s])
        g_gate = (d_act * up * sig * (1.0 + gate * (1.0 - sig))).astype(BF)
        g_up = (d_act * silu).astype(BF)
        grad_gate.append(g_gate)
        grad_up.append(g_up)
        inner_two.append(
            wt_total(
                jnp.sum(g_gate.astype(F32) * gate + g_up.astype(F32) * up, 0, keepdims=True)
            )
        )
        d_norm_two.append(
            wt_scatter((mm_nn(gate_full, g_gate) + mm_nn(up_full, g_up)).astype(BF))
        )

    down_grad = ctx_scatter(sum(mm_nt(grad_out_full[s], act[s]) for s in both).astype(BF))
    gate_grad = ctx_scatter(sum(mm_nt(normed_two[s], grad_gate[s]) for s in both).astype(BF))
    up_grad = ctx_scatter(sum(mm_nt(normed_two[s], grad_up[s]) for s in both).astype(BF))

    gain_two = gain_ffn.astype(F32)[:, None]
    gain_one = gain_attn.astype(F32)[:, None]
    gain_two_part, d_resid, resid_full, weighted, d_state = 0.0, [], [], [], []
    for s in both:
        gain_two_part += jnp.sum(resid[s] * inv_two[s] * d_norm_two[s], 1)
        d_resid.append(
            grad_out[s].astype(F32)
            + inv_two[s] * gain_two * d_norm_two[s]
            - resid[s] * (inv_two[s] * inv_two[s] * inner_two[s] / D)
        )
        resid_full.append(wt_gather(d_resid[s].astype(BF)))
        g_attn = mm_tn(w_out, resid_full[s]).astype(BF)
        whole, spread = call(
            spread_kernel,
            "spread",
            ins=("feat", "head", "head", "row"),
            outs=(("ext", BF), ("state", BF)),
            cost=flops // 2,
        )(query[s], g_attn, mixed[s], denom[s])
        weighted.append(whole)
        d_state.append(ctx_before(spread, -1))
    gain_two_grad = ctx_total(gain_two_part)

    gain_one_part, grad_input, d_qkv = 0.0, [], []
    for s in both:
        dq, dk_part, dv_part = call(
            local_kernel,
            "local",
            ins=("feat", "feat", "head", "valid", "state", "ext"),
            outs=(("feat", BF), ("feat", F32), ("head", F32)),
            cost=flops * 2,
        )(query[s], key_in[s], value_in[s], valid[s], state[s], weighted[s])
        dk, dv = call(
            later_kernel,
            "later",
            ins=("feat", "head", "valid", "state", "feat", "head"),
            outs=(("feat", BF), ("head", BF)),
            cost=flops // 2,
        )(key_in[s], value_in[s], valid[s], d_state[s], dk_part, dv_part)
        d_qkv.append(jnp.concatenate([dq, dk, dv], 0))
        inner = 0.0
        for grad, made in ((dq, query[s]), (dk, key_in[s]), (dv, value_in[s])):
            inner += jnp.sum(grad.astype(F32) * made.astype(F32), 0, keepdims=True)
        inner = wt_total(inner)
        d_norm_one = wt_scatter(mm_nn(w_qkv, d_qkv[s]).astype(BF))
        value = hidden[s].astype(F32)
        gain_one_part += jnp.sum(value * inv_one[s] * d_norm_one, 1)
        grad_input.append(
            d_resid[s]
            + inv_one[s] * gain_one * d_norm_one
            - value * (inv_one[s] * inv_one[s] * inner / D)
        )
    attn_part = jnp.concatenate(
        [
            sum(mm_nt(normed_one[s], d_qkv[s]) for s in both).astype(BF),
            sum(mm_nt(resid_full[s], mixed[s]) for s in both).astype(BF),
        ],
        1,
    )
    attn_grad = ctx_scatter(attn_part)
    gain_one_grad = ctx_total(gain_one_part)

    return (
        jnp.stack([v.T for v in layer_out]),
        jnp.stack([v.T for v in grad_input]),
        gain_one_grad,
        gain_two_grad,
        attn_grad[:, :q_rows],
        attn_grad[:, q_rows : 2 * q_rows],
        attn_grad[:, 2 * q_rows : qkv_columns],
        attn_grad[:, qkv_columns:].T,
        gate_grad,
        up_grad,
        down_grad.T,
    )


def solution(mesh):
    acts, rows, columns = P(None, "ctx", "wt"), P("ctx", "wt"), P("wt", "ctx")
    in_specs = (acts, P(), P("wt"), P("wt"), rows, rows, rows, columns, rows, rows, columns, acts)
    out_specs = (acts, acts, P("wt"), P("wt"), rows, rows, rows, columns, rows, rows, columns)
    return jax.shard_map(body, mesh=mesh, in_specs=in_specs, out_specs=out_specs, check_vma=False)
```

```python
from functools import partial

import jax
import jax.numpy as jnp
from jax import lax
from jax.experimental import pallas as pl
from jax.experimental.pallas import tpu as pltpu
from jax.sharding import PartitionSpec as P

D = 1792
FEAT = 16
HEAD_DIM = 112
EXT = 128
PHI = 160
EPS = 1e-05
BF = jnp.bfloat16
F32 = jnp.float32


def mm_nn(left, right):
    return lax.dot_general(left, right, (((1,), (0,)), ((), ())), preferred_element_type=F32)


def mm_tn(left, right):
    return lax.dot_general(left, right, (((0,), (0,)), ((), ())), preferred_element_type=F32)


def mm_nt(left, right):
    return lax.dot_general(left, right, (((1,), (1,)), ((), ())), preferred_element_type=F32)


def swap(value, bit):
    count = lax.axis_size("wt")
    return lax.ppermute(value, "wt", [(i, i ^ bit) for i in range(count)])


def in_order(own, near, far, both):
    me = lax.axis_index("wt")
    odd, high = (me & 1) == 1, me >= 2
    first = jnp.where(high, far, own), jnp.where(high, both, near)
    second = jnp.where(high, own, far), jnp.where(high, near, both)
    return jnp.concatenate(
        [
            jnp.where(odd, first[1], first[0]),
            jnp.where(odd, first[0], first[1]),
            jnp.where(odd, second[1], second[0]),
            jnp.where(odd, second[0], second[1]),
        ],
        0,
    )


class Spread:
    def __init__(self, block):
        self.block, self.far, self.near = block, swap(block, 2), swap(block, 1)

    def cross(self):
        self.both = swap(self.far, 1)

    def full(self, s=None):
        found = self.block, self.near, self.far, self.both
        return in_order(*(found if s is None else [v[s] for v in found]))


def wt_gather(block):
    spread = Spread(block)
    spread.cross()
    return spread.full()


class Scatter:
    def __init__(self, partial_sum, row=None):
        core = lax.axis_index("wt") & 1
        self.rows, self.columns = partial_sum.shape[0] // 4, partial_sum.shape[1]
        shaped = partial_sum.reshape(2, 2, self.rows, self.columns)
        sent = lax.dynamic_index_in_dim(shaped, 1 - core, 1, keepdims=False)
        self.kept = lax.dynamic_index_in_dim(shaped, core, 1, keepdims=False)
        self.row = row
        self.got = swap(self._with_row(sent, row), 1)

    def _with_row(self, blocks, row):
        if row is None:
            return blocks
        high = row.astype(BF)
        low = (row - high.astype(F32)).astype(BF)
        tail = jnp.concatenate([high, low, jnp.zeros((6, self.columns), BF)], 0)
        tail = jnp.broadcast_to(tail, blocks.shape[:-2] + tail.shape)
        return jnp.concatenate([blocks, tail], -2)

    def _row_of(self, block):
        two = block[self.rows : self.rows + 2].astype(F32)
        return two[:1] + two[1:]

    def _pair(self, which):
        kept = lax.dynamic_index_in_dim(self.kept, which, 0, keepdims=False)
        got = lax.dynamic_index_in_dim(self.got, which, 0, keepdims=False)
        return kept.astype(F32) + got[: self.rows].astype(F32)

    def cross(self):
        self.chip = lax.axis_index("wt") >> 1
        self.half = None if self.row is None else self.row + self._row_of(self.got[0])
        self.last = swap(self._with_row(self._pair(1 - self.chip).astype(BF), self.half), 2)

    def sums(self):
        total = self._pair(self.chip) + self.last[: self.rows].astype(F32)
        return total if self.row is None else (total, self.half + self._row_of(self.last))


def ring_order(count):
    half = count // 2
    return [2 * r for r in range(half)] + [2 * r + 1 for r in reversed(range(half))]


def ringed():
    return lax.axis_size("ctx") == 8


def hop(value, step):
    order = ring_order(lax.axis_size("ctx"))
    count = len(order)
    pairs = [(order[r], order[(r + step) % count]) for r in range(count)]
    return lax.ppermute(value, "ctx", pairs)


def ring_index(*offsets):
    order = ring_order(lax.axis_size("ctx"))
    count = len(order)
    place = {device: r for r, device in enumerate(order)}
    table = [[order[(place[i] + offset) % count] for offset in offsets] for i in range(count)]
    return jnp.array(table, jnp.int32)[lax.axis_index("ctx")]


ANY = pl.BlockSpec(memory_space=pl.ANY)


def assembled(pieces, starts, rows):
    count = len(pieces)

    def kernel(start_ref, *refs):
        out, sems = refs[count], refs[count + 1]
        copies = []
        for k in range(count):
            size = pieces[k].shape[-2]
            at = pl.ds(pl.multiple_of(start_ref[k], 16), size)
            where = out.at[at, :] if len(out.shape) == 2 else out.at[:, at, :]
            copies.append(pltpu.make_async_copy(refs[k], where, sems.at[k]))
            copies[-1].start()
        for copy in copies:
            copy.wait()

    shape = pieces[0].shape[:-2] + (rows, pieces[0].shape[-1])
    return pl.pallas_call(
        kernel,
        name="assemble",
        in_specs=[pl.BlockSpec(memory_space=pltpu.SMEM)] + [ANY] * count,
        out_specs=pl.BlockSpec(memory_space=pltpu.VMEM),
        out_shape=jax.ShapeDtypeStruct(shape, pieces[0].dtype),
        scratch_shapes=[pltpu.SemaphoreType.DMA((count,))],
        compiler_params=pltpu.CompilerParams(vmem_limit_bytes=24 << 20),
        cost_estimate=pl.CostEstimate(flops=0, bytes_accessed=8 << 20, transcendentals=0),
    )(starts, *pieces)


def tie(value, *others):
    return lax.optimization_barrier((value,) + others)[0] if others else value


class Gather:
    def __init__(self, shard):
        self.shard, self.axis = shard, shard.ndim - 2
        self.right, self.left = [shard], [shard]

    def advance(self, *others):
        if not ringed():
            return
        right, left = self.right[-1], self.left[-1]
        if len(self.right) == 4:
            rows = right.shape[self.axis]
            right = lax.slice_in_dim(right, 0, rows // 2, axis=self.axis)
            left = lax.slice_in_dim(left, rows // 2, rows, axis=self.axis)
        if others:
            right, left = lax.optimization_barrier((right, left) + others)[:2]
        self.right.append(hop(right, 1))
        self.left.append(hop(left, -1))

    def here(self):
        return (self.right[-1], self.left[-1]) if ringed() else ()

    def full(self):
        if not ringed():
            return lax.all_gather(self.shard, "ctx", axis=self.axis, tiled=True)
        rows = self.shard.shape[self.axis]
        starts = ring_index(0, -1, -2, -3, 4, 1, 2, 3, 4) * rows
        starts += jnp.array([0] * 8 + [rows // 2], jnp.int32)
        return assembled(self.right + self.left[1:], starts, rows * 8)


def grad_products(lefts, rights, index, got, rows, out, name):
    seqs = len(lefts[0])
    widths = [r[0].shape[0] for r in rights]
    columns = sum(widths)
    chunks = index.shape[0]
    length = lefts[0][0].shape[1]
    half = rows // 2
    n_left, n_right = len(lefts) * seqs, len(rights) * seqs
    same = [k for k in range(len(lefts)) if k and lefts[k][0] is lefts[k - 1][0]]
    unique = [k for k in range(len(lefts)) if k not in same]
    source = []
    for k in range(len(lefts)):
        source.append(len([u for u in unique if u <= k]) - 1)
    if out == "halves":
        shapes = [((half, columns), BF)] * 2
    elif out == "sums":
        shapes = [((rows, columns), BF)] * chunks
    else:
        shapes = [((rows, w), F32) for w in widths]

    def kernel(index_ref, *refs):
        n_l = len(unique) * seqs
        left_refs = refs[:n_l]
        right_refs = refs[n_l : n_l + n_right]
        got_refs = refs[n_l + n_right : n_l + n_right + len(got)]
        rest = refs[n_l + n_right + len(got) :]
        outs, scratch = rest[: len(shapes)], rest[len(shapes) :]
        left_bufs, right_bufs, sems = scratch[:n_l], scratch[n_l : n_l + n_right], scratch[-1]
        copies = {}
        for k in range(len(lefts)):
            for s in range(seqs):
                if k in unique:
                    u = source[k] * seqs + s
                    for c in range(chunks):
                        at = pl.ds(pl.multiple_of(index_ref[c] * rows, 16), rows)
                        key = ("l", u, c)
                        copies[key] = pltpu.make_async_copy(
                            left_refs[u].at[at, :], left_bufs[u].at[c], sems.at[len(copies)]
                        )
                        copies[key].start()
                r = k * seqs + s
                copies["r", r] = pltpu.make_async_copy(
                    right_refs[r], right_bufs[r], sems.at[len(copies)]
                )
                copies["r", r].start()
        first = 0
        for k in range(len(lefts)):
            for s in range(seqs):
                if k in unique:
                    for c in range(chunks):
                        copies["l", source[k] * seqs + s, c].wait()
                copies["r", k * seqs + s].wait()
            for c in range(chunks):
                total = 0.0
                for s in range(seqs):
                    total += mm_nt(
                        left_bufs[source[k] * seqs + s][c], right_bufs[k * seqs + s][...]
                    )
                span = pl.ds(first, widths[k])
                if out == "final":
                    for ref in got_refs:
                        total += ref[:, span].astype(F32)
                    outs[k][...] = total
                elif out == "halves":
                    outs[0][:, span] = total[:half].astype(BF)
                    outs[1][:, span] = total[half:].astype(BF)
                elif got_refs[c].shape[0] == rows:
                    outs[c][:, span] = (total + got_refs[c][:, span].astype(F32)).astype(BF)
                else:
                    more = got_refs[c][:, span].astype(F32)
                    top = total[:half] + more if c == 0 else total[:half]
                    low = total[half:] + more if c == 1 else total[half:]
                    outs[c][:half, span] = top.astype(BF)
                    outs[c][half:, span] = low.astype(BF)
            first += widths[k]

    whole = pl.BlockSpec(memory_space=pltpu.VMEM)
    left_arrays = [lefts[k][s] for k in unique for s in range(seqs)]
    right_arrays = [r[s] for r in rights for s in range(seqs)]
    n_copies = len(left_arrays) * chunks + len(right_arrays)
    flops = 2 * chunks * rows * columns * length * seqs
    return pl.pallas_call(
        kernel,
        name=name,
        in_specs=[pl.BlockSpec(memory_space=pltpu.SMEM)]
        + [ANY] * (len(left_arrays) + len(right_arrays))
        + [whole] * len(got),
        out_specs=[whole] * len(shapes),
        out_shape=[jax.ShapeDtypeStruct(*s) for s in shapes],
        scratch_shapes=[pltpu.VMEM((chunks, rows, length), BF)] * len(left_arrays)
        + [pltpu.VMEM(a.shape, BF) for a in right_arrays]
        + [pltpu.SemaphoreType.DMA((n_copies,))],
        compiler_params=pltpu.CompilerParams(vmem_limit_bytes=40 << 20),
        cost_estimate=pl.CostEstimate(
            flops=flops, bytes_accessed=2 * length * seqs * columns + 4 * rows * columns, transcendentals=0
        ),
    )(index, *left_arrays, *right_arrays, *got)


class Products:
    def __init__(self, lefts, rights, name):
        self.given = lefts, rights
        self.name, self.step = name, 4

    def _kernel(self, index, got, out):
        lefts, rights = self.given
        rows = lefts[0][0].shape[0] // 8
        return grad_products(lefts, rights, index, got, rows, out, f"{self.name}_{self.step}")

    def advance(self, *others):
        if not ringed():
            return others
        if self.step == 4:
            sent = self._kernel(tie(ring_index(4), *others), [], "halves")
        else:
            index = tie(ring_index(self.step, -self.step), *others)
            sent = self._kernel(index, self.got, "sums")
        self.got = [hop(sent[0], 1), hop(sent[1], -1)]
        self.step -= 1
        return tuple(sent)

    def final(self):
        if not ringed():
            found = []
            for left, right in zip(*self.given):
                total = sum(mm_nt(a, b) for a, b in zip(left, right)).astype(BF)
                found.append(lax.psum_scatter(total, "ctx", scatter_dimension=0, tiled=True).astype(F32))
            return found
        return self._kernel(ring_index(0), self.got, "final")


def shifted(value, by):
    count = lax.axis_size("ctx")
    pairs = [(i, i + by) for i in range(count) if 0 <= i + by < count]
    return lax.ppermute(value, "ctx", pairs)


class Before:
    def __init__(self, value, sign):
        self.value, self.sign = value, sign
        if ringed():
            count = lax.axis_size("ctx")
            self.other = lax.ppermute(value, "ctx", [(i, i ^ 1) for i in range(count)])

    def first(self):
        if ringed():
            self.total = (self.value.astype(F32) + self.other.astype(F32)).astype(BF)
            self.one = shifted(self.total, 2 * self.sign)

    def second(self):
        if ringed():
            two = (self.total.astype(F32) + self.one.astype(F32)).astype(BF)
            self.two = shifted(two, 4 * self.sign)

    def result(self):
        count, index = lax.axis_size("ctx"), lax.axis_index("ctx")
        if not ringed():
            everything = lax.all_gather(self.value, "ctx").astype(F32)
            place = jnp.arange(count)
            keep = (place < index) if self.sign > 0 else (place > index)
            keep = keep.reshape((count,) + (1,) * self.value.ndim)
            return jnp.sum(jnp.where(keep, everything, 0.0), 0).astype(BF)
        behind = (index & 1) == (1 if self.sign > 0 else 0)
        result = self.one.astype(F32) + self.two.astype(F32)
        return (result + jnp.where(behind, self.other.astype(F32), 0.0)).astype(BF)


def ctx_total(value):
    if not ringed():
        return lax.psum(value, "ctx")
    for bit in (1, 2, 4):
        value = value + lax.ppermute(value, "ctx", [(i, i ^ bit) for i in range(8)])
    return value


def turned(rows, by):
    return jnp.concatenate([rows[by:], rows[:by]], 0)


def feature_rows(vectors, square, cross, linear):
    length = vectors.shape[1]
    half = FEAT // 2
    pieces = [vectors * vectors * square]
    pieces += [vectors * turned(vectors, by) * cross for by in range(1, half)]
    pieces += [vectors[:half] * vectors[half:] * cross]
    place = lax.broadcasted_iota(jnp.int32, (half, length), 0)
    pieces += [jnp.where(place == 0, 1.0, 0.0), vectors * linear]
    return jnp.concatenate(pieces, 0).astype(BF)


def feature_pull(grad, vectors, square, cross, linear):
    half = FEAT // 2
    total = 2.0 * square * grad[:FEAT] * vectors
    for by in range(1, half):
        part = grad[FEAT * by : FEAT * (by + 1)] * cross
        total += part * turned(vectors, by) + turned(part * vectors, FEAT - by)
    part = grad[FEAT * half : FEAT * half + half] * cross
    total += jnp.concatenate([part * vectors[half:], part * vectors[:half]], 0)
    return total + grad[PHI - FEAT :] * linear


QUERY_SCALE = (1.0 / 32.0, 1.0 / 16.0, 0.25)
KEY_SCALE = (1.0, 1.0, 1.0)


def extended(value, valid):
    place = lax.broadcasted_iota(jnp.int32, (EXT - HEAD_DIM, value.shape[1]), 0)
    tail = jnp.where(place == 0, jnp.broadcast_to(valid, place.shape), 0.0)
    return jnp.concatenate([(value.astype(F32) * valid).astype(BF), tail.astype(BF)], 0)


def causal_of(length):
    key_place = lax.broadcasted_iota(jnp.int32, (length, length), 0)
    query_place = lax.broadcasted_iota(jnp.int32, (length, length), 1)
    return key_place <= query_place


def state_kernel(key_ref, value_ref, valid_ref, state_ref):
    mapped = feature_rows(key_ref[...].astype(F32), *KEY_SCALE)
    state_ref[0] = mm_nt(mapped, extended(value_ref[...], valid_ref[...])).astype(BF)


def attend_kernel(query_ref, key_ref, value_ref, valid_ref, state_ref, mixed_ref, denom_ref):
    query = query_ref[...]
    scores = mm_tn(key_ref[...], query) * 0.25
    weights = jnp.where(causal_of(query.shape[1]), 1.0 + scores + 0.5 * scores * scores, 0.0)
    total = mm_nn(extended(value_ref[...], valid_ref[...]), weights.astype(BF))
    mapped = feature_rows(query.astype(F32), *QUERY_SCALE)
    total += mm_tn(state_ref[0], mapped)
    denom = total[HEAD_DIM : HEAD_DIM + 1]
    denom_ref[0] = denom
    mixed_ref[...] = (total[:HEAD_DIM] / denom).astype(BF)


def spread_kernel(query_ref, grad_ref, mixed_ref, denom_ref, weighted_ref, state_ref):
    weighted = grad_ref[...].astype(F32) / denom_ref[0]
    shift = jnp.sum(weighted * mixed_ref[...].astype(F32), 0, keepdims=True)
    place = lax.broadcasted_iota(jnp.int32, (EXT - HEAD_DIM, weighted.shape[1]), 0)
    tail = jnp.where(place == 0, -jnp.broadcast_to(shift, place.shape), 0.0)
    whole = jnp.concatenate([weighted, tail], 0).astype(BF)
    weighted_ref[0] = whole
    mapped = feature_rows(query_ref[...].astype(F32), *QUERY_SCALE)
    state_ref[0] = mm_nt(mapped, whole).astype(BF)


def local_kernel(
    query_ref, key_ref, value_ref, valid_ref, state_ref, weighted_ref, dq_ref, dk_ref, dv_ref
):
    query, key_in, weighted = query_ref[...], key_ref[...], weighted_ref[0]
    causal = causal_of(query.shape[1])
    scores = mm_tn(key_in, query) * 0.25
    weights = jnp.where(causal, 1.0 + scores + 0.5 * scores * scores, 0.0).astype(BF)
    dv_ref[...] = mm_nt(weighted[:HEAD_DIM], weights) * valid_ref[...]
    slope = mm_tn(extended(value_ref[...], valid_ref[...]), weighted)
    slope = jnp.where(causal, slope * (1.0 + scores), 0.0).astype(BF)
    mapped = mm_nn(state_ref[0], weighted)
    pulled = feature_pull(mapped, query.astype(F32), *QUERY_SCALE)
    dq_ref[...] = (mm_nn(key_in, slope) * 0.25 + pulled).astype(BF)
    dk_ref[...] = mm_nt(query, slope) * 0.25


def later_kernel(key_ref, value_ref, valid_ref, state_ref, dk_in, dv_in, dk_ref, dv_ref):
    key_in = key_ref[...].astype(F32)
    valid = valid_ref[...]
    mapped = mm_nn(state_ref[0], extended(value_ref[...], valid))
    dk_ref[...] = (dk_in[...] + feature_pull(mapped, key_in, *KEY_SCALE)).astype(BF)
    spread = mm_tn(state_ref[0], feature_rows(key_in, *KEY_SCALE))
    dv_ref[...] = (dv_in[...] + spread[:HEAD_DIM] * valid).astype(BF)


def head_call(kernel, name, heads, length, ins, outs, cost):
    specs = {
        "feat": (pl.BlockSpec((FEAT, length), lambda h: (h, 0)), (heads * FEAT, length)),
        "head": (pl.BlockSpec((HEAD_DIM, length), lambda h: (h, 0)), (heads * HEAD_DIM, length)),
        "valid": (pl.BlockSpec((1, length), lambda h: (0, 0)), (1, length)),
        "state": (pl.BlockSpec((1, PHI, EXT), lambda h: (h, 0, 0)), (heads, PHI, EXT)),
        "row": (pl.BlockSpec((1, 1, length), lambda h: (h, 0, 0)), (heads, 1, length)),
        "ext": (pl.BlockSpec((1, EXT, length), lambda h: (h, 0, 0)), (heads, EXT, length)),
    }
    return pl.pallas_call(
        kernel,
        name=name,
        grid=(heads,),
        in_specs=[specs[i][0] for i in ins],
        out_specs=[specs[o][0] for o, _ in outs],
        out_shape=[jax.ShapeDtypeStruct(specs[o][1], kind) for o, kind in outs],
        compiler_params=pltpu.CompilerParams(vmem_limit_bytes=32 << 20),
        cost_estimate=pl.CostEstimate(flops=cost, bytes_accessed=4 << 20, transcendentals=0),
    )


def body(
    hidden_in,
    lengths,
    gain_attn,
    gain_ffn,
    w_query,
    w_key,
    w_value,
    w_output,
    w_gate,
    w_up,
    w_down,
    cotangent,
):
    seqs, length, width = hidden_in.shape
    heads = w_value.shape[1] // HEAD_DIM
    q_rows = heads * FEAT
    both = range(seqs)
    position = lax.axis_index("ctx") * length + jnp.arange(length, dtype=jnp.int32)
    valid = [(position < lengths[s]).astype(F32)[None, :] for s in both]

    hidden = [hidden_in[s].T for s in both]
    call = partial(head_call, heads=heads, length=length)
    flops = heads * 2 * length * length * 256
    qkv_columns = 2 * q_rows + heads * HEAD_DIM
    last = []

    def turn(value, *others):
        return tie(value, *(tuple(last) + others))

    def mark(value):
        last[:] = [value]
        return value

    def normed(full, gain):
        value = full.astype(F32)
        inverse = lax.rsqrt(jnp.sum(value * value, 0, keepdims=True) / D + EPS)
        return inverse, (value * inverse * gain[:, None]).astype(BF)

    spread_in = Spread(hidden_in.transpose(0, 2, 1))
    ring_attn = Gather(jnp.concatenate([w_query, w_key, w_value, w_output.T], 1))
    ring_gate_up = Gather(jnp.stack([w_gate, w_up]))
    ring_down = Gather(w_down.T)
    ring_attn.advance()
    gains = wt_gather(jnp.stack([gain_attn, gain_ffn], 1)).astype(F32)
    ring_attn.advance()
    ring_gate_up.advance(*ring_attn.here())
    spread_in.cross()
    ring_attn.advance()
    grad_out = (cotangent.transpose(0, 2, 1).astype(F32) * jnp.stack(valid)).astype(BF)
    spread_out = Spread(tie(grad_out, spread_in.far))
    ring_attn.advance()
    w_attn = ring_attn.full()
    w_qkv, w_out = w_attn[:, :qkv_columns], w_attn[:, qkv_columns:]
    spread_out.cross()

    inv_one, normed_one, query, key_in, value_in, before = [], [], [], [], [], []
    for s in both:
        inverse, normal = normed(spread_in.full(s), gains[:, 0])
        inv_one.append(inverse)
        normed_one.append(normal)
        qkv = mm_tn(w_qkv, turn(normal)).astype(BF)
        query.append(qkv[:q_rows])
        key_in.append(qkv[q_rows : 2 * q_rows])
        value_in.append(qkv[2 * q_rows :])
        (own,) = call(
            state_kernel, "state", ins=("feat", "head", "valid"), outs=(("state", BF),), cost=flops // 2
        )(key_in[s], value_in[s], valid[s])
        mark(own)
        before.append(Before(own, 1))
    ring_gate_up.advance(*last)
    for s in both:
        before[s].first()
    for s in both:
        before[s].second()
    grad_out_full = [spread_out.full(s) for s in both]

    state, mixed, denom, scatter_attn = [], [], [], []
    for s in both:
        state.append(before[s].result())
        mix, den = call(
            attend_kernel,
            "attend",
            ins=("feat", "feat", "head", "valid", "state"),
            outs=(("head", BF), ("row", F32)),
            cost=flops,
        )(turn(query[s]), key_in[s], value_in[s], valid[s], state[s])
        mixed.append(mix)
        denom.append(den)
        scatter_attn.append(Scatter(mark(mm_nn(w_out, mix).astype(BF))))
    ring_gate_up.advance(*last)
    resid, spread_resid = [], []
    for s in both:
        scatter_attn[s].cross()
    for s in both:
        resid.append(hidden[s].astype(F32) + scatter_attn[s].sums())
        spread_resid.append(Spread(resid[s].astype(BF)))
    ring_gate_up.advance(*last)
    ring_down.advance(*last)
    ring_down.advance()
    for s in both:
        spread_resid[s].cross()

    gate_up = ring_gate_up.full()
    gate_full, up_full = gate_up[0], gate_up[1]
    inv_two, normed_two, gate, up, act = [], [], [], [], []
    for s in both:
        inverse, normal = normed(spread_resid[s].full(), gains[:, 1])
        inv_two.append(inverse)
        normed_two.append(normal)
        ready = turn(normal)
        gate.append(mm_tn(gate_full, ready))
        up.append(mm_tn(up_full, ready))
        act.append(mark((gate[s] * jax.nn.sigmoid(gate[s]) * up[s]).astype(BF)))
    ring_down.advance()
    ring_down.advance()
    down_full = ring_down.full()

    grad_gate, grad_up, scatter_two = [], [], []
    for s in both:
        sig = jax.nn.sigmoid(gate[s])
        d_act = mm_tn(down_full, turn(grad_out_full[s]))
        g_gate = (d_act * up[s] * sig * (1.0 + gate[s] * (1.0 - sig))).astype(BF)
        g_up = (d_act * gate[s] * sig).astype(BF)
        grad_gate.append(g_gate)
        grad_up.append(g_up)
        inner = jnp.sum(
            g_gate.astype(F32) * gate[s] + g_up.astype(F32) * up[s], 0, keepdims=True
        )
        d_norm = mark((mm_nn(gate_full, g_gate) + mm_nn(up_full, g_up)).astype(BF))
        scatter_two.append(Scatter(d_norm, inner))
    scatter_two[0].cross()
    ffn_products = Products(
        [grad_out_full, normed_two, normed_two], [act, grad_gate, grad_up], "ffn_grad"
    )
    mark(ffn_products.advance(*last)[0])
    scatter_two[1].cross()
    scatter_out = []
    for s in both:
        scatter_out.append(Scatter(mark(mm_nn(down_full, turn(act[s])).astype(BF))))

    gain_two = gain_ffn.astype(F32)[:, None]
    gain_one = gain_attn.astype(F32)[:, None]
    gain_two_part, d_resid, spread_grad = 0.0, [], []
    for s in both:
        d_norm, inner = scatter_two[s].sums()
        gain_two_part += jnp.sum(resid[s] * inv_two[s] * d_norm, 1)
        d_resid.append(
            grad_out[s].astype(F32)
            + inv_two[s] * gain_two * d_norm
            - resid[s] * (inv_two[s] * inv_two[s] * inner / D)
        )
        spread_grad.append(Spread(d_resid[s].astype(BF)))
    for s in both:
        spread_grad[s].cross()
    for s in both:
        scatter_out[s].cross()
    resid_full, weighted, after = [], [], []
    for s in both:
        resid_full.append(turn(spread_grad[s].full()))
        g_attn = mm_tn(w_out, resid_full[s]).astype(BF)
        whole, spread = call(
            spread_kernel,
            "spread",
            ins=("feat", "head", "head", "row"),
            outs=(("ext", BF), ("state", BF)),
            cost=flops // 2,
        )(query[s], g_attn, mixed[s], denom[s])
        mark(spread)
        weighted.append(whole)
        after.append(Before(spread, -1))
    mark(ffn_products.advance(*last)[0])
    for s in both:
        after[s].first()
    local = []
    for s in both:
        found = call(
            local_kernel,
            "local",
            ins=("feat", "feat", "head", "valid", "state", "ext"),
            outs=(("feat", BF), ("feat", F32), ("head", F32)),
            cost=flops * 2,
        )(turn(query[s]), key_in[s], value_in[s], valid[s], state[s], weighted[s])
        mark(found[0])
        local.append(found)
        after[s].second()
    layer_out = [(resid[s] + scatter_out[s].sums()).astype(BF) for s in both]

    d_qkv, scatter_one = [], []
    for s in both:
        dq, dk_part, dv_part = local[s]
        dk, dv = call(
            later_kernel,
            "later",
            ins=("feat", "head", "valid", "state", "feat", "head"),
            outs=(("feat", BF), ("head", BF)),
            cost=flops // 2,
        )(turn(key_in[s]), value_in[s], valid[s], after[s].result(), dk_part, dv_part)
        d_qkv.append(jnp.concatenate([dq, dk, dv], 0))
        inner = 0.0
        for grad, made in ((dq, query[s]), (dk, key_in[s]), (dv, value_in[s])):
            inner += jnp.sum(grad.astype(F32) * made.astype(F32), 0, keepdims=True)
        scatter_one.append(Scatter(mark(mm_nn(w_qkv, d_qkv[s]).astype(BF)), inner))
    attn_products = Products([normed_one, resid_full], [d_qkv, mixed], "attn_grad")
    mark(attn_products.advance(*last)[0])
    for s in both:
        scatter_one[s].cross()
    mark(ffn_products.advance(*last)[0])
    mark(attn_products.advance(*last)[0])
    gain_one_part, grad_input = 0.0, []
    for s in both:
        value = hidden[s].astype(F32)
        d_norm, inner = scatter_one[s].sums()
        gain_one_part += jnp.sum(value * inv_one[s] * d_norm, 1)
        grad_input.append(
            d_resid[s]
            + inv_one[s] * gain_one * d_norm
            - value * (inv_one[s] * inv_one[s] * inner / D)
        )
    mark(attn_products.advance(*last)[0])
    mark(ffn_products.advance(*last)[0])
    mark(attn_products.advance(*last)[0])
    gain_grads = ctx_total(jnp.stack([gain_one_part, gain_two_part]))
    down_grad, gate_grad, up_grad = ffn_products.final()
    qkv_grad, out_grad = attn_products.final()

    return (
        jnp.stack([v.T for v in layer_out]),
        jnp.stack([v.T for v in grad_input]),
        gain_grads[0],
        gain_grads[1],
        qkv_grad[:, :q_rows],
        qkv_grad[:, q_rows : 2 * q_rows],
        qkv_grad[:, 2 * q_rows :],
        out_grad.T,
        gate_grad,
        up_grad,
        down_grad.T,
    )


def solution(mesh):
    acts, rows, columns = P(None, "ctx", "wt"), P("ctx", "wt"), P("wt", "ctx")
    in_specs = (acts, P(), P("wt"), P("wt"), rows, rows, rows, columns, rows, rows, columns, acts)
    out_specs = (acts, acts, P("wt"), P("wt"), rows, rows, rows, columns, rows, rows, columns)
    return jax.shard_map(body, mesh=mesh, in_specs=in_specs, out_specs=out_specs, check_vma=False)
```

```python
import jax
import jax.numpy as jnp
from jax import lax
from jax.experimental import pallas as pl
from jax.experimental.pallas import tpu as pltpu
from jax.sharding import PartitionSpec as P


D = 1792
FEAT = 16
HEAD_DIM = 112
EXT = 128
PHI = 160
EPS = 1e-05
BF = jnp.bfloat16
F32 = jnp.float32
ANY = pl.BlockSpec(memory_space=pl.ANY)
WHOLE = pl.BlockSpec(memory_space=pltpu.VMEM)
SMEM = pl.BlockSpec(memory_space=pltpu.SMEM)
OFFSETS = (0, 1, 2, 3, 4, -1, -2, -3)
PLACE = {offset: 1 + k for k, offset in enumerate(OFFSETS)}
PLACE[-4] = PLACE[4]


def mm_nn(left, right):
    return lax.dot_general(left, right, (((1,), (0,)), ((), ())), preferred_element_type=F32)


def mm_tn(left, right):
    return lax.dot_general(left, right, (((0,), (0,)), ((), ())), preferred_element_type=F32)


def mm_nt(left, right):
    return lax.dot_general(left, right, (((1,), (1,)), ((), ())), preferred_element_type=F32)


def tie(value, *others):
    others = jax.tree.leaves(others)
    return lax.optimization_barrier((value, *others))[0] if others else value


def params(mib=24):
    return pltpu.CompilerParams(vmem_limit_bytes=mib << 20)


def cost(flops=0, moved=4 << 20):
    return pl.CostEstimate(flops=flops, bytes_accessed=moved, transcendentals=0)


def swap(value, bit):
    count = lax.axis_size("wt")
    return lax.ppermute(value, "wt", [(i, i ^ bit) for i in range(count)])


class Spread:
    def __init__(self, block):
        self.block, self.far, self.near = block, swap(block, 2), swap(block, 1)

    def cross(self):
        self.both = swap(self.far, 1)

    def blocks(self):
        return self.block, self.near, self.far, self.both


def gathered(index, blocks, gains=None, column=0):
    seqs, rows, length = blocks[0].shape

    def kernel(index_ref, *refs):
        values = [ref[0] for ref in refs[:4]]
        out = refs[8 if gains is not None else 4]
        if gains is not None:
            values = [v.astype(F32) for v in values]
            total = sum(jnp.sum(v * v, 0, keepdims=True) for v in values)
            inverse = lax.rsqrt(total / D + EPS)
            refs[9][0] = inverse
            scaled = []
            for v, gain_ref in zip(values, refs[4:8]):
                gain = gain_ref[...][:, column : column + 1].astype(F32)
                scaled.append((v * inverse * gain).astype(BF))
            values = scaled
        me = index_ref[0]
        for bit in range(4):
            out[pl.ds(pl.multiple_of((me ^ bit) * rows, 16), rows), :] = values[bit]

    block = pl.BlockSpec((1, rows, length), lambda s, index_ref: (s, 0, 0))
    full = pl.BlockSpec((4 * rows, length), lambda s, index_ref: (0, s))
    row = pl.BlockSpec((1, 1, length), lambda s, index_ref: (s, 0, 0))
    gain = pl.BlockSpec((rows, 2), lambda s, index_ref: (0, 0))
    shape = jax.ShapeDtypeStruct((4 * rows, seqs * length), BF)
    inverse = jax.ShapeDtypeStruct((seqs, 1, length), F32)
    normed = gains is not None
    return pl.pallas_call(
        kernel,
        name="gather_norm" if normed else "gather",
        grid_spec=pltpu.PrefetchScalarGridSpec(
            num_scalar_prefetch=1,
            grid=(seqs,),
            in_specs=[block] * 4 + ([gain] * 4 if normed else []),
            out_specs=[full, row] if normed else full,
        ),
        out_shape=[shape, inverse] if normed else shape,
        compiler_params=params(),
        cost_estimate=cost(1 << 30),
    )(index, *blocks, *(gains if normed else ()))


def projected(index, weights, rights, name, columns=None, row=None):
    rows = D // 4
    depth, width = rights[0].shape
    extra = 0 if row is None else 8
    start = 0 if columns is None else columns
    stacked = weights.ndim == 3

    def kernel(index_ref, weight_ref, *refs):
        right_refs = refs[: len(rights)]
        sent, kept = refs[-2:]
        total = 0.0
        for k, right in enumerate(right_refs):
            left = weight_ref[k] if stacked else weight_ref[...][:, start : start + depth]
            total += mm_nn(left, right[...])
        step = pl.program_id(0)
        total = total.astype(BF)

        @pl.when(step < 2)
        def _():
            sent[0, :rows] = total
            if row is not None:
                value = refs[len(rights)][...]
                high = value.astype(BF).astype(F32)
                place = lax.broadcasted_iota(jnp.int32, (8, width), 0)
                tail = jnp.where(place == 0, high, jnp.where(place == 1, value - high, 0.0))
                sent[0, rows:] = tail.astype(BF)

        @pl.when(step >= 2)
        def _():
            kept[0] = total

    def of(i, index_ref):
        core = index_ref[0] % 2
        return (i % 2) * 2 + jnp.where(i < 2, 1 - core, core)

    if stacked:
        left_spec = pl.BlockSpec((len(rights), rows, depth), lambda i, r: (0, of(i, r), 0))
    else:
        left_spec = pl.BlockSpec((rows, weights.shape[1]), lambda i, r: (of(i, r), 0))
    in_specs = [left_spec] + [pl.BlockSpec((depth, width), lambda i, r: (0, 0))] * len(rights)
    if row is not None:
        in_specs.append(pl.BlockSpec((1, width), lambda i, r: (0, 0)))
    return pl.pallas_call(
        kernel,
        name=name,
        grid_spec=pltpu.PrefetchScalarGridSpec(
            num_scalar_prefetch=1,
            grid=(4,),
            in_specs=in_specs,
            out_specs=[
                pl.BlockSpec((1, rows + extra, width), lambda i, r: (jnp.minimum(i, 1), 0, 0)),
                pl.BlockSpec((1, rows, width), lambda i, r: (jnp.maximum(i - 2, 0), 0, 0)),
            ],
        ),
        out_shape=[
            jax.ShapeDtypeStruct((2, rows + extra, width), BF),
            jax.ShapeDtypeStruct((2, rows, width), BF),
        ],
        compiler_params=params(32),
        cost_estimate=cost(2 * D * depth * len(rights) * width, 8 << 20),
    )(index, weights, *rights, *(() if row is None else (row,)))


class Scatter:
    def __init__(self, index, parts, seqs, row=None):
        self.index, self.row, self.seqs = index, row, seqs
        self.sent, self.kept = parts
        self.got = swap(self.sent, 1)

    def cross(self):
        seqs, row = self.seqs, self.row
        rows, width = self.kept.shape[1:]
        length = width // seqs
        extra = 0 if row is None else 8

        def kernel(index_ref, kept_ref, got_ref, *refs):
            far, mine = refs[-2:] if row is None else refs[-3:-1]
            chip = index_ref[0] // 2
            other = kept_ref[1 - chip].astype(F32) + got_ref[1 - chip, :rows].astype(F32)
            far[0, :rows] = other.astype(BF)
            mine[0] = kept_ref[chip].astype(F32) + got_ref[chip, :rows].astype(F32)
            if row is not None:
                two = got_ref[0, rows:].astype(F32)
                value = refs[0][...] + two[:1] + two[1:2]
                refs[-1][0] = value
                high = value.astype(BF).astype(F32)
                place = lax.broadcasted_iota(jnp.int32, (8, length), 0)
                tail = jnp.where(place == 0, high, jnp.where(place == 1, value - high, 0.0))
                far[0, rows:] = tail.astype(BF)

        def spec(height):
            return pl.BlockSpec((1, height, length), lambda s, r: (s, 0, 0))

        out = [((seqs, rows + extra, length), BF), ((seqs, rows, length), F32)]
        out += [] if row is None else [((seqs, 1, length), F32)]
        in_specs = [
            pl.BlockSpec((2, rows, length), lambda s, r: (0, 0, s)),
            pl.BlockSpec((2, rows + extra, length), lambda s, r: (0, 0, s)),
        ]
        in_specs += [] if row is None else [pl.BlockSpec((1, length), lambda s, r: (0, s))]
        found = pl.pallas_call(
            kernel,
            name="pair_sum",
            grid_spec=pltpu.PrefetchScalarGridSpec(
                num_scalar_prefetch=1,
                grid=(seqs,),
                in_specs=in_specs,
                out_specs=[spec(shape[1]) for shape, _ in out],
            ),
            out_shape=[jax.ShapeDtypeStruct(*o) for o in out],
            compiler_params=params(),
            cost_estimate=cost(1 << 28),
        )(self.index, self.kept, self.got, *(() if row is None else (row,)))
        self.sent_far, self.mine, self.rows = found[0], found[1], rows
        self.half = None if row is None else found[2]
        self.last = swap(self.sent_far, 2)

    def sums(self, *others):
        last = tie(self.last, *others)
        total = self.mine + last[:, : self.rows].astype(F32)
        if self.row is None:
            return total
        two = last[:, self.rows : self.rows + 2].astype(F32)
        return total, self.half + two[:, :1] + two[:, 1:]


def ring_order(count):
    half = count // 2
    return [2 * r for r in range(half)] + [2 * r + 1 for r in reversed(range(half))]


def ringed():
    return lax.axis_size("ctx") == 8


def hop(value, step):
    order = ring_order(lax.axis_size("ctx"))
    count = len(order)
    pairs = [(order[r], order[(r + step) % count]) for r in range(count)]
    return lax.ppermute(value, "ctx", pairs)


def places():
    count = lax.axis_size("ctx")
    order = ring_order(count)
    place = {device: r for r, device in enumerate(order)}
    table = [[0] + [order[(place[i] + offset) % count] for offset in OFFSETS] for i in range(count)]
    found = jnp.array(table, jnp.int32)[lax.axis_index("ctx")]
    return found + jnp.where(jnp.arange(len(OFFSETS) + 1) == 0, lax.axis_index("wt"), 0)


class Gather:
    def __init__(self, shard):
        self.shard, self.axis = shard, shard.ndim - 2
        self.right, self.left = [shard], [shard]

    def advance(self, *others):
        if not ringed():
            return
        right, left = self.right[-1], self.left[-1]
        if len(self.right) == 4:
            rows = right.shape[self.axis]
            right = lax.slice_in_dim(right, 0, rows // 2, axis=self.axis)
            left = lax.slice_in_dim(left, rows // 2, rows, axis=self.axis)
        others = jax.tree.leaves(others)
        if others:
            right, left = lax.optimization_barrier((right, left, *others))[:2]
        self.right.append(hop(right, 1))
        self.left.append(hop(left, -1))

    def here(self):
        return (self.right[-1], self.left[-1]) if ringed() else ()

    def full(self, index):
        if not ringed():
            return lax.all_gather(self.shard, "ctx", axis=self.axis, tiled=True)
        rows = self.shard.shape[self.axis]
        pieces = self.right + self.left[1:]
        offsets = (0, -1, -2, -3, 4, 1, 2, 3, 4)
        count = len(pieces)

        def kernel(index_ref, *refs):
            out, sems = refs[count], refs[count + 1]
            copies = []
            for k in range(count):
                first = index_ref[PLACE[offsets[k]]] * rows + (rows // 2 if k == 8 else 0)
                at = pl.ds(pl.multiple_of(first, 16), pieces[k].shape[-2])
                where = out.at[at, :] if len(out.shape) == 2 else out.at[:, at, :]
                copies.append(pltpu.make_async_copy(refs[k], where, sems.at[k]))
                copies[-1].start()
            for copy in copies:
                copy.wait()

        shape = self.shard.shape[:-2] + (rows * 8, self.shard.shape[-1])
        return pl.pallas_call(
            kernel,
            name="assemble",
            in_specs=[SMEM] + [ANY] * count,
            out_specs=WHOLE,
            out_shape=jax.ShapeDtypeStruct(shape, BF),
            scratch_shapes=[pltpu.SemaphoreType.DMA((count,))],
            compiler_params=params(),
            cost_estimate=cost(),
        )(index, *pieces)


def products(lefts, rights, name):
    rows, length = lefts[0].shape
    widths = [r.shape[0] for r in rights]
    used = lefts[:1] if all(left is lefts[0] for left in lefts) else lefts

    def kernel(*refs):
        out = refs[-1]
        first = 0
        for k, width in enumerate(widths):
            left = refs[k if len(used) > 1 else 0]
            out[:, pl.ds(first, width)] = mm_nt(left[...], refs[len(used) + k][...]).astype(BF)
            first += width

    return pl.pallas_call(
        kernel,
        name=name,
        grid=(4,),
        in_specs=[pl.BlockSpec((rows // 4, length), lambda i: (i, 0))] * len(used)
        + [pl.BlockSpec((width, length), lambda i: (0, 0)) for width in widths],
        out_specs=pl.BlockSpec((rows // 4, sum(widths)), lambda i: (i, 0)),
        out_shape=jax.ShapeDtypeStruct((rows, sum(widths)), BF),
        compiler_params=params(32),
        cost_estimate=cost(2 * rows * length * sum(widths), 2 * rows * sum(widths)),
    )(*used, *rights)


class Products:
    def __init__(self, index, full):
        self.index, self.full, self.step, self.sent = index, full, 4, ()
        if ringed():
            self.rows, self.width = full.shape[0] // 8, full.shape[1]
            self._send()

    def _send(self):
        half, step = self.rows // 2, self.step
        first, second = step == 4, step == 3

        def kernel(index_ref, *refs):
            row = pl.program_id(0)
            if first:
                own, right, left = refs

                @pl.when(row == 0)
                def _():
                    right[...] = own[...]

                @pl.when(row == 1)
                def _():
                    left[...] = own[...]

                return
            from_right, from_left, own_right, own_left, right, left = refs
            more_right, more_left = from_right[...].astype(F32), from_left[...].astype(F32)
            if second:
                more_right = jnp.where(row == 0, more_right, 0.0)
                more_left = jnp.where(row == 1, more_left, 0.0)
            right[...] = (own_right[...].astype(F32) + more_right).astype(BF)
            left[...] = (own_left[...].astype(F32) + more_left).astype(BF)

        def own(offset):
            return pl.BlockSpec((half, self.width), lambda i, r: (r[PLACE[offset]] * 2 + i, 0))

        still = pl.BlockSpec((half, self.width), lambda i, r: (0, 0))
        moving = pl.BlockSpec((half, self.width), lambda i, r: (i, 0))
        if first:
            in_specs, out_spec, given, rows = [own(4)], still, (self.full,), half
        else:
            in_specs = [still if second else moving] * 2 + [own(step), own(-step)]
            out_spec, given, rows = moving, (self.right, self.left, self.full, self.full), self.rows
        self.sent = pl.pallas_call(
            kernel,
            name="ring_sum",
            grid_spec=pltpu.PrefetchScalarGridSpec(
                num_scalar_prefetch=1, grid=(2,), in_specs=in_specs, out_specs=[out_spec] * 2
            ),
            out_shape=[jax.ShapeDtypeStruct((rows, self.width), BF)] * 2,
            compiler_params=params(),
            cost_estimate=cost(1 << 24),
        )(self.index, *given)
        self.right, self.left = hop(self.sent[0], 1), hop(self.sent[1], -1)

    def here(self):
        return (self.right, self.left) if ringed() else ()

    def advance(self, *others):
        if ringed():
            self.step -= 1
            self.right = tie(self.right, self.left, *others)
            self._send()

    def final(self, *others):
        if not ringed():
            return lax.psum_scatter(self.full, "ctx", scatter_dimension=0, tiled=True).astype(F32)
        right = tie(self.right, self.left, *others)

        def kernel(index_ref, own, right_ref, left_ref, out):
            out[...] = own[...].astype(F32) + right_ref[...].astype(F32) + left_ref[...].astype(F32)

        half = self.rows // 2
        moving = pl.BlockSpec((half, self.width), lambda i, r: (i, 0))
        own = pl.BlockSpec((half, self.width), lambda i, r: (r[PLACE[0]] * 2 + i, 0))
        return pl.pallas_call(
            kernel,
            name="ring_end",
            grid_spec=pltpu.PrefetchScalarGridSpec(
                num_scalar_prefetch=1, grid=(2,), in_specs=[own, moving, moving], out_specs=moving
            ),
            out_shape=jax.ShapeDtypeStruct((self.rows, self.width), F32),
            compiler_params=params(),
            cost_estimate=cost(1 << 24),
        )(self.index, self.full, right, self.left)


def shifted(value, by):
    count = lax.axis_size("ctx")
    pairs = [(i, i + by) for i in range(count) if 0 <= i + by < count]
    return lax.ppermute(value, "ctx", pairs)


class Before:
    def __init__(self, value, sign):
        self.value, self.sign = value, sign
        self.other = self.one = self.two = self.sent = ()
        if ringed():
            count = lax.axis_size("ctx")
            self.other = lax.ppermute(value, "ctx", [(i, i ^ 1) for i in range(count)])

    def first(self):
        if ringed():
            self.total = (self.value.astype(F32) + self.other.astype(F32)).astype(BF)
            self.one = shifted(self.total, 2 * self.sign)

    def second(self):
        if ringed():
            self.sent = (self.total.astype(F32) + self.one.astype(F32)).astype(BF)
            self.two = shifted(self.sent, 4 * self.sign)

    def result(self):
        count, index = lax.axis_size("ctx"), lax.axis_index("ctx")
        if not ringed():
            everything = lax.all_gather(self.value, "ctx").astype(F32)
            place = jnp.arange(count)
            keep = (place < index) if self.sign > 0 else (place > index)
            keep = keep.reshape((count,) + (1,) * self.value.ndim)
            return jnp.sum(jnp.where(keep, everything, 0.0), 0).astype(BF)
        behind = (index & 1) == (1 if self.sign > 0 else 0)
        result = self.one.astype(F32) + self.two.astype(F32)
        return (result + jnp.where(behind, self.other.astype(F32), 0.0)).astype(BF)


def ctx_total(value):
    if not ringed():
        return lax.psum(value, "ctx")
    for bit in (1, 2, 4):
        value = value + lax.ppermute(value, "ctx", [(i, i ^ bit) for i in range(8)])
    return value


def turned(rows, by):
    return jnp.concatenate([rows[by:], rows[:by]], 0)


def feature_rows(vectors, square, cross, linear):
    length = vectors.shape[1]
    half = FEAT // 2
    pieces = [vectors * vectors * square]
    pieces += [vectors * turned(vectors, by) * cross for by in range(1, half)]
    pieces += [vectors[:half] * vectors[half:] * cross]
    place = lax.broadcasted_iota(jnp.int32, (half, length), 0)
    pieces += [jnp.where(place == 0, 1.0, 0.0), vectors * linear]
    return jnp.concatenate(pieces, 0).astype(BF)


def feature_pull(grad, vectors, square, cross, linear):
    half = FEAT // 2
    total = 2.0 * square * grad[:FEAT] * vectors
    for by in range(1, half):
        part = grad[FEAT * by : FEAT * (by + 1)] * cross
        total += part * turned(vectors, by) + turned(part * vectors, FEAT - by)
    part = grad[FEAT * half : FEAT * half + half] * cross
    total += jnp.concatenate([part * vectors[half:], part * vectors[:half]], 0)
    return total + grad[PHI - FEAT :] * linear


QUERY_SCALE = (1.0 / 32.0, 1.0 / 16.0, 0.25)
KEY_SCALE = (1.0, 1.0, 1.0)


def extended(value, valid):
    place = lax.broadcasted_iota(jnp.int32, (EXT - HEAD_DIM, value.shape[1]), 0)
    tail = jnp.where(place == 0, jnp.broadcast_to(valid, place.shape), 0.0)
    return jnp.concatenate([(value.astype(F32) * valid).astype(BF), tail.astype(BF)], 0)


def causal_of(length):
    key_place = lax.broadcasted_iota(jnp.int32, (length, length), 0)
    query_place = lax.broadcasted_iota(jnp.int32, (length, length), 1)
    return key_place <= query_place


def state_kernel(key_ref, value_ref, valid_ref, state_ref):
    mapped = feature_rows(key_ref[...].astype(F32), *KEY_SCALE)
    state_ref[0, 0] = mm_nt(mapped, extended(value_ref[...], valid_ref[0])).astype(BF)


def attend_kernel(query_ref, key_ref, value_ref, valid_ref, state_ref, mixed_ref, denom_ref):
    query = query_ref[...]
    scores = mm_tn(key_ref[...], query) * 0.25
    weights = jnp.where(causal_of(query.shape[1]), 1.0 + scores + 0.5 * scores * scores, 0.0)
    total = mm_nn(extended(value_ref[...], valid_ref[0]), weights.astype(BF))
    mapped = feature_rows(query.astype(F32), *QUERY_SCALE)
    total += mm_tn(state_ref[0, 0], mapped)
    denom = total[HEAD_DIM : HEAD_DIM + 1]
    denom_ref[0, 0] = denom
    mixed_ref[...] = (total[:HEAD_DIM] / denom).astype(BF)


def spread_kernel(query_ref, grad_ref, mixed_ref, denom_ref, weighted_ref, state_ref):
    weighted = grad_ref[...].astype(F32) / denom_ref[0, 0]
    shift = jnp.sum(weighted * mixed_ref[...].astype(F32), 0, keepdims=True)
    place = lax.broadcasted_iota(jnp.int32, (EXT - HEAD_DIM, weighted.shape[1]), 0)
    tail = jnp.where(place == 0, -jnp.broadcast_to(shift, place.shape), 0.0)
    whole = jnp.concatenate([weighted, tail], 0).astype(BF)
    weighted_ref[0, 0] = whole
    mapped = feature_rows(query_ref[...].astype(F32), *QUERY_SCALE)
    state_ref[0, 0] = mm_nt(mapped, whole).astype(BF)


def local_kernel(
    query_ref, key_ref, value_ref, valid_ref, state_ref, weighted_ref, dq_ref, dk_ref, dv_ref
):
    query, key_in, weighted = query_ref[...], key_ref[...], weighted_ref[0, 0]
    causal = causal_of(query.shape[1])
    scores = mm_tn(key_in, query) * 0.25
    weights = jnp.where(causal, 1.0 + scores + 0.5 * scores * scores, 0.0).astype(BF)
    dv_ref[...] = mm_nt(weighted[:HEAD_DIM], weights) * valid_ref[0]
    slope = mm_tn(extended(value_ref[...], valid_ref[0]), weighted)
    slope = jnp.where(causal, slope * (1.0 + scores), 0.0).astype(BF)
    mapped = mm_nn(state_ref[0, 0], weighted)
    pulled = feature_pull(mapped, query.astype(F32), *QUERY_SCALE)
    dq_ref[...] = (mm_nn(key_in, slope) * 0.25 + pulled).astype(BF)
    dk_ref[...] = mm_nt(query, slope) * 0.25


def later_kernel(heads, key_ref, value_ref, valid_ref, state_ref, dq_in, dk_in, dv_in, out_ref):
    head = pl.program_id(1)
    key_in = key_ref[...].astype(F32)
    valid = valid_ref[0]
    mapped = mm_nn(state_ref[0, 0], extended(value_ref[...], valid))
    d_key = (dk_in[...] + feature_pull(mapped, key_in, *KEY_SCALE)).astype(BF)
    spread = mm_tn(state_ref[0, 0], feature_rows(key_in, *KEY_SCALE))
    d_value = (dv_in[...] + spread[:HEAD_DIM] * valid).astype(BF)
    values, queries = heads * HEAD_DIM, heads * FEAT
    out_ref[pl.ds(pl.multiple_of(head * HEAD_DIM, 16), HEAD_DIM), :] = d_value
    out_ref[pl.ds(pl.multiple_of(values + head * FEAT, 16), FEAT), :] = dq_in[...]
    out_ref[pl.ds(pl.multiple_of(values + queries + head * FEAT, 16), FEAT), :] = d_key


def head_call(kernel, name, seqs, heads, length, ins, outs, flops):
    first_query = heads * HEAD_DIM // FEAT
    columns = heads * (HEAD_DIM + 2 * FEAT)
    specs = {
        "value": pl.BlockSpec((HEAD_DIM, length), lambda s, h: (h, s)),
        "query": pl.BlockSpec((FEAT, length), lambda s, h: (first_query + h, s)),
        "key": pl.BlockSpec((FEAT, length), lambda s, h: (first_query + heads + h, s)),
        "all": pl.BlockSpec((columns, length), lambda s, h: (0, s)),
        "feat": pl.BlockSpec((FEAT, length), lambda s, h: (h, s)),
        "head": pl.BlockSpec((HEAD_DIM, length), lambda s, h: (h, s)),
        "valid": pl.BlockSpec((1, 1, length), lambda s, h: (s, 0, 0)),
        "state": pl.BlockSpec((1, 1, PHI, EXT), lambda s, h: (s, h, 0, 0)),
        "row": pl.BlockSpec((1, 1, 1, length), lambda s, h: (s, h, 0, 0)),
        "ext": pl.BlockSpec((1, 1, EXT, length), lambda s, h: (s, h, 0, 0)),
    }
    shapes = {
        "all": (columns, seqs * length),
        "feat": (heads * FEAT, seqs * length),
        "head": (heads * HEAD_DIM, seqs * length),
        "state": (seqs, heads, PHI, EXT),
        "row": (seqs, heads, 1, length),
        "ext": (seqs, heads, EXT, length),
    }
    return pl.pallas_call(
        kernel,
        name=name,
        grid=(seqs, heads),
        in_specs=[specs[i] for i in ins],
        out_specs=[specs[o] for o, _ in outs],
        out_shape=[jax.ShapeDtypeStruct(shapes[o], kind) for o, kind in outs],
        compiler_params=params(),
        cost_estimate=cost(flops),
    )


def body(
    hidden_in,
    lengths,
    gain_attn,
    gain_ffn,
    w_query,
    w_key,
    w_value,
    w_output,
    w_gate,
    w_up,
    w_down,
    cotangent,
):
    seqs, length, width = hidden_in.shape
    heads = w_value.shape[1] // HEAD_DIM
    hidden_units = w_gate.shape[1]
    columns = heads * (HEAD_DIM + 2 * FEAT)
    index = places()
    position = lax.axis_index("ctx") * length + jnp.arange(length, dtype=jnp.int32)
    valid = (position[None, :] < lengths[:, None]).astype(F32)[:, None, :]
    hidden = hidden_in.transpose(0, 2, 1)
    unit = seqs * heads * 2 * length * length * 256
    token = [jnp.zeros((8, 128), F32)]

    def call(kernel, name, ins, outs, share):
        return head_call(kernel, name, seqs, heads, length, ins, outs, int(unit * share))

    def turn(value, *others):
        return tie(value, token[0], *others)

    def fence(*values):
        token[0] = tie(token[0], *values)

    ring_attn = Gather(jnp.concatenate([w_value, w_query, w_key, w_output.T], 1))
    ring_down = Gather(w_down.T)
    ring_gate_up = Gather(jnp.stack([w_gate, w_up]))
    ring_attn.advance()
    spread_in = Spread(hidden)
    gains = Spread(jnp.stack([gain_attn, gain_ffn], 1))
    gains.cross()
    fence(ring_attn.here())
    ring_attn.advance(*token)
    fence(ring_attn.here(), ring_gate_up.shard)
    ring_attn.advance(*token)
    ring_gate_up.advance(*token)
    fence(spread_in.far)
    spread_in.cross()
    grad_out = (cotangent.transpose(0, 2, 1).astype(F32) * valid).astype(BF)
    spread_out = Spread(turn(grad_out))
    fence(spread_in.near, spread_in.both)
    blocks = spread_in.blocks()
    normed_one, inv_one = gathered(index, (turn(blocks[0]),) + blocks[1:], gains.blocks(), 0)
    fence(ring_attn.here(), normed_one)
    ring_attn.advance(*token)
    fence(ring_attn.here())
    w_attn = ring_attn.full(turn(index))
    fence(w_attn, ring_gate_up.here())
    ring_gate_up.advance(*token)

    qkv = mm_tn(w_attn[:, :columns], turn(normed_one)).astype(BF)
    (own,) = call(state_kernel, "state", ("key", "value", "valid"), (("state", BF),), 0.5)(
        qkv, qkv, valid
    )
    before = Before(own, 1)
    fence(ring_gate_up.here(), before.other)
    before.first()
    fence(before.one)
    before.second()
    fence(before.sent)
    ring_gate_up.advance(*token)
    fence(spread_out.far)
    spread_out.cross()
    blocks = spread_out.blocks()
    grad_out_full = gathered(index, (turn(blocks[0]),) + blocks[1:])
    fence(grad_out_full)

    state = before.result()
    mixed, denom = call(
        attend_kernel,
        "attend",
        ("query", "key", "value", "valid", "state"),
        (("head", BF), ("row", F32)),
        1,
    )(turn(qkv), qkv, qkv, valid, state)
    scatter_attn = Scatter(index, projected(index, w_attn, [mixed], "out_proj", columns), seqs)
    fence(scatter_attn.got)
    scatter_attn.cross()
    fence(scatter_attn.sent_far, ring_gate_up.here())
    ring_down.advance(*token)
    ring_gate_up.advance(*token)
    resid = hidden.astype(F32) + scatter_attn.sums(*token)
    spread_resid = Spread(resid.astype(BF))
    fence(spread_resid.block, ring_down.here())
    ring_down.advance(*token)
    fence(ring_gate_up.here())
    gate_up = ring_gate_up.full(turn(index))
    fence(gate_up)
    fence(spread_resid.far)
    spread_resid.cross()
    fence(ring_down.here())
    ring_down.advance(*token)

    blocks = spread_resid.blocks()
    normed_two, inv_two = gathered(index, (turn(blocks[0]),) + blocks[1:], gains.blocks(), 1)
    fence(normed_two)
    gate = mm_tn(gate_up[0], turn(normed_two))
    fence(ring_down.here())
    ring_down.advance(*token)
    up = mm_tn(gate_up[1], normed_two)
    act = (gate * jax.nn.sigmoid(gate) * up).astype(BF)
    fence(act)
    fence(ring_down.here())
    down_full = ring_down.full(turn(index))
    fence(down_full)

    sig = jax.nn.sigmoid(gate)
    d_act = mm_tn(down_full, turn(grad_out_full))
    g_gate = (d_act * up * sig * (1.0 + gate * (1.0 - sig))).astype(BF)
    g_up = (d_act * gate * sig).astype(BF)
    inner = jnp.sum(g_gate.astype(F32) * gate + g_up.astype(F32) * up, 0, keepdims=True)
    fence(g_gate, g_up)
    scatter_two = Scatter(
        index, projected(index, gate_up, [turn(g_gate), g_up], "ffn_back", row=inner), seqs, inner
    )
    fence(scatter_two.sent)
    down_ring = Products(index, products([turn(grad_out_full)], [act], "down_grad"))
    fence(down_ring.sent)
    fence(scatter_two.got)
    scatter_two.cross()
    fence(scatter_two.sent_far)
    gate_up_ring = Products(
        index, products([normed_two, normed_two], [turn(g_gate), g_up], "gate_up_grad")
    )
    fence(gate_up_ring.sent)
    fence(down_ring.here())
    down_ring.advance(*token)
    fence(down_ring.sent)

    gain_one, gain_two = gain_attn.astype(F32)[:, None], gain_ffn.astype(F32)[:, None]
    d_norm, inner = scatter_two.sums(*token)
    gain_two_part = jnp.sum(resid * inv_two * d_norm, (0, 2))
    d_resid = (
        grad_out.astype(F32)
        + inv_two * gain_two * d_norm
        - resid * (inv_two * inv_two * inner / D)
    )
    spread_grad = Spread(d_resid.astype(BF))
    fence(spread_grad.block)
    fence(gate_up_ring.here())
    gate_up_ring.advance(*token)
    fence(gate_up_ring.sent)
    fence(down_ring.here())
    down_ring.advance(*token)
    fence(down_ring.sent)
    ffn_out = projected(index, down_full, [turn(act)], "ffn_out")
    fence(ffn_out)
    fence(spread_grad.far)
    spread_grad.cross()
    fence(down_ring.here())
    down_ring.advance(*token)
    fence(down_ring.sent)
    blocks = spread_grad.blocks()
    resid_full = gathered(index, (turn(blocks[0]),) + blocks[1:])
    g_attn = mm_tn(w_attn[:, columns:], resid_full).astype(BF)
    weighted, spread = call(
        spread_kernel, "spread", ("query", "head", "head", "row"), (("ext", BF), ("state", BF)), 0.5
    )(qkv, g_attn, mixed, denom)
    after = Before(spread, -1)
    fence(spread)
    scatter_out = Scatter(index, [tie(ffn_out[0], *token), ffn_out[1]], seqs)
    local = call(
        local_kernel,
        "local",
        ("query", "key", "value", "valid", "state", "ext"),
        (("feat", BF), ("feat", F32), ("head", F32)),
        2,
    )(turn(qkv), qkv, qkv, valid, state, weighted)
    fence(after.other)
    after.first()
    fence(after.one)
    after.second()
    fence(after.sent)
    fence(gate_up_ring.here(), local)
    gate_up_ring.advance(*token)
    fence(gate_up_ring.sent)
    fence(scatter_out.got)
    scatter_out.cross()
    down_grad = down_ring.final(*token)
    fence(down_grad)

    def later(*refs):
        later_kernel(heads, *refs)

    (d_qkv,) = call(
        later,
        "later",
        ("key", "value", "valid", "state", "feat", "feat", "head"),
        (("all", BF),),
        0.5,
    )(turn(qkv), qkv, valid, after.result(), *local)
    inner = jnp.sum(d_qkv.astype(F32) * qkv.astype(F32), 0, keepdims=True)
    scatter_one = Scatter(
        index, projected(index, w_attn, [d_qkv], "qkv_back", 0, row=inner), seqs, inner
    )
    fence(scatter_one.sent)
    attn_ring = Products(
        index, products([turn(normed_one), resid_full], [d_qkv, mixed], "attn_grad")
    )
    fence(attn_ring.sent)
    fence(scatter_one.got)
    scatter_one.cross()
    fence(scatter_one.sent_far)
    fence(attn_ring.here())
    attn_ring.advance(*token)
    fence(attn_ring.sent)
    fence(gate_up_ring.here())
    gate_up_ring.advance(*token)
    fence(gate_up_ring.sent)
    layer_out = (resid + scatter_out.sums(*token)).astype(BF)
    fence(layer_out)
    fence(attn_ring.here())
    attn_ring.advance(*token)
    fence(attn_ring.sent)
    d_norm, inner = scatter_one.sums(*token)
    value = hidden.astype(F32)
    gain_one_part = jnp.sum(value * inv_one * d_norm, (0, 2))
    grad_input = (
        d_resid + inv_one * gain_one * d_norm - value * (inv_one * inv_one * inner / D)
    )
    gain_grads = ctx_total(jnp.stack([gain_one_part, gain_two_part]))
    fence(grad_input)
    fence(attn_ring.here())
    attn_ring.advance(*token)
    fence(attn_ring.sent)
    gate_up_grad = gate_up_ring.final(*token)
    fence(gate_up_grad, gain_grads)
    attn_grad = attn_ring.final(*token)

    values, queries = heads * HEAD_DIM, heads * FEAT
    return (
        layer_out.transpose(0, 2, 1),
        grad_input.transpose(0, 2, 1),
        gain_grads[0],
        gain_grads[1],
        attn_grad[:, values : values + queries],
        attn_grad[:, values + queries : columns],
        attn_grad[:, :values],
        attn_grad[:, columns:].T,
        gate_up_grad[:, :hidden_units],
        gate_up_grad[:, hidden_units:],
        down_grad.T,
    )


def solution(mesh):
    acts, rows, columns = P(None, "ctx", "wt"), P("ctx", "wt"), P("wt", "ctx")
    in_specs = (acts, P(), P("wt"), P("wt"), rows, rows, rows, columns, rows, rows, columns, acts)
    out_specs = (acts, acts, P("wt"), P("wt"), rows, rows, rows, columns, rows, rows, columns)
    return jax.shard_map(body, mesh=mesh, in_specs=in_specs, out_specs=out_specs, check_vma=False)
```

```python
import jax
import jax.numpy as jnp
from jax import lax
from jax.experimental import pallas as pl
from jax.experimental.pallas import tpu as pltpu
from jax.sharding import PartitionSpec as P


D = 1792
FEAT = 16
HEAD_DIM = 112
EXT = 128
PHI = 160
EPS = 1e-05
BF = jnp.bfloat16
F32 = jnp.float32
ANY = pl.BlockSpec(memory_space=pl.ANY)
WHOLE = pl.BlockSpec(memory_space=pltpu.VMEM)
SMEM = pl.BlockSpec(memory_space=pltpu.SMEM)
OFFSETS = (0, 1, 2, 3, 4, -1, -2, -3)
PLACE = {offset: 1 + k for k, offset in enumerate(OFFSETS)}
PLACE[-4] = PLACE[4]


def mm_nn(left, right):
    return lax.dot_general(left, right, (((1,), (0,)), ((), ())), preferred_element_type=F32)


def mm_tn(left, right):
    return lax.dot_general(left, right, (((0,), (0,)), ((), ())), preferred_element_type=F32)


def mm_nt(left, right):
    return lax.dot_general(left, right, (((1,), (1,)), ((), ())), preferred_element_type=F32)


def tie(value, *others):
    others = jax.tree.leaves(others)
    return lax.optimization_barrier((value, *others))[0] if others else value


def params(mib=24):
    return pltpu.CompilerParams(vmem_limit_bytes=mib << 20)


def cost(flops=0, moved=4 << 20):
    return pl.CostEstimate(flops=flops, bytes_accessed=moved, transcendentals=0)


def swap(value, bit):
    count = lax.axis_size("wt")
    return lax.ppermute(value, "wt", [(i, i ^ bit) for i in range(count)])


class Spread:
    def __init__(self, block):
        self.block, self.far, self.near = block, swap(block, 2), swap(block, 1)

    def cross(self, *others):
        self.far = tie(self.far, *others)
        self.both = swap(self.far, 1)

    def blocks(self):
        return self.block, self.near, self.far, self.both


def gathered(index, blocks, gains=None, column=0):
    seqs, rows, length = blocks[0].shape

    def kernel(index_ref, *refs):
        values = [ref[0] for ref in refs[:4]]
        out = refs[8 if gains is not None else 4]
        if gains is not None:
            values = [v.astype(F32) for v in values]
            total = sum(jnp.sum(v * v, 0, keepdims=True) for v in values)
            inverse = lax.rsqrt(total / D + EPS)
            refs[9][0] = inverse
            scaled = []
            for v, gain_ref in zip(values, refs[4:8]):
                gain = gain_ref[...][:, column : column + 1].astype(F32)
                scaled.append((v * inverse * gain).astype(BF))
            values = scaled
        me = index_ref[0]
        for bit in range(4):
            out[pl.ds(pl.multiple_of((me ^ bit) * rows, 16), rows), :] = values[bit]

    block = pl.BlockSpec((1, rows, length), lambda s, index_ref: (s, 0, 0))
    full = pl.BlockSpec((4 * rows, length), lambda s, index_ref: (0, s))
    row = pl.BlockSpec((1, 1, length), lambda s, index_ref: (s, 0, 0))
    gain = pl.BlockSpec((rows, 2), lambda s, index_ref: (0, 0))
    shape = jax.ShapeDtypeStruct((4 * rows, seqs * length), BF)
    inverse = jax.ShapeDtypeStruct((seqs, 1, length), F32)
    normed = gains is not None
    return pl.pallas_call(
        kernel,
        name="gather_norm" if normed else "gather",
        grid_spec=pltpu.PrefetchScalarGridSpec(
            num_scalar_prefetch=1,
            grid=(seqs,),
            in_specs=[block] * 4 + ([gain] * 4 if normed else []),
            out_specs=[full, row] if normed else full,
        ),
        out_shape=[shape, inverse] if normed else shape,
        compiler_params=params(),
        cost_estimate=cost(1 << 30),
    )(index, *blocks, *(gains if normed else ()))


def halves(value):
    high = value.astype(BF).astype(F32)
    place = lax.broadcasted_iota(jnp.int32, (8, value.shape[1]), 0)
    return jnp.where(place == 0, high, jnp.where(place == 1, value - high, 0.0)).astype(BF)


def projected(index, weights, rights, name, columns=None, row=None):
    rows = D // 4
    depth, width = rights[0].shape
    extra = 0 if row is None else 8
    start = 0 if columns is None else columns
    stacked = weights.ndim == 3

    def kernel(index_ref, weight_ref, *refs):
        right_refs = refs[: len(rights)]
        kept = refs[-1]
        total = 0.0
        for k, right in enumerate(right_refs):
            left = weight_ref[k] if stacked else weight_ref[...][:, start : start + depth]
            total += mm_nn(left, right[...])
        step = pl.program_id(0)
        total = total.astype(BF)

        def send(sent):
            sent[:rows] = total
            if row is not None:
                sent[rows:] = halves(refs[len(rights)][...])

        for place in range(2):
            pl.when(step == place)(lambda place=place: send(refs[place - 3]))

        @pl.when(step >= 2)
        def _():
            kept[0] = total

    def of(i, index_ref):
        core = index_ref[0] % 2
        return (i % 2) * 2 + jnp.where(i < 2, 1 - core, core)

    if stacked:
        left_spec = pl.BlockSpec((len(rights), rows, depth), lambda i, r: (0, of(i, r), 0))
    else:
        left_spec = pl.BlockSpec((rows, weights.shape[1]), lambda i, r: (of(i, r), 0))
    in_specs = [left_spec] + [pl.BlockSpec((depth, width), lambda i, r: (0, 0))] * len(rights)
    if row is not None:
        in_specs.append(pl.BlockSpec((1, width), lambda i, r: (0, 0)))
    return pl.pallas_call(
        kernel,
        name=name,
        grid_spec=pltpu.PrefetchScalarGridSpec(
            num_scalar_prefetch=1,
            grid=(4,),
            in_specs=in_specs,
            out_specs=[pl.BlockSpec((rows + extra, width), lambda i, r: (0, 0))] * 2
            + [pl.BlockSpec((1, rows, width), lambda i, r: (jnp.maximum(i - 2, 0), 0, 0))],
        ),
        out_shape=[jax.ShapeDtypeStruct((rows + extra, width), BF)] * 2
        + [jax.ShapeDtypeStruct((2, rows, width), BF)],
        compiler_params=params(32),
        cost_estimate=cost(2 * D * depth * len(rights) * width, 8 << 20),
    )(index, weights, *rights, *(() if row is None else (row,)))


class Reduce:
    def __init__(self, index, parts, row=None):
        self.index, self.row = index, row
        self.sent, self.kept = tuple(parts[:2]), parts[2]
        self.got = [swap(sent, 1) for sent in self.sent]
        self.here, self.there = [], []

    def cross(self, *others):
        rows, width = self.kept.shape[1:]
        extra = self.sent[0].shape[0] - rows
        length = width // 2

        def kernel(kept_ref, got_ref, *refs):
            out = refs[-1]
            out[:rows] = (kept_ref[0].astype(F32) + got_ref[:rows].astype(F32)).astype(BF)
            if extra:
                two = got_ref[rows:].astype(F32)
                out[rows:] = halves(refs[0][...] + two[:1] + two[1:2])

        for place in range(2):
            given = (self.kept, tie(self.got[place], *others))
            given += () if self.row is None else (self.row,)
            tall = pl.BlockSpec((rows + extra, length), lambda i: (0, i))
            kept = pl.BlockSpec((1, rows, length), lambda i, place=place: (place, 0, i))
            found = pl.pallas_call(
                kernel,
                name="core_sum",
                grid=(2,),
                in_specs=[kept, tall]
                + ([] if self.row is None else [pl.BlockSpec((1, length), lambda i: (0, i))]),
                out_specs=tall,
                out_shape=jax.ShapeDtypeStruct((rows + extra, width), BF),
                compiler_params=params(),
                cost_estimate=cost(1 << 28),
            )(*given)
            self.here.append(found)
            self.there.append(swap(found, 2))


class Scatter:
    def __init__(self, index, parts, seqs, row=None):
        self.index, self.row, self.seqs = index, row, seqs
        self.sent, self.kept = tuple(parts[:2]), parts[2]
        self.got = [swap(sent, 1) for sent in self.sent]

    def cross(self, *others):
        seqs, row = self.seqs, self.row
        rows, width = self.kept.shape[1:]
        length = width // seqs
        extra = self.sent[0].shape[0] - rows
        got = (tie(self.got[0], *others), self.got[1])

        def kernel(index_ref, kept_ref, first_ref, second_ref, *refs):
            far, mine = refs[-2:] if row is None else refs[-3:-1]
            chip = index_ref[0] // 2

            def pair(place):
                got = jnp.where(place == 0, first_ref[:rows], second_ref[:rows])
                return kept_ref[place].astype(F32) + got.astype(F32)

            far[0, :rows] = pair(1 - chip).astype(BF)
            mine[0] = pair(chip)
            if row is not None:
                two = first_ref[rows:].astype(F32)
                value = refs[0][...] + two[:1] + two[1:2]
                refs[-1][0] = value
                far[0, rows:] = halves(value)

        def spec(height):
            return pl.BlockSpec((1, height, length), lambda s, r: (s, 0, 0))

        out = [((seqs, rows + extra, length), BF), ((seqs, rows, length), F32)]
        out += [] if row is None else [((seqs, 1, length), F32)]
        in_specs = [pl.BlockSpec((2, rows, length), lambda s, r: (0, 0, s))]
        in_specs += [pl.BlockSpec((rows + extra, length), lambda s, r: (0, s))] * 2
        in_specs += [] if row is None else [pl.BlockSpec((1, length), lambda s, r: (0, s))]
        found = pl.pallas_call(
            kernel,
            name="pair_sum",
            grid_spec=pltpu.PrefetchScalarGridSpec(
                num_scalar_prefetch=1,
                grid=(seqs,),
                in_specs=in_specs,
                out_specs=[spec(shape[1]) for shape, _ in out],
            ),
            out_shape=[jax.ShapeDtypeStruct(*o) for o in out],
            compiler_params=params(),
            cost_estimate=cost(1 << 28),
        )(self.index, self.kept, *got, *(() if row is None else (row,)))
        self.sent_far, self.mine, self.rows = found[0], found[1], rows
        self.half = None if row is None else found[2]
        self.last = swap(self.sent_far, 2)

    def sums(self, *others):
        last = tie(self.last, *others)
        total = self.mine + last[:, : self.rows].astype(F32)
        if self.row is None:
            return total
        two = last[:, self.rows : self.rows + 2].astype(F32)
        return total, self.half + two[:, :1] + two[:, 1:]


def resid_added(index, reduce, own, far, *others):
    seqs, rows, length = own.shape
    width = seqs * length

    def kernel(index_ref, here_0, here_1, there_0, there_1, own_ref, far_ref, resid, both_0, both_1):
        chip = index_ref[0] // 2
        given = (here_0, there_0, both_0), (here_1, there_1, both_1)
        for place, (here, there, both) in enumerate(given):
            mine = chip == place
            base = jnp.where(mine, own_ref[0].astype(F32), far_ref[0].astype(F32))
            value = base + (here[...].astype(F32) + there[...].astype(F32))
            both[...] = value.astype(BF)

            @pl.when(mine)
            def _():
                resid[0] = value

    wide = pl.BlockSpec((rows, length), lambda s, r: (0, s))
    one = pl.BlockSpec((1, rows, length), lambda s, r: (s, 0, 0))
    resid, *both = pl.pallas_call(
        kernel,
        name="resid",
        grid_spec=pltpu.PrefetchScalarGridSpec(
            num_scalar_prefetch=1,
            grid=(seqs,),
            in_specs=[wide] * 4 + [one, one],
            out_specs=[one, wide, wide],
        ),
        out_shape=[jax.ShapeDtypeStruct((seqs, rows, length), F32)]
        + [jax.ShapeDtypeStruct((rows, width), BF)] * 2,
        compiler_params=params(),
        cost_estimate=cost(1 << 28),
    )(index, *reduce.here, tie(reduce.there[0], *others), reduce.there[1], own, far)
    return resid, both


def resid_back(index, reduce, grad_own, grad_far, resid, resid_both, inverse, gains, *others):
    seqs, rows, length = grad_own.shape
    width = seqs * length

    def kernel(index_ref, *refs):
        here, there, held_both, both = refs[:2], refs[2:4], refs[4:6], refs[-3:-1]
        own_ref, far_ref, resid_ref, inverse_ref, own_gain_ref, far_gain_ref, grad = refs[6:13]
        chip = index_ref[0] // 2
        tail = here[0][rows:].astype(F32) + there[0][rows:].astype(F32)
        inv = inverse_ref[0]
        scale = inv * inv * (tail[:1] + tail[1:2]) / D
        own_gain_column = own_gain_ref[...][:, 1:2].astype(F32)
        far_gain_column = far_gain_ref[...][:, 1:2].astype(F32)
        for place in range(2):
            mine = chip == place
            normed = here[place][:rows].astype(F32) + there[place][:rows].astype(F32)
            base = jnp.where(mine, own_ref[0].astype(F32), far_ref[0].astype(F32))
            gain = jnp.where(mine, own_gain_column, far_gain_column)
            most = base + inv * gain * normed
            both[place][...] = (most - held_both[place][...].astype(F32) * scale).astype(BF)

            @pl.when(mine)
            def _():
                held = resid_ref[0]
                grad[0] = most - held * scale
                refs[-1][0] = jnp.sum(held * inv * normed, 1, keepdims=True)

    wide = pl.BlockSpec((rows, length), lambda s, r: (0, s))
    more = pl.BlockSpec((rows + 8, length), lambda s, r: (0, s))
    one = pl.BlockSpec((1, rows, length), lambda s, r: (s, 0, 0))
    row = pl.BlockSpec((1, 1, length), lambda s, r: (s, 0, 0))
    gain = pl.BlockSpec((rows, 2), lambda s, r: (0, 0))
    grad, *both, gain_sum = pl.pallas_call(
        kernel,
        name="resid_back",
        grid_spec=pltpu.PrefetchScalarGridSpec(
            num_scalar_prefetch=1,
            grid=(seqs,),
            in_specs=[more] * 4 + [wide] * 2 + [one, one, one, row, gain, gain],
            out_specs=[one, wide, wide, pl.BlockSpec((1, rows, 1), lambda s, r: (s, 0, 0))],
        ),
        out_shape=[jax.ShapeDtypeStruct((seqs, rows, length), F32)]
        + [jax.ShapeDtypeStruct((rows, width), BF)] * 2
        + [jax.ShapeDtypeStruct((seqs, rows, 1), F32)],
        compiler_params=params(),
        cost_estimate=cost(1 << 28),
    )(
        index,
        *reduce.here,
        tie(reduce.there[0], *others),
        reduce.there[1],
        *resid_both,
        grad_own,
        grad_far,
        resid,
        inverse,
        *gains,
    )
    return grad, both, gain_sum


def gathered_pair(index, here, there, seqs, gains=None, column=0):
    rows, width = here[0].shape
    length = width // seqs
    normed = gains is not None

    def kernel(index_ref, *refs):
        me = index_ref[0]
        chip, core = me // 2, me % 2
        blocks = refs[:2], refs[2:4]
        out = refs[8 if normed else 4]
        if normed:
            total = 0.0
            for ref in refs[:4]:
                value = ref[...].astype(F32)
                total += jnp.sum(value * value, 0, keepdims=True)
            inverse = lax.rsqrt(total / D + EPS)
            refs[9][0] = inverse
            columns = [ref[...][:, column : column + 1].astype(F32) for ref in refs[4:8]]
        for other in range(2):
            for place in range(2):
                value = blocks[other][place][...]
                if normed:
                    gain = jnp.where(chip == place, columns[other], columns[2 + other])
                    value = (value.astype(F32) * inverse * gain).astype(BF)
                row = 2 * place + (core ^ other)
                out[pl.ds(pl.multiple_of(row * rows, 16), rows), :] = value

    wide = pl.BlockSpec((rows, length), lambda s, r: (0, s))
    full = pl.BlockSpec((4 * rows, length), lambda s, r: (0, s))
    row = pl.BlockSpec((1, 1, length), lambda s, r: (s, 0, 0))
    gain = pl.BlockSpec((rows, 2), lambda s, r: (0, 0))
    shape = jax.ShapeDtypeStruct((4 * rows, width), BF)
    inverse = jax.ShapeDtypeStruct((seqs, 1, length), F32)
    return pl.pallas_call(
        kernel,
        name="pair_norm" if normed else "pair",
        grid_spec=pltpu.PrefetchScalarGridSpec(
            num_scalar_prefetch=1,
            grid=(seqs,),
            in_specs=[wide] * 4 + ([gain] * 4 if normed else []),
            out_specs=[full, row] if normed else full,
        ),
        out_shape=[shape, inverse] if normed else shape,
        compiler_params=params(),
        cost_estimate=cost(1 << 30),
    )(index, *here, *there, *(gains if normed else ()))


def ring_order(count):
    half = count // 2
    return [2 * r for r in range(half)] + [2 * r + 1 for r in reversed(range(half))]


def ringed():
    return lax.axis_size("ctx") == 8


def hop(value, step):
    order = ring_order(lax.axis_size("ctx"))
    count = len(order)
    pairs = [(order[r], order[(r + step) % count]) for r in range(count)]
    return lax.ppermute(value, "ctx", pairs)


def places():
    count = lax.axis_size("ctx")
    order = ring_order(count)
    place = {device: r for r, device in enumerate(order)}
    table = [[0] + [order[(place[i] + offset) % count] for offset in OFFSETS] for i in range(count)]
    found = jnp.array(table, jnp.int32)[lax.axis_index("ctx")]
    return found + jnp.where(jnp.arange(len(OFFSETS) + 1) == 0, lax.axis_index("wt"), 0)


class Gather:
    def __init__(self, shard):
        self.shard, self.axis, self.sent = shard, shard.ndim - 2, ()
        self.right, self.left = [shard], [shard]

    def advance(self, *others):
        if not ringed():
            return
        right, left = self.right[-1], self.left[-1]
        if len(self.right) == 4:
            rows = right.shape[self.axis]
            right = lax.slice_in_dim(right, 0, rows // 2, axis=self.axis)
            left = lax.slice_in_dim(left, rows // 2, rows, axis=self.axis)
        others = jax.tree.leaves(others)
        if others:
            right, left = lax.optimization_barrier((right, left, *others))[:2]
        self.sent = right, left
        self.right.append(hop(right, 1))
        self.left.append(hop(left, -1))

    def here(self):
        return (self.right[-1], self.left[-1]) if ringed() else ()

    def full(self, index):
        if not ringed():
            return lax.all_gather(self.shard, "ctx", axis=self.axis, tiled=True)
        rows = self.shard.shape[self.axis]
        pieces = self.right + self.left[1:]
        offsets = (0, -1, -2, -3, 4, 1, 2, 3, 4)
        count = len(pieces)

        def kernel(index_ref, *refs):
            out, sems = refs[count], refs[count + 1]
            copies = []
            for k in range(count):
                first = index_ref[PLACE[offsets[k]]] * rows + (rows // 2 if k == 8 else 0)
                at = pl.ds(pl.multiple_of(first, 16), pieces[k].shape[-2])
                where = out.at[at, :] if len(out.shape) == 2 else out.at[:, at, :]
                copies.append(pltpu.make_async_copy(refs[k], where, sems.at[k]))
                copies[-1].start()
            for copy in copies:
                copy.wait()

        shape = self.shard.shape[:-2] + (rows * 8, self.shard.shape[-1])
        return pl.pallas_call(
            kernel,
            name="assemble",
            in_specs=[SMEM] + [ANY] * count,
            out_specs=WHOLE,
            out_shape=jax.ShapeDtypeStruct(shape, BF),
            scratch_shapes=[pltpu.SemaphoreType.DMA((count,))],
            compiler_params=params(),
            cost_estimate=cost(),
        )(index, *pieces)


def products(lefts, rights, name):
    rows, length = lefts[0].shape
    widths = [r.shape[0] for r in rights]
    used = lefts[:1] if all(left is lefts[0] for left in lefts) else lefts

    def kernel(*refs):
        out = refs[-1]
        first = 0
        for k, width in enumerate(widths):
            left = refs[k if len(used) > 1 else 0]
            out[:, pl.ds(first, width)] = mm_nt(left[...], refs[len(used) + k][...]).astype(BF)
            first += width

    return pl.pallas_call(
        kernel,
        name=name,
        grid=(4,),
        in_specs=[pl.BlockSpec((rows // 4, length), lambda i: (i, 0))] * len(used)
        + [pl.BlockSpec((width, length), lambda i: (0, 0)) for width in widths],
        out_specs=pl.BlockSpec((rows // 4, sum(widths)), lambda i: (i, 0)),
        out_shape=jax.ShapeDtypeStruct((rows, sum(widths)), BF),
        compiler_params=params(32),
        cost_estimate=cost(2 * rows * length * sum(widths), 2 * rows * sum(widths)),
    )(*used, *rights)


class Products:
    def __init__(self, index, full):
        self.index, self.full, self.step, self.sent = index, full, 4, ()
        if ringed():
            self.rows, self.width = full.shape[0] // 8, full.shape[1]
            self._send()

    def _send(self):
        half, step = self.rows // 2, self.step
        first, second = step == 4, step == 3

        def kernel(index_ref, *refs):
            row = pl.program_id(0)
            if first:
                own, right, left = refs

                @pl.when(row == 0)
                def _():
                    right[...] = own[...]

                @pl.when(row == 1)
                def _():
                    left[...] = own[...]

                return
            from_right, from_left, own_right, own_left, right, left = refs
            more_right, more_left = from_right[...].astype(F32), from_left[...].astype(F32)
            if second:
                more_right = jnp.where(row == 0, more_right, 0.0)
                more_left = jnp.where(row == 1, more_left, 0.0)
            right[...] = (own_right[...].astype(F32) + more_right).astype(BF)
            left[...] = (own_left[...].astype(F32) + more_left).astype(BF)

        def own(offset):
            return pl.BlockSpec((half, self.width), lambda i, r: (r[PLACE[offset]] * 2 + i, 0))

        still = pl.BlockSpec((half, self.width), lambda i, r: (0, 0))
        moving = pl.BlockSpec((half, self.width), lambda i, r: (i, 0))
        if first:
            in_specs, out_spec, given, rows = [own(4)], still, (self.full,), half
        else:
            in_specs = [still if second else moving] * 2 + [own(step), own(-step)]
            out_spec, given, rows = moving, (self.right, self.left, self.full, self.full), self.rows
        self.sent = pl.pallas_call(
            kernel,
            name="ring_sum",
            grid_spec=pltpu.PrefetchScalarGridSpec(
                num_scalar_prefetch=1, grid=(2,), in_specs=in_specs, out_specs=[out_spec] * 2
            ),
            out_shape=[jax.ShapeDtypeStruct((rows, self.width), BF)] * 2,
            compiler_params=params(),
            cost_estimate=cost(1 << 24),
        )(self.index, *given)
        self.right, self.left = hop(self.sent[0], 1), hop(self.sent[1], -1)

    def here(self):
        return (self.right, self.left) if ringed() else ()

    def advance(self, *others):
        if ringed():
            self.step -= 1
            self.right = tie(self.right, self.left, *others)
            self._send()

    def final(self, *others):
        if not ringed():
            return lax.psum_scatter(self.full, "ctx", scatter_dimension=0, tiled=True).astype(F32)
        right = tie(self.right, self.left, *others)

        def kernel(index_ref, own, right_ref, left_ref, out):
            out[...] = own[...].astype(F32) + right_ref[...].astype(F32) + left_ref[...].astype(F32)

        half = self.rows // 2
        moving = pl.BlockSpec((half, self.width), lambda i, r: (i, 0))
        own = pl.BlockSpec((half, self.width), lambda i, r: (r[PLACE[0]] * 2 + i, 0))
        return pl.pallas_call(
            kernel,
            name="ring_end",
            grid_spec=pltpu.PrefetchScalarGridSpec(
                num_scalar_prefetch=1, grid=(2,), in_specs=[own, moving, moving], out_specs=moving
            ),
            out_shape=jax.ShapeDtypeStruct((self.rows, self.width), F32),
            compiler_params=params(),
            cost_estimate=cost(1 << 24),
        )(self.index, self.full, right, self.left)


def shifted(value, by):
    count = lax.axis_size("ctx")
    pairs = [(i, i + by) for i in range(count) if 0 <= i + by < count]
    return lax.ppermute(value, "ctx", pairs)


class Before:
    def __init__(self, value, sign):
        self.value, self.sign = value, sign
        self.other = self.one = self.two = self.sent = ()
        if ringed():
            count = lax.axis_size("ctx")
            self.other = lax.ppermute(value, "ctx", [(i, i ^ 1) for i in range(count)])

    def first(self, *others):
        if ringed():
            other = tie(self.other, *others)
            self.total = (self.value.astype(F32) + other.astype(F32)).astype(BF)
            self.one = shifted(self.total, 2 * self.sign)

    def second(self, *others):
        if ringed():
            one = tie(self.one, *others)
            self.sent = (self.total.astype(F32) + one.astype(F32)).astype(BF)
            self.two = shifted(self.sent, 4 * self.sign)

    def result(self):
        count, index = lax.axis_size("ctx"), lax.axis_index("ctx")
        if not ringed():
            everything = lax.all_gather(self.value, "ctx").astype(F32)
            place = jnp.arange(count)
            keep = (place < index) if self.sign > 0 else (place > index)
            keep = keep.reshape((count,) + (1,) * self.value.ndim)
            return jnp.sum(jnp.where(keep, everything, 0.0), 0).astype(BF)
        behind = (index & 1) == (1 if self.sign > 0 else 0)
        result = self.one.astype(F32) + self.two.astype(F32)
        return (result + jnp.where(behind, self.other.astype(F32), 0.0)).astype(BF)


def ctx_total(value):
    if not ringed():
        return lax.psum(value, "ctx")
    for bit in (1, 2, 4):
        value = value + lax.ppermute(value, "ctx", [(i, i ^ bit) for i in range(8)])
    return value


def turned(rows, by):
    return jnp.concatenate([rows[by:], rows[:by]], 0)


def feature_rows(vectors, square, cross, linear):
    length = vectors.shape[1]
    half = FEAT // 2
    pieces = [vectors * vectors * square]
    pieces += [vectors * turned(vectors, by) * cross for by in range(1, half)]
    pieces += [vectors[:half] * vectors[half:] * cross]
    place = lax.broadcasted_iota(jnp.int32, (half, length), 0)
    pieces += [jnp.where(place == 0, 1.0, 0.0), vectors * linear]
    return jnp.concatenate(pieces, 0).astype(BF)


def feature_pull(grad, vectors, square, cross, linear):
    half = FEAT // 2
    total = 2.0 * square * grad[:FEAT] * vectors
    for by in range(1, half):
        part = grad[FEAT * by : FEAT * (by + 1)] * cross
        total += part * turned(vectors, by) + turned(part * vectors, FEAT - by)
    part = grad[FEAT * half : FEAT * half + half] * cross
    total += jnp.concatenate([part * vectors[half:], part * vectors[:half]], 0)
    return total + grad[PHI - FEAT :] * linear


QUERY_SCALE = (1.0 / 32.0, 1.0 / 16.0, 0.25)
KEY_SCALE = (1.0, 1.0, 1.0)


def extended(value, valid):
    place = lax.broadcasted_iota(jnp.int32, (EXT - HEAD_DIM, value.shape[1]), 0)
    tail = jnp.where(place == 0, jnp.broadcast_to(valid, place.shape), 0.0)
    return jnp.concatenate([(value.astype(F32) * valid).astype(BF), tail.astype(BF)], 0)


def causal_of(length):
    key_place = lax.broadcasted_iota(jnp.int32, (length, length), 0)
    query_place = lax.broadcasted_iota(jnp.int32, (length, length), 1)
    return key_place <= query_place


def state_kernel(key_ref, value_ref, valid_ref, state_ref):
    mapped = feature_rows(key_ref[...].astype(F32), *KEY_SCALE)
    state_ref[0, 0] = mm_nt(mapped, extended(value_ref[...], valid_ref[0])).astype(BF)


def attend_kernel(query_ref, key_ref, value_ref, valid_ref, state_ref, mixed_ref, denom_ref):
    query = query_ref[...]
    scores = mm_tn(key_ref[...], query) * 0.25
    weights = jnp.where(causal_of(query.shape[1]), 1.0 + scores + 0.5 * scores * scores, 0.0)
    total = mm_nn(extended(value_ref[...], valid_ref[0]), weights.astype(BF))
    mapped = feature_rows(query.astype(F32), *QUERY_SCALE)
    total += mm_tn(state_ref[0, 0], mapped)
    denom = total[HEAD_DIM : HEAD_DIM + 1]
    denom_ref[0, 0] = denom
    mixed_ref[...] = (total[:HEAD_DIM] / denom).astype(BF)


def spread_kernel(query_ref, grad_ref, mixed_ref, denom_ref, weighted_ref, state_ref):
    weighted = grad_ref[...].astype(F32) / denom_ref[0, 0]
    shift = jnp.sum(weighted * mixed_ref[...].astype(F32), 0, keepdims=True)
    place = lax.broadcasted_iota(jnp.int32, (EXT - HEAD_DIM, weighted.shape[1]), 0)
    tail = jnp.where(place == 0, -jnp.broadcast_to(shift, place.shape), 0.0)
    whole = jnp.concatenate([weighted, tail], 0).astype(BF)
    weighted_ref[0, 0] = whole
    mapped = feature_rows(query_ref[...].astype(F32), *QUERY_SCALE)
    state_ref[0, 0] = mm_nt(mapped, whole).astype(BF)


def local_kernel(
    query_ref, key_ref, value_ref, valid_ref, state_ref, weighted_ref, dq_ref, dk_ref, dv_ref
):
    query, key_in, weighted = query_ref[...], key_ref[...], weighted_ref[0, 0]
    causal = causal_of(query.shape[1])
    scores = mm_tn(key_in, query) * 0.25
    weights = jnp.where(causal, 1.0 + scores + 0.5 * scores * scores, 0.0).astype(BF)
    dv_ref[...] = mm_nt(weighted[:HEAD_DIM], weights) * valid_ref[0]
    slope = mm_tn(extended(value_ref[...], valid_ref[0]), weighted)
    slope = jnp.where(causal, slope * (1.0 + scores), 0.0).astype(BF)
    mapped = mm_nn(state_ref[0, 0], weighted)
    pulled = feature_pull(mapped, query.astype(F32), *QUERY_SCALE)
    dq_ref[...] = (mm_nn(key_in, slope) * 0.25 + pulled).astype(BF)
    dk_ref[...] = mm_nt(query, slope) * 0.25


def later_kernel(heads, key_ref, value_ref, valid_ref, state_ref, dq_in, dk_in, dv_in, out_ref):
    head = pl.program_id(1)
    key_in = key_ref[...].astype(F32)
    valid = valid_ref[0]
    mapped = mm_nn(state_ref[0, 0], extended(value_ref[...], valid))
    d_key = (dk_in[...] + feature_pull(mapped, key_in, *KEY_SCALE)).astype(BF)
    spread = mm_tn(state_ref[0, 0], feature_rows(key_in, *KEY_SCALE))
    d_value = (dv_in[...] + spread[:HEAD_DIM] * valid).astype(BF)
    values, queries = heads * HEAD_DIM, heads * FEAT
    out_ref[pl.ds(pl.multiple_of(head * HEAD_DIM, 16), HEAD_DIM), :] = d_value
    out_ref[pl.ds(pl.multiple_of(values + head * FEAT, 16), FEAT), :] = dq_in[...]
    out_ref[pl.ds(pl.multiple_of(values + queries + head * FEAT, 16), FEAT), :] = d_key


def head_call(kernel, name, seqs, heads, length, ins, outs, flops):
    first_query = heads * HEAD_DIM // FEAT
    columns = heads * (HEAD_DIM + 2 * FEAT)
    specs = {
        "value": pl.BlockSpec((HEAD_DIM, length), lambda s, h: (h, s)),
        "query": pl.BlockSpec((FEAT, length), lambda s, h: (first_query + h, s)),
        "key": pl.BlockSpec((FEAT, length), lambda s, h: (first_query + heads + h, s)),
        "all": pl.BlockSpec((columns, length), lambda s, h: (0, s)),
        "feat": pl.BlockSpec((FEAT, length), lambda s, h: (h, s)),
        "head": pl.BlockSpec((HEAD_DIM, length), lambda s, h: (h, s)),
        "valid": pl.BlockSpec((1, 1, length), lambda s, h: (s, 0, 0)),
        "state": pl.BlockSpec((1, 1, PHI, EXT), lambda s, h: (s, h, 0, 0)),
        "row": pl.BlockSpec((1, 1, 1, length), lambda s, h: (s, h, 0, 0)),
        "ext": pl.BlockSpec((1, 1, EXT, length), lambda s, h: (s, h, 0, 0)),
    }
    shapes = {
        "all": (columns, seqs * length),
        "feat": (heads * FEAT, seqs * length),
        "head": (heads * HEAD_DIM, seqs * length),
        "state": (seqs, heads, PHI, EXT),
        "row": (seqs, heads, 1, length),
        "ext": (seqs, heads, EXT, length),
    }
    return pl.pallas_call(
        kernel,
        name=name,
        grid=(seqs, heads),
        in_specs=[specs[i] for i in ins],
        out_specs=[specs[o] for o, _ in outs],
        out_shape=[jax.ShapeDtypeStruct(shapes[o], kind) for o, kind in outs],
        compiler_params=params(),
        cost_estimate=cost(flops),
    )


def body(
    hidden_in,
    lengths,
    gain_attn,
    gain_ffn,
    w_query,
    w_key,
    w_value,
    w_output,
    w_gate,
    w_up,
    w_down,
    cotangent,
):
    seqs, length, width = hidden_in.shape
    heads = w_value.shape[1] // HEAD_DIM
    hidden_units = w_gate.shape[1]
    columns = heads * (HEAD_DIM + 2 * FEAT)
    index = places()
    position = lax.axis_index("ctx") * length + jnp.arange(length, dtype=jnp.int32)
    valid = (position[None, :] < lengths[:, None]).astype(F32)[:, None, :]
    hidden = hidden_in.transpose(0, 2, 1)
    unit = seqs * heads * 2 * length * length * 256
    token = [jnp.zeros((8, 128), F32)]

    def call(kernel, name, ins, outs, share):
        return head_call(kernel, name, seqs, heads, length, ins, outs, int(unit * share))

    def turn(value, *others):
        return tie(value, token[0], *others)

    def fence(*values):
        token[0] = tie(token[0], *values)

    ring_attn = Gather(jnp.concatenate([w_value, w_query, w_key, w_output.T], 1))
    ring_down = Gather(w_down.T)
    ring_gate_up = Gather(jnp.stack([w_gate, w_up]))
    ring_attn.advance()
    spread_in = Spread(hidden)
    gains = Spread(jnp.stack([gain_attn, gain_ffn], 1))
    gains.cross()
    fence(ring_attn.here())
    ring_attn.advance(*token)
    fence(ring_attn.here(), ring_gate_up.shard)
    ring_attn.advance(*token)
    spread_in.cross(*token)
    grad_out = (cotangent.transpose(0, 2, 1).astype(F32) * valid).astype(BF)
    spread_out = Spread(tie(grad_out, spread_in.far))
    fence(ring_attn.here())
    ring_attn.advance(*token)
    ring_gate_up.advance(ring_attn.sent)
    fence(spread_in.near, spread_in.both)
    blocks = spread_in.blocks()
    normed_one, inv_one = gathered(index, (turn(blocks[0]),) + blocks[1:], gains.blocks(), 0)
    fence(normed_one)
    fence(ring_attn.here())
    w_attn = ring_attn.full(turn(index))

    qkv = mm_tn(w_attn[:, :columns], normed_one).astype(BF)
    (own,) = call(state_kernel, "state", ("key", "value", "valid"), (("state", BF),), 0.5)(
        qkv, qkv, valid
    )
    before = Before(own, 1)
    fence(own)
    fence(before.other)
    before.first(*token)
    fence(before.total if ringed() else ())
    fence(ring_gate_up.here())
    ring_gate_up.advance(*token)
    fence(before.one)
    before.second(*token)
    fence(before.sent)
    spread_out.cross(*token)
    blocks = spread_out.blocks()
    grad_out_full = gathered(index, (turn(blocks[0]),) + blocks[1:])
    fence(grad_out_full)
    fence(ring_gate_up.here())
    ring_gate_up.advance(*token)

    state = before.result()
    mixed, denom = call(
        attend_kernel,
        "attend",
        ("query", "key", "value", "valid", "state"),
        (("head", BF), ("row", F32)),
        1,
    )(turn(qkv), qkv, qkv, valid, state)
    scatter_attn = Scatter(index, projected(index, w_attn, [mixed], "out_proj", columns), seqs)
    fence(scatter_attn.sent)
    scatter_attn.cross(*token)
    fence(scatter_attn.sent_far)
    fence(ring_gate_up.here())
    ring_gate_up.advance(*token)
    ring_down.advance(*token)
    resid = hidden.astype(F32) + scatter_attn.sums(*token)
    spread_resid = Spread(resid.astype(BF))
    fence(spread_resid.block)
    fence(ring_gate_up.here(), ring_down.here())
    ring_down.advance(*token)
    gate_up = ring_gate_up.full(turn(index))
    fence(gate_up)
    fence(ring_down.here())
    ring_down.advance(*token)
    spread_resid.cross(*token)

    blocks = spread_resid.blocks()
    normed_two, inv_two = gathered(index, blocks, gains.blocks(), 1)
    fence(normed_two)
    fence(ring_down.here())
    ring_down.advance(*token)
    gate = mm_tn(gate_up[0], turn(normed_two))
    up = mm_tn(gate_up[1], normed_two)
    act = (gate * jax.nn.sigmoid(gate) * up).astype(BF)
    fence(act)
    fence(ring_down.here())
    down_full = ring_down.full(turn(index))
    fence(down_full)

    sig = jax.nn.sigmoid(gate)
    d_act = mm_tn(down_full, turn(grad_out_full))
    g_gate = (d_act * up * sig * (1.0 + gate * (1.0 - sig))).astype(BF)
    g_up = (d_act * gate * sig).astype(BF)
    inner = jnp.sum(g_gate.astype(F32) * gate + g_up.astype(F32) * up, 0, keepdims=True)
    fence(g_gate, g_up)
    scatter_two = Scatter(
        index, projected(index, gate_up, [turn(g_gate), g_up], "ffn_back", row=inner), seqs, inner
    )
    fence(scatter_two.sent)
    down_ring = Products(index, products([turn(grad_out_full)], [act], "down_grad"))
    fence(down_ring.sent)
    scatter_two.cross(*token)
    fence(scatter_two.sent_far)
    gate_up_ring = Products(
        index, products([normed_two, normed_two], [turn(g_gate), g_up], "gate_up_grad")
    )
    fence(gate_up_ring.sent)
    fence(down_ring.here())
    down_ring.advance(*token)
    fence(down_ring.sent)

    gain_one, gain_two = gain_attn.astype(F32)[:, None], gain_ffn.astype(F32)[:, None]
    d_norm, inner = scatter_two.sums(*token)
    gain_two_part = jnp.sum(resid * inv_two * d_norm, (0, 2))
    d_resid = (
        grad_out.astype(F32)
        + inv_two * gain_two * d_norm
        - resid * (inv_two * inv_two * inner / D)
    )
    spread_grad = Spread(d_resid.astype(BF))
    fence(spread_grad.block)
    fence(gate_up_ring.here())
    gate_up_ring.advance(*token)
    fence(gate_up_ring.sent)
    ffn_out = projected(index, down_full, [turn(act)], "ffn_out")
    fence(ffn_out)
    fence(down_ring.here())
    down_ring.advance(*token)
    fence(down_ring.sent)
    spread_grad.cross(*token)
    blocks = spread_grad.blocks()
    resid_full = gathered(index, blocks)
    fence(resid_full)
    g_attn = mm_tn(w_attn[:, columns:], turn(resid_full)).astype(BF)
    weighted, spread = call(
        spread_kernel, "spread", ("query", "head", "head", "row"), (("ext", BF), ("state", BF)), 0.5
    )(turn(qkv), g_attn, mixed, denom)
    after = Before(spread, -1)
    fence(spread)
    fence(gate_up_ring.here())
    fence(after.other)
    after.first(*token)
    fence(after.total if ringed() else ())
    scatter_out = Scatter(index, [*lax.optimization_barrier((*ffn_out, *token))[:3]], seqs)
    fence(after.one)
    after.second(*token)
    fence(after.sent)
    gate_up_ring.advance(*token)
    fence(gate_up_ring.sent)
    scatter_out.cross(*token)
    fence(scatter_out.sent_far)
    local = call(
        local_kernel,
        "local",
        ("query", "key", "value", "valid", "state", "ext"),
        (("feat", BF), ("feat", F32), ("head", F32)),
        2,
    )(turn(qkv), qkv, qkv, valid, state, weighted)
    fence(local)

    def later(*refs):
        later_kernel(heads, *refs)

    (d_qkv,) = call(
        later,
        "later",
        ("key", "value", "valid", "state", "feat", "feat", "head"),
        (("all", BF),),
        0.5,
    )(turn(qkv), qkv, valid, after.result(), *local)
    inner = jnp.sum(d_qkv.astype(F32) * qkv.astype(F32), 0, keepdims=True)
    scatter_one = Scatter(
        index, projected(index, w_attn, [d_qkv], "qkv_back", row=inner), seqs, inner
    )
    fence(scatter_one.sent)
    fence(down_ring.here())
    down_ring.advance(*token)
    fence(down_ring.sent)
    attn_ring = Products(
        index, products([turn(normed_one), resid_full], [d_qkv, mixed], "attn_grad")
    )
    fence(attn_ring.sent)
    fence(gate_up_ring.here())
    gate_up_ring.advance(*token)
    fence(gate_up_ring.sent)
    scatter_one.cross(*token)
    fence(scatter_one.sent_far)
    fence(attn_ring.here())
    attn_ring.advance(*token)
    fence(attn_ring.sent)
    layer_out = (resid + scatter_out.sums(*token)).astype(BF)
    fence(layer_out)
    d_norm, inner = scatter_one.sums(*token)
    value = hidden.astype(F32)
    gain_one_part = jnp.sum(value * inv_one * d_norm, (0, 2))
    grad_input = (
        d_resid + inv_one * gain_one * d_norm - value * (inv_one * inv_one * inner / D)
    )
    fence(gain_one_part, grad_input)
    gain_grads = ctx_total(jnp.stack([gain_one_part, gain_two_part]) + token[0][:1, :1])
    fence(attn_ring.here())
    attn_ring.advance(*token)
    fence(attn_ring.sent)
    down_grad = down_ring.final(*token)
    fence(down_grad)
    fence(attn_ring.here())
    attn_ring.advance(*token)
    fence(attn_ring.sent)
    gate_up_grad = gate_up_ring.final(*token)
    fence(gate_up_grad)
    fence(gain_grads)
    attn_grad = attn_ring.final(*token)

    values, queries = heads * HEAD_DIM, heads * FEAT
    return (
        layer_out.transpose(0, 2, 1),
        grad_input.transpose(0, 2, 1),
        gain_grads[0],
        gain_grads[1],
        attn_grad[:, values : values + queries],
        attn_grad[:, values + queries : columns],
        attn_grad[:, :values],
        attn_grad[:, columns:].T,
        gate_up_grad[:, :hidden_units],
        gate_up_grad[:, hidden_units:],
        down_grad.T,
    )


def solution(mesh):
    acts, rows, columns = P(None, "ctx", "wt"), P("ctx", "wt"), P("wt", "ctx")
    in_specs = (acts, P(), P("wt"), P("wt"), rows, rows, rows, columns, rows, rows, columns, acts)
    out_specs = (acts, acts, P("wt"), P("wt"), rows, rows, rows, columns, rows, rows, columns)
    return jax.shard_map(body, mesh=mesh, in_specs=in_specs, out_specs=out_specs, check_vma=False)
```

```python
import jax
import jax.numpy as jnp
from jax import lax
from jax.experimental import pallas as pl
from jax.experimental.pallas import tpu as pltpu
from jax.sharding import PartitionSpec as P


D = 1792
FEAT = 16
HEAD_DIM = 112
EXT = 128
PHI = 160
EPS = 1e-05
BF = jnp.bfloat16
F32 = jnp.float32
ANY = pl.BlockSpec(memory_space=pl.ANY)
WHOLE = pl.BlockSpec(memory_space=pltpu.VMEM)
SMEM = pl.BlockSpec(memory_space=pltpu.SMEM)
OFFSETS = (0, 1, 2, 3, 4, -1, -2, -3)
PLACE = {offset: 1 + k for k, offset in enumerate(OFFSETS)}
PLACE[-4] = PLACE[4]


def mm_nn(left, right):
    return lax.dot_general(left, right, (((1,), (0,)), ((), ())), preferred_element_type=F32)


def mm_tn(left, right):
    return lax.dot_general(left, right, (((0,), (0,)), ((), ())), preferred_element_type=F32)


def mm_nt(left, right):
    return lax.dot_general(left, right, (((1,), (1,)), ((), ())), preferred_element_type=F32)


def tie(value, *others):
    others = jax.tree.leaves(others)
    return lax.optimization_barrier((value, *others))[0] if others else value


def params(mib=24):
    return pltpu.CompilerParams(vmem_limit_bytes=mib << 20)


def cost(flops=0, moved=4 << 20):
    return pl.CostEstimate(flops=flops, bytes_accessed=moved, transcendentals=0)


def swap(value, bit):
    count = lax.axis_size("wt")
    return lax.ppermute(value, "wt", [(i, i ^ bit) for i in range(count)])


class Spread:
    def __init__(self, block):
        self.block, self.far, self.near = block, swap(block, 2), swap(block, 1)

    def cross(self, *others):
        self.far = tie(self.far, *others)
        self.both = swap(self.far, 1)

    def blocks(self):
        return self.block, self.near, self.far, self.both


def gathered(index, blocks, gains=None, column=0):
    seqs, rows, length = blocks[0].shape

    def kernel(index_ref, *refs):
        values = [ref[0] for ref in refs[:4]]
        out = refs[8 if gains is not None else 4]
        if gains is not None:
            values = [v.astype(F32) for v in values]
            total = sum(jnp.sum(v * v, 0, keepdims=True) for v in values)
            inverse = lax.rsqrt(total / D + EPS)
            refs[9][0] = inverse
            scaled = []
            for v, gain_ref in zip(values, refs[4:8]):
                gain = gain_ref[...][:, column : column + 1].astype(F32)
                scaled.append((v * inverse * gain).astype(BF))
            values = scaled
        me = index_ref[0]
        for bit in range(4):
            out[pl.ds(pl.multiple_of((me ^ bit) * rows, 16), rows), :] = values[bit]

    block = pl.BlockSpec((1, rows, length), lambda s, index_ref: (s, 0, 0))
    full = pl.BlockSpec((4 * rows, length), lambda s, index_ref: (0, s))
    row = pl.BlockSpec((1, 1, length), lambda s, index_ref: (s, 0, 0))
    gain = pl.BlockSpec((rows, 2), lambda s, index_ref: (0, 0))
    shape = jax.ShapeDtypeStruct((4 * rows, seqs * length), BF)
    inverse = jax.ShapeDtypeStruct((seqs, 1, length), F32)
    normed = gains is not None
    return pl.pallas_call(
        kernel,
        name="gather_norm" if normed else "gather",
        grid_spec=pltpu.PrefetchScalarGridSpec(
            num_scalar_prefetch=1,
            grid=(seqs,),
            in_specs=[block] * 4 + ([gain] * 4 if normed else []),
            out_specs=[full, row] if normed else full,
        ),
        out_shape=[shape, inverse] if normed else shape,
        compiler_params=params(),
        cost_estimate=cost(1 << 30),
    )(index, *blocks, *(gains if normed else ()))


def halves(value):
    high = value.astype(BF).astype(F32)
    place = lax.broadcasted_iota(jnp.int32, (8, value.shape[1]), 0)
    return jnp.where(place == 0, high, jnp.where(place == 1, value - high, 0.0)).astype(BF)


def projected(index, weights, rights, name, columns=None, row=None):
    rows = D // 4
    depth, width = rights[0].shape
    extra = 0 if row is None else 8
    start = 0 if columns is None else columns
    stacked = weights.ndim == 3

    def kernel(index_ref, weight_ref, *refs):
        right_refs = refs[: len(rights)]
        kept = refs[-1]
        total = 0.0
        for k, right in enumerate(right_refs):
            left = weight_ref[k] if stacked else weight_ref[...][:, start : start + depth]
            total += mm_nn(left, right[...])
        step = pl.program_id(0)
        total = total.astype(BF)

        def send(sent):
            sent[:rows] = total
            if row is not None:
                sent[rows:] = halves(refs[len(rights)][...])

        for place in range(2):
            pl.when(step == place)(lambda place=place: send(refs[place - 3]))

        @pl.when(step >= 2)
        def _():
            kept[0] = total

    def of(i, index_ref):
        core = index_ref[0] % 2
        return (i % 2) * 2 + jnp.where(i < 2, 1 - core, core)

    if stacked:
        left_spec = pl.BlockSpec((len(rights), rows, depth), lambda i, r: (0, of(i, r), 0))
    else:
        left_spec = pl.BlockSpec((rows, weights.shape[1]), lambda i, r: (of(i, r), 0))
    in_specs = [left_spec] + [pl.BlockSpec((depth, width), lambda i, r: (0, 0))] * len(rights)
    if row is not None:
        in_specs.append(pl.BlockSpec((1, width), lambda i, r: (0, 0)))
    return pl.pallas_call(
        kernel,
        name=name,
        grid_spec=pltpu.PrefetchScalarGridSpec(
            num_scalar_prefetch=1,
            grid=(4,),
            in_specs=in_specs,
            out_specs=[pl.BlockSpec((rows + extra, width), lambda i, r: (0, 0))] * 2
            + [pl.BlockSpec((1, rows, width), lambda i, r: (jnp.maximum(i - 2, 0), 0, 0))],
        ),
        out_shape=[jax.ShapeDtypeStruct((rows + extra, width), BF)] * 2
        + [jax.ShapeDtypeStruct((2, rows, width), BF)],
        compiler_params=params(32),
        cost_estimate=cost(2 * D * depth * len(rights) * width, 8 << 20),
    )(index, weights, *rights, *(() if row is None else (row,)))


class Reduce:
    def __init__(self, index, parts, row=None):
        self.index, self.row = index, row
        self.sent, self.kept = tuple(parts[:2]), parts[2]
        self.got = [swap(sent, 1) for sent in self.sent]
        self.here, self.there = [], []

    def cross(self, *others):
        rows, width = self.kept.shape[1:]
        extra = self.sent[0].shape[0] - rows
        length = width // 2

        def kernel(kept_ref, got_ref, *refs):
            out = refs[-1]
            out[:rows] = (kept_ref[0].astype(F32) + got_ref[:rows].astype(F32)).astype(BF)
            if extra:
                two = got_ref[rows:].astype(F32)
                out[rows:] = halves(refs[0][...] + two[:1] + two[1:2])

        for place in range(2):
            given = (self.kept, tie(self.got[place], *others))
            given += () if self.row is None else (self.row,)
            tall = pl.BlockSpec((rows + extra, length), lambda i: (0, i))
            kept = pl.BlockSpec((1, rows, length), lambda i, place=place: (place, 0, i))
            found = pl.pallas_call(
                kernel,
                name="core_sum",
                grid=(2,),
                in_specs=[kept, tall]
                + ([] if self.row is None else [pl.BlockSpec((1, length), lambda i: (0, i))]),
                out_specs=tall,
                out_shape=jax.ShapeDtypeStruct((rows + extra, width), BF),
                compiler_params=params(),
                cost_estimate=cost(1 << 28),
            )(*given)
            self.here.append(found)
            self.there.append(swap(found, 2))


class Scatter:
    def __init__(self, index, parts, seqs, row=None):
        self.index, self.row, self.seqs = index, row, seqs
        self.sent, self.kept = tuple(parts[:2]), parts[2]
        self.got = [swap(sent, 1) for sent in self.sent]

    def cross(self, *others):
        seqs, row = self.seqs, self.row
        rows, width = self.kept.shape[1:]
        length = width // seqs
        extra = self.sent[0].shape[0] - rows
        got = (tie(self.got[0], *others), self.got[1])

        def kernel(index_ref, kept_ref, first_ref, second_ref, *refs):
            far, mine = refs[-2:] if row is None else refs[-3:-1]
            chip = index_ref[0] // 2

            def pair(place):
                got = jnp.where(place == 0, first_ref[:rows], second_ref[:rows])
                return kept_ref[place].astype(F32) + got.astype(F32)

            far[0, :rows] = pair(1 - chip).astype(BF)
            mine[0] = pair(chip)
            if row is not None:
                two = first_ref[rows:].astype(F32)
                value = refs[0][...] + two[:1] + two[1:2]
                refs[-1][0] = value
                far[0, rows:] = halves(value)

        def spec(height):
            return pl.BlockSpec((1, height, length), lambda s, r: (s, 0, 0))

        out = [((seqs, rows + extra, length), BF), ((seqs, rows, length), F32)]
        out += [] if row is None else [((seqs, 1, length), F32)]
        in_specs = [pl.BlockSpec((2, rows, length), lambda s, r: (0, 0, s))]
        in_specs += [pl.BlockSpec((rows + extra, length), lambda s, r: (0, s))] * 2
        in_specs += [] if row is None else [pl.BlockSpec((1, length), lambda s, r: (0, s))]
        found = pl.pallas_call(
            kernel,
            name="pair_sum",
            grid_spec=pltpu.PrefetchScalarGridSpec(
                num_scalar_prefetch=1,
                grid=(seqs,),
                in_specs=in_specs,
                out_specs=[spec(shape[1]) for shape, _ in out],
            ),
            out_shape=[jax.ShapeDtypeStruct(*o) for o in out],
            compiler_params=params(),
            cost_estimate=cost(1 << 28),
        )(self.index, self.kept, *got, *(() if row is None else (row,)))
        self.sent_far, self.mine, self.rows = found[0], found[1], rows
        self.half = None if row is None else found[2]
        self.last = swap(self.sent_far, 2)

    def sums(self, *others):
        last = tie(self.last, *others)
        total = self.mine + last[:, : self.rows].astype(F32)
        if self.row is None:
            return total
        two = last[:, self.rows : self.rows + 2].astype(F32)
        return total, self.half + two[:, :1] + two[:, 1:]


def resid_added(index, reduce, own, far, *others):
    seqs, rows, length = own.shape
    width = seqs * length

    def kernel(index_ref, here_0, here_1, there_0, there_1, own_ref, far_ref, resid, both_0, both_1):
        chip = index_ref[0] // 2
        given = (here_0, there_0, both_0), (here_1, there_1, both_1)
        for place, (here, there, both) in enumerate(given):
            mine = chip == place
            base = jnp.where(mine, own_ref[0].astype(F32), far_ref[0].astype(F32))
            value = base + (here[...].astype(F32) + there[...].astype(F32))
            both[...] = value.astype(BF)

            @pl.when(mine)
            def _():
                resid[0] = value

    wide = pl.BlockSpec((rows, length), lambda s, r: (0, s))
    one = pl.BlockSpec((1, rows, length), lambda s, r: (s, 0, 0))
    resid, *both = pl.pallas_call(
        kernel,
        name="resid",
        grid_spec=pltpu.PrefetchScalarGridSpec(
            num_scalar_prefetch=1,
            grid=(seqs,),
            in_specs=[wide] * 4 + [one, one],
            out_specs=[one, wide, wide],
        ),
        out_shape=[jax.ShapeDtypeStruct((seqs, rows, length), F32)]
        + [jax.ShapeDtypeStruct((rows, width), BF)] * 2,
        compiler_params=params(),
        cost_estimate=cost(1 << 28),
    )(index, *reduce.here, tie(reduce.there[0], *others), reduce.there[1], own, far)
    return resid, both


def resid_back(index, reduce, grad_own, grad_far, resid, resid_both, inverse, gains, *others):
    seqs, rows, length = grad_own.shape
    width = seqs * length

    def kernel(index_ref, *refs):
        here, there, held_both, both = refs[:2], refs[2:4], refs[4:6], refs[-3:-1]
        own_ref, far_ref, resid_ref, inverse_ref, own_gain_ref, far_gain_ref, grad = refs[6:13]
        chip = index_ref[0] // 2
        tail = here[0][rows:].astype(F32) + there[0][rows:].astype(F32)
        inv = inverse_ref[0]
        scale = inv * inv * (tail[:1] + tail[1:2]) / D
        own_gain_column = own_gain_ref[...][:, 1:2].astype(F32)
        far_gain_column = far_gain_ref[...][:, 1:2].astype(F32)
        for place in range(2):
            mine = chip == place
            normed = here[place][:rows].astype(F32) + there[place][:rows].astype(F32)
            base = jnp.where(mine, own_ref[0].astype(F32), far_ref[0].astype(F32))
            gain = jnp.where(mine, own_gain_column, far_gain_column)
            most = base + inv * gain * normed
            both[place][...] = (most - held_both[place][...].astype(F32) * scale).astype(BF)

            @pl.when(mine)
            def _():
                held = resid_ref[0]
                grad[0] = most - held * scale
                refs[-1][0] = jnp.sum(held * inv * normed, 1, keepdims=True)

    wide = pl.BlockSpec((rows, length), lambda s, r: (0, s))
    more = pl.BlockSpec((rows + 8, length), lambda s, r: (0, s))
    one = pl.BlockSpec((1, rows, length), lambda s, r: (s, 0, 0))
    row = pl.BlockSpec((1, 1, length), lambda s, r: (s, 0, 0))
    gain = pl.BlockSpec((rows, 2), lambda s, r: (0, 0))
    grad, *both, gain_sum = pl.pallas_call(
        kernel,
        name="resid_back",
        grid_spec=pltpu.PrefetchScalarGridSpec(
            num_scalar_prefetch=1,
            grid=(seqs,),
            in_specs=[more] * 4 + [wide] * 2 + [one, one, one, row, gain, gain],
            out_specs=[one, wide, wide, pl.BlockSpec((1, rows, 1), lambda s, r: (s, 0, 0))],
        ),
        out_shape=[jax.ShapeDtypeStruct((seqs, rows, length), F32)]
        + [jax.ShapeDtypeStruct((rows, width), BF)] * 2
        + [jax.ShapeDtypeStruct((seqs, rows, 1), F32)],
        compiler_params=params(),
        cost_estimate=cost(1 << 28),
    )(
        index,
        *reduce.here,
        tie(reduce.there[0], *others),
        reduce.there[1],
        *resid_both,
        grad_own,
        grad_far,
        resid,
        inverse,
        *gains,
    )
    return grad, both, gain_sum


def gathered_pair(index, here, there, seqs, gains=None, column=0):
    rows, width = here[0].shape
    length = width // seqs
    normed = gains is not None

    def kernel(index_ref, *refs):
        me = index_ref[0]
        chip, core = me // 2, me % 2
        blocks = refs[:2], refs[2:4]
        out = refs[8 if normed else 4]
        if normed:
            total = 0.0
            for ref in refs[:4]:
                value = ref[...].astype(F32)
                total += jnp.sum(value * value, 0, keepdims=True)
            inverse = lax.rsqrt(total / D + EPS)
            refs[9][0] = inverse
            columns = [ref[...][:, column : column + 1].astype(F32) for ref in refs[4:8]]
        for other in range(2):
            for place in range(2):
                value = blocks[other][place][...]
                if normed:
                    gain = jnp.where(chip == place, columns[other], columns[2 + other])
                    value = (value.astype(F32) * inverse * gain).astype(BF)
                row = 2 * place + (core ^ other)
                out[pl.ds(pl.multiple_of(row * rows, 16), rows), :] = value

    wide = pl.BlockSpec((rows, length), lambda s, r: (0, s))
    full = pl.BlockSpec((4 * rows, length), lambda s, r: (0, s))
    row = pl.BlockSpec((1, 1, length), lambda s, r: (s, 0, 0))
    gain = pl.BlockSpec((rows, 2), lambda s, r: (0, 0))
    shape = jax.ShapeDtypeStruct((4 * rows, width), BF)
    inverse = jax.ShapeDtypeStruct((seqs, 1, length), F32)
    return pl.pallas_call(
        kernel,
        name="pair_norm" if normed else "pair",
        grid_spec=pltpu.PrefetchScalarGridSpec(
            num_scalar_prefetch=1,
            grid=(seqs,),
            in_specs=[wide] * 4 + ([gain] * 4 if normed else []),
            out_specs=[full, row] if normed else full,
        ),
        out_shape=[shape, inverse] if normed else shape,
        compiler_params=params(),
        cost_estimate=cost(1 << 30),
    )(index, *here, *there, *(gains if normed else ()))


def ring_order(count):
    half = count // 2
    return [2 * r for r in range(half)] + [2 * r + 1 for r in reversed(range(half))]


def ringed():
    return lax.axis_size("ctx") == 8


def hop(value, step):
    order = ring_order(lax.axis_size("ctx"))
    count = len(order)
    pairs = [(order[r], order[(r + step) % count]) for r in range(count)]
    return lax.ppermute(value, "ctx", pairs)


def places():
    count = lax.axis_size("ctx")
    order = ring_order(count)
    place = {device: r for r, device in enumerate(order)}
    table = [[0] + [order[(place[i] + offset) % count] for offset in OFFSETS] for i in range(count)]
    found = jnp.array(table, jnp.int32)[lax.axis_index("ctx")]
    return found + jnp.where(jnp.arange(len(OFFSETS) + 1) == 0, lax.axis_index("wt"), 0)


class Gather:
    def __init__(self, shard):
        self.shard, self.axis, self.sent = shard, shard.ndim - 2, ()
        self.right, self.left = [shard], [shard]

    def advance(self, *others):
        if not ringed():
            return
        right, left = self.right[-1], self.left[-1]
        if len(self.right) == 4:
            rows = right.shape[self.axis]
            right = lax.slice_in_dim(right, 0, rows // 2, axis=self.axis)
            left = lax.slice_in_dim(left, rows // 2, rows, axis=self.axis)
        others = jax.tree.leaves(others)
        if others:
            right, left = lax.optimization_barrier((right, left, *others))[:2]
        self.sent = right, left
        self.right.append(hop(right, 1))
        self.left.append(hop(left, -1))

    def here(self):
        return (self.right[-1], self.left[-1]) if ringed() else ()

    def full(self, index):
        if not ringed():
            return lax.all_gather(self.shard, "ctx", axis=self.axis, tiled=True)
        rows = self.shard.shape[self.axis]
        pieces = self.right + self.left[1:]
        offsets = (0, -1, -2, -3, 4, 1, 2, 3, 4)
        count = len(pieces)

        def kernel(index_ref, *refs):
            out, sems = refs[count], refs[count + 1]
            copies = []
            for k in range(count):
                first = index_ref[PLACE[offsets[k]]] * rows + (rows // 2 if k == 8 else 0)
                at = pl.ds(pl.multiple_of(first, 16), pieces[k].shape[-2])
                where = out.at[at, :] if len(out.shape) == 2 else out.at[:, at, :]
                copies.append(pltpu.make_async_copy(refs[k], where, sems.at[k]))
                copies[-1].start()
            for copy in copies:
                copy.wait()

        shape = self.shard.shape[:-2] + (rows * 8, self.shard.shape[-1])
        return pl.pallas_call(
            kernel,
            name="assemble",
            in_specs=[SMEM] + [ANY] * count,
            out_specs=WHOLE,
            out_shape=jax.ShapeDtypeStruct(shape, BF),
            scratch_shapes=[pltpu.SemaphoreType.DMA((count,))],
            compiler_params=params(),
            cost_estimate=cost(),
        )(index, *pieces)


def products(lefts, rights, name):
    rows, length = lefts[0].shape
    widths = [r.shape[0] for r in rights]
    used = lefts[:1] if all(left is lefts[0] for left in lefts) else lefts

    def kernel(*refs):
        out = refs[-1]
        first = 0
        for k, width in enumerate(widths):
            left = refs[k if len(used) > 1 else 0]
            out[:, pl.ds(first, width)] = mm_nt(left[...], refs[len(used) + k][...]).astype(BF)
            first += width

    return pl.pallas_call(
        kernel,
        name=name,
        grid=(4,),
        in_specs=[pl.BlockSpec((rows // 4, length), lambda i: (i, 0))] * len(used)
        + [pl.BlockSpec((width, length), lambda i: (0, 0)) for width in widths],
        out_specs=pl.BlockSpec((rows // 4, sum(widths)), lambda i: (i, 0)),
        out_shape=jax.ShapeDtypeStruct((rows, sum(widths)), BF),
        compiler_params=params(32),
        cost_estimate=cost(2 * rows * length * sum(widths), 2 * rows * sum(widths)),
    )(*used, *rights)


class Products:
    def __init__(self, index, full):
        self.index, self.full, self.step, self.sent = index, full, 4, ()
        if ringed():
            self.rows, self.width = full.shape[0] // 8, full.shape[1]
            self._send()

    def _send(self):
        half, step = self.rows // 2, self.step
        first, second = step == 4, step == 3

        def kernel(index_ref, *refs):
            row = pl.program_id(0)
            if first:
                own, right, left = refs

                @pl.when(row == 0)
                def _():
                    right[...] = own[...]

                @pl.when(row == 1)
                def _():
                    left[...] = own[...]

                return
            from_right, from_left, own_right, own_left, right, left = refs
            more_right, more_left = from_right[...].astype(F32), from_left[...].astype(F32)
            if second:
                more_right = jnp.where(row == 0, more_right, 0.0)
                more_left = jnp.where(row == 1, more_left, 0.0)
            right[...] = (own_right[...].astype(F32) + more_right).astype(BF)
            left[...] = (own_left[...].astype(F32) + more_left).astype(BF)

        def own(offset):
            return pl.BlockSpec((half, self.width), lambda i, r: (r[PLACE[offset]] * 2 + i, 0))

        still = pl.BlockSpec((half, self.width), lambda i, r: (0, 0))
        moving = pl.BlockSpec((half, self.width), lambda i, r: (i, 0))
        if first:
            in_specs, out_spec, given, rows = [own(4)], still, (self.full,), half
        else:
            in_specs = [still if second else moving] * 2 + [own(step), own(-step)]
            out_spec, given, rows = moving, (self.right, self.left, self.full, self.full), self.rows
        self.sent = pl.pallas_call(
            kernel,
            name="ring_sum",
            grid_spec=pltpu.PrefetchScalarGridSpec(
                num_scalar_prefetch=1, grid=(2,), in_specs=in_specs, out_specs=[out_spec] * 2
            ),
            out_shape=[jax.ShapeDtypeStruct((rows, self.width), BF)] * 2,
            compiler_params=params(),
            cost_estimate=cost(1 << 24),
        )(self.index, *given)
        self.right, self.left = hop(self.sent[0], 1), hop(self.sent[1], -1)

    def here(self):
        return (self.right, self.left) if ringed() else ()

    def advance(self, *others):
        if ringed():
            self.step -= 1
            self.right = tie(self.right, self.left, *others)
            self._send()

    def final(self, *others):
        if not ringed():
            return lax.psum_scatter(self.full, "ctx", scatter_dimension=0, tiled=True).astype(F32)
        right = tie(self.right, self.left, *others)

        def kernel(index_ref, own, right_ref, left_ref, out):
            out[...] = own[...].astype(F32) + right_ref[...].astype(F32) + left_ref[...].astype(F32)

        half = self.rows // 2
        moving = pl.BlockSpec((half, self.width), lambda i, r: (i, 0))
        own = pl.BlockSpec((half, self.width), lambda i, r: (r[PLACE[0]] * 2 + i, 0))
        return pl.pallas_call(
            kernel,
            name="ring_end",
            grid_spec=pltpu.PrefetchScalarGridSpec(
                num_scalar_prefetch=1, grid=(2,), in_specs=[own, moving, moving], out_specs=moving
            ),
            out_shape=jax.ShapeDtypeStruct((self.rows, self.width), F32),
            compiler_params=params(),
            cost_estimate=cost(1 << 24),
        )(self.index, self.full, right, self.left)


def shifted(value, by):
    count = lax.axis_size("ctx")
    pairs = [(i, i + by) for i in range(count) if 0 <= i + by < count]
    return lax.ppermute(value, "ctx", pairs)


class Before:
    def __init__(self, value, sign):
        self.value, self.sign = value, sign
        self.other = self.one = self.two = self.sent = ()
        if ringed():
            count = lax.axis_size("ctx")
            self.other = lax.ppermute(value, "ctx", [(i, i ^ 1) for i in range(count)])

    def first(self, *others):
        if ringed():
            other = tie(self.other, *others)
            self.total = (self.value.astype(F32) + other.astype(F32)).astype(BF)
            self.one = shifted(self.total, 2 * self.sign)

    def second(self, *others):
        if ringed():
            one = tie(self.one, *others)
            self.sent = (self.total.astype(F32) + one.astype(F32)).astype(BF)
            self.two = shifted(self.sent, 4 * self.sign)

    def result(self):
        count, index = lax.axis_size("ctx"), lax.axis_index("ctx")
        if not ringed():
            everything = lax.all_gather(self.value, "ctx").astype(F32)
            place = jnp.arange(count)
            keep = (place < index) if self.sign > 0 else (place > index)
            keep = keep.reshape((count,) + (1,) * self.value.ndim)
            return jnp.sum(jnp.where(keep, everything, 0.0), 0).astype(BF)
        behind = (index & 1) == (1 if self.sign > 0 else 0)
        result = self.one.astype(F32) + self.two.astype(F32)
        return (result + jnp.where(behind, self.other.astype(F32), 0.0)).astype(BF)


def ctx_total(value):
    if not ringed():
        return lax.psum(value, "ctx")
    for bit in (1, 2, 4):
        value = value + lax.ppermute(value, "ctx", [(i, i ^ bit) for i in range(8)])
    return value


def turned(rows, by):
    return jnp.concatenate([rows[by:], rows[:by]], 0)


def feature_rows(vectors, square, cross, linear):
    length = vectors.shape[1]
    half = FEAT // 2
    pieces = [vectors * vectors * square]
    pieces += [vectors * turned(vectors, by) * cross for by in range(1, half)]
    pieces += [vectors[:half] * vectors[half:] * cross]
    place = lax.broadcasted_iota(jnp.int32, (half, length), 0)
    pieces += [jnp.where(place == 0, 1.0, 0.0), vectors * linear]
    return jnp.concatenate(pieces, 0).astype(BF)


def feature_pull(grad, vectors, square, cross, linear):
    half = FEAT // 2
    total = 2.0 * square * grad[:FEAT] * vectors
    for by in range(1, half):
        part = grad[FEAT * by : FEAT * (by + 1)] * cross
        total += part * turned(vectors, by) + turned(part * vectors, FEAT - by)
    part = grad[FEAT * half : FEAT * half + half] * cross
    total += jnp.concatenate([part * vectors[half:], part * vectors[:half]], 0)
    return total + grad[PHI - FEAT :] * linear


QUERY_SCALE = (1.0 / 32.0, 1.0 / 16.0, 0.25)
KEY_SCALE = (1.0, 1.0, 1.0)


def extended(value, valid):
    place = lax.broadcasted_iota(jnp.int32, (EXT - HEAD_DIM, value.shape[1]), 0)
    tail = jnp.where(place == 0, jnp.broadcast_to(valid, place.shape), 0.0)
    return jnp.concatenate([(value.astype(F32) * valid).astype(BF), tail.astype(BF)], 0)


def causal_of(length):
    key_place = lax.broadcasted_iota(jnp.int32, (length, length), 0)
    query_place = lax.broadcasted_iota(jnp.int32, (length, length), 1)
    return key_place <= query_place


def state_kernel(key_ref, value_ref, valid_ref, state_ref):
    mapped = feature_rows(key_ref[...].astype(F32), *KEY_SCALE)
    state_ref[0, 0] = mm_nt(mapped, extended(value_ref[...], valid_ref[0])).astype(BF)


def attend_kernel(query_ref, key_ref, value_ref, valid_ref, state_ref, mixed_ref, denom_ref):
    query = query_ref[...]
    scores = mm_tn(key_ref[...], query) * 0.25
    weights = jnp.where(causal_of(query.shape[1]), 1.0 + scores + 0.5 * scores * scores, 0.0)
    total = mm_nn(extended(value_ref[...], valid_ref[0]), weights.astype(BF))
    mapped = feature_rows(query.astype(F32), *QUERY_SCALE)
    total += mm_tn(state_ref[0, 0], mapped)
    denom = total[HEAD_DIM : HEAD_DIM + 1]
    denom_ref[0, 0] = denom
    mixed_ref[...] = (total[:HEAD_DIM] / denom).astype(BF)


def spread_kernel(query_ref, grad_ref, mixed_ref, denom_ref, weighted_ref, state_ref):
    weighted = grad_ref[...].astype(F32) / denom_ref[0, 0]
    shift = jnp.sum(weighted * mixed_ref[...].astype(F32), 0, keepdims=True)
    place = lax.broadcasted_iota(jnp.int32, (EXT - HEAD_DIM, weighted.shape[1]), 0)
    tail = jnp.where(place == 0, -jnp.broadcast_to(shift, place.shape), 0.0)
    whole = jnp.concatenate([weighted, tail], 0).astype(BF)
    weighted_ref[0, 0] = whole
    mapped = feature_rows(query_ref[...].astype(F32), *QUERY_SCALE)
    state_ref[0, 0] = mm_nt(mapped, whole).astype(BF)


def local_kernel(
    query_ref, key_ref, value_ref, valid_ref, state_ref, weighted_ref, dq_ref, dk_ref, dv_ref
):
    query, key_in, weighted = query_ref[...], key_ref[...], weighted_ref[0, 0]
    causal = causal_of(query.shape[1])
    scores = mm_tn(key_in, query) * 0.25
    weights = jnp.where(causal, 1.0 + scores + 0.5 * scores * scores, 0.0).astype(BF)
    dv_ref[...] = mm_nt(weighted[:HEAD_DIM], weights) * valid_ref[0]
    slope = mm_tn(extended(value_ref[...], valid_ref[0]), weighted)
    slope = jnp.where(causal, slope * (1.0 + scores), 0.0).astype(BF)
    mapped = mm_nn(state_ref[0, 0], weighted)
    pulled = feature_pull(mapped, query.astype(F32), *QUERY_SCALE)
    dq_ref[...] = (mm_nn(key_in, slope) * 0.25 + pulled).astype(BF)
    dk_ref[...] = mm_nt(query, slope) * 0.25


def later_kernel(heads, key_ref, value_ref, valid_ref, state_ref, dq_in, dk_in, dv_in, out_ref):
    head = pl.program_id(1)
    key_in = key_ref[...].astype(F32)
    valid = valid_ref[0]
    mapped = mm_nn(state_ref[0, 0], extended(value_ref[...], valid))
    d_key = (dk_in[...] + feature_pull(mapped, key_in, *KEY_SCALE)).astype(BF)
    spread = mm_tn(state_ref[0, 0], feature_rows(key_in, *KEY_SCALE))
    d_value = (dv_in[...] + spread[:HEAD_DIM] * valid).astype(BF)
    values, queries = heads * HEAD_DIM, heads * FEAT
    out_ref[pl.ds(pl.multiple_of(head * HEAD_DIM, 16), HEAD_DIM), :] = d_value
    out_ref[pl.ds(pl.multiple_of(values + head * FEAT, 16), FEAT), :] = dq_in[...]
    out_ref[pl.ds(pl.multiple_of(values + queries + head * FEAT, 16), FEAT), :] = d_key


def head_call(kernel, name, seqs, heads, length, ins, outs, flops):
    first_query = heads * HEAD_DIM // FEAT
    columns = heads * (HEAD_DIM + 2 * FEAT)
    specs = {
        "value": pl.BlockSpec((HEAD_DIM, length), lambda s, h: (h, s)),
        "query": pl.BlockSpec((FEAT, length), lambda s, h: (first_query + h, s)),
        "key": pl.BlockSpec((FEAT, length), lambda s, h: (first_query + heads + h, s)),
        "all": pl.BlockSpec((columns, length), lambda s, h: (0, s)),
        "feat": pl.BlockSpec((FEAT, length), lambda s, h: (h, s)),
        "head": pl.BlockSpec((HEAD_DIM, length), lambda s, h: (h, s)),
        "valid": pl.BlockSpec((1, 1, length), lambda s, h: (s, 0, 0)),
        "state": pl.BlockSpec((1, 1, PHI, EXT), lambda s, h: (s, h, 0, 0)),
        "row": pl.BlockSpec((1, 1, 1, length), lambda s, h: (s, h, 0, 0)),
        "ext": pl.BlockSpec((1, 1, EXT, length), lambda s, h: (s, h, 0, 0)),
    }
    shapes = {
        "all": (columns, seqs * length),
        "feat": (heads * FEAT, seqs * length),
        "head": (heads * HEAD_DIM, seqs * length),
        "state": (seqs, heads, PHI, EXT),
        "row": (seqs, heads, 1, length),
        "ext": (seqs, heads, EXT, length),
    }
    return pl.pallas_call(
        kernel,
        name=name,
        grid=(seqs, heads),
        in_specs=[specs[i] for i in ins],
        out_specs=[specs[o] for o, _ in outs],
        out_shape=[jax.ShapeDtypeStruct(shapes[o], kind) for o, kind in outs],
        compiler_params=params(),
        cost_estimate=cost(flops),
    )


def body(
    hidden_in,
    lengths,
    gain_attn,
    gain_ffn,
    w_query,
    w_key,
    w_value,
    w_output,
    w_gate,
    w_up,
    w_down,
    cotangent,
):
    seqs, length, width = hidden_in.shape
    heads = w_value.shape[1] // HEAD_DIM
    hidden_units = w_gate.shape[1]
    columns = heads * (HEAD_DIM + 2 * FEAT)
    index = places()
    position = lax.axis_index("ctx") * length + jnp.arange(length, dtype=jnp.int32)
    valid = (position[None, :] < lengths[:, None]).astype(F32)[:, None, :]
    hidden = hidden_in.transpose(0, 2, 1)
    unit = seqs * heads * 2 * length * length * 256
    token = [jnp.zeros((8, 128), F32)]

    def call(kernel, name, ins, outs, share):
        return head_call(kernel, name, seqs, heads, length, ins, outs, int(unit * share))

    def turn(value, *others):
        return tie(value, token[0], *others)

    def fence(*values):
        token[0] = tie(token[0], *values)

    ring_attn = Gather(jnp.concatenate([w_value, w_query, w_key, w_output.T], 1))
    ring_down = Gather(w_down.T)
    ring_gate_up = Gather(jnp.stack([w_gate, w_up]))
    ring_attn.advance()
    spread_in = Spread(hidden)
    gains = Spread(jnp.stack([gain_attn, gain_ffn], 1))
    gains.cross()
    fence(ring_attn.here())
    ring_attn.advance(*token)
    fence(ring_attn.here(), ring_gate_up.shard)
    ring_attn.advance(*token)
    spread_in.cross(*token)
    grad_out = (cotangent.transpose(0, 2, 1).astype(F32) * valid).astype(BF)
    spread_out = Spread(tie(grad_out, spread_in.far))
    fence(ring_attn.here())
    ring_attn.advance(*token)
    ring_gate_up.advance(ring_attn.sent)
    fence(spread_in.near, spread_in.both)
    blocks = spread_in.blocks()
    normed_one, inv_one = gathered(index, (turn(blocks[0]),) + blocks[1:], gains.blocks(), 0)
    fence(normed_one)
    fence(ring_attn.here())
    w_attn = ring_attn.full(turn(index))

    qkv = mm_tn(w_attn[:, :columns], normed_one).astype(BF)
    (own,) = call(state_kernel, "state", ("key", "value", "valid"), (("state", BF),), 0.5)(
        qkv, qkv, valid
    )
    before = Before(own, 1)
    fence(own)
    fence(before.other)
    before.first(*token)
    fence(before.total if ringed() else ())
    fence(ring_gate_up.here())
    ring_gate_up.advance(*token)
    fence(before.one)
    before.second(*token)
    fence(before.sent)
    ring_down.advance(*token)
    spread_out.cross(*token)
    fence(ring_gate_up.here())
    ring_gate_up.advance(*token)

    state = before.result()
    mixed, denom = call(
        attend_kernel,
        "attend",
        ("query", "key", "value", "valid", "state"),
        (("head", BF), ("row", F32)),
        1,
    )(turn(qkv), qkv, qkv, valid, state)
    fence(ring_down.here())
    scatter_attn = Scatter(
        index, projected(index, w_attn, [turn(mixed)], "out_proj", columns), seqs
    )
    fence(scatter_attn.sent)
    fence(ring_gate_up.here())
    scatter_attn.cross(*token)
    fence(scatter_attn.sent_far)
    blocks = spread_out.blocks()
    grad_out_full = gathered(index, (turn(blocks[0]),) + blocks[1:])
    fence(grad_out_full)
    fence(ring_gate_up.here())
    ring_gate_up.advance(*token)
    ring_down.advance(*token)
    resid = hidden.astype(F32) + scatter_attn.sums(*token)
    spread_resid = Spread(resid.astype(BF))
    fence(spread_resid.block)
    fence(ring_gate_up.here(), ring_down.here())
    ring_down.advance(*token)
    gate_up = ring_gate_up.full(turn(index))
    fence(gate_up)
    fence(ring_down.here())
    ring_down.advance(*token)
    spread_resid.cross(*token)

    blocks = spread_resid.blocks()
    normed_two, inv_two = gathered(index, blocks, gains.blocks(), 1)
    fence(normed_two)
    gate = mm_tn(gate_up[0], turn(normed_two))
    up = mm_tn(gate_up[1], normed_two)
    act = (gate * jax.nn.sigmoid(gate) * up).astype(BF)
    fence(act)
    fence(ring_down.here())
    down_full = ring_down.full(turn(index))
    fence(down_full)

    sig = jax.nn.sigmoid(gate)
    d_act = mm_tn(down_full, turn(grad_out_full))
    g_gate = (d_act * up * sig * (1.0 + gate * (1.0 - sig))).astype(BF)
    g_up = (d_act * gate * sig).astype(BF)
    inner = jnp.sum(g_gate.astype(F32) * gate + g_up.astype(F32) * up, 0, keepdims=True)
    fence(g_gate, g_up)
    scatter_two = Scatter(
        index, projected(index, gate_up, [turn(g_gate), g_up], "ffn_back", row=inner), seqs, inner
    )
    fence(scatter_two.sent)
    down_ring = Products(index, products([turn(grad_out_full)], [act], "down_grad"))
    fence(down_ring.sent)
    scatter_two.cross(*token)
    fence(scatter_two.sent_far)
    gate_up_ring = Products(
        index, products([normed_two, normed_two], [turn(g_gate), g_up], "gate_up_grad")
    )
    fence(gate_up_ring.sent)
    fence(down_ring.here())
    down_ring.advance(*token)
    fence(down_ring.sent)

    gain_one, gain_two = gain_attn.astype(F32)[:, None], gain_ffn.astype(F32)[:, None]
    d_norm, inner = scatter_two.sums(*token)
    gain_two_part = jnp.sum(resid * inv_two * d_norm, (0, 2))
    d_resid = (
        grad_out.astype(F32)
        + inv_two * gain_two * d_norm
        - resid * (inv_two * inv_two * inner / D)
    )
    spread_grad = Spread(d_resid.astype(BF))
    fence(spread_grad.block)
    fence(gate_up_ring.here())
    gate_up_ring.advance(*token)
    fence(gate_up_ring.sent)
    ffn_out = projected(index, down_full, [turn(act)], "ffn_out")
    fence(ffn_out)
    fence(down_ring.here())
    down_ring.advance(*token)
    fence(down_ring.sent)
    spread_grad.cross(*token)
    blocks = spread_grad.blocks()
    resid_full = gathered(index, blocks)
    fence(resid_full)
    g_attn = mm_tn(w_attn[:, columns:], turn(resid_full)).astype(BF)
    weighted, spread = call(
        spread_kernel, "spread", ("query", "head", "head", "row"), (("ext", BF), ("state", BF)), 0.5
    )(turn(qkv), g_attn, mixed, denom)
    after = Before(spread, -1)
    fence(spread)
    fence(gate_up_ring.here())
    fence(after.other)
    after.first(*token)
    fence(after.total if ringed() else ())
    local = call(
        local_kernel,
        "local",
        ("query", "key", "value", "valid", "state", "ext"),
        (("feat", BF), ("feat", F32), ("head", F32)),
        2,
    )(turn(qkv), qkv, qkv, valid, state, weighted)
    fence(local)
    scatter_out = Scatter(index, [*lax.optimization_barrier((*ffn_out, *token))[:3]], seqs)
    fence(after.one)
    after.second(*token)
    fence(after.sent)
    gate_up_ring.advance(*token)
    fence(gate_up_ring.sent)
    scatter_out.cross(*token)
    fence(scatter_out.sent_far)

    def later(*refs):
        later_kernel(heads, *refs)

    (d_qkv,) = call(
        later,
        "later",
        ("key", "value", "valid", "state", "feat", "feat", "head"),
        (("all", BF),),
        0.5,
    )(turn(qkv), qkv, valid, after.result(), *local)
    inner = jnp.sum(d_qkv.astype(F32) * qkv.astype(F32), 0, keepdims=True)
    scatter_one = Scatter(
        index, projected(index, w_attn, [d_qkv], "qkv_back", row=inner), seqs, inner
    )
    fence(scatter_one.sent)
    fence(down_ring.here())
    down_ring.advance(*token)
    fence(down_ring.sent)
    attn_ring = Products(
        index, products([turn(normed_one), resid_full], [d_qkv, mixed], "attn_grad")
    )
    fence(attn_ring.sent)
    fence(gate_up_ring.here())
    gate_up_ring.advance(*token)
    fence(gate_up_ring.sent)
    scatter_one.cross(*token)
    fence(scatter_one.sent_far)
    fence(attn_ring.here())
    attn_ring.advance(*token)
    fence(attn_ring.sent)
    layer_out = (resid + scatter_out.sums(*token)).astype(BF)
    fence(layer_out)
    d_norm, inner = scatter_one.sums(*token)
    value = hidden.astype(F32)
    gain_one_part = jnp.sum(value * inv_one * d_norm, (0, 2))
    grad_input = (
        d_resid + inv_one * gain_one * d_norm - value * (inv_one * inv_one * inner / D)
    )
    fence(gain_one_part, grad_input)
    gain_grads = ctx_total(jnp.stack([gain_one_part, gain_two_part]) + token[0][:1, :1])
    fence(attn_ring.here())
    attn_ring.advance(*token)
    fence(attn_ring.sent)
    down_grad = down_ring.final(*token)
    fence(down_grad)
    fence(attn_ring.here())
    attn_ring.advance(*token)
    fence(attn_ring.sent)
    gate_up_grad = gate_up_ring.final(*token)
    fence(gate_up_grad)
    fence(gain_grads)
    attn_grad = attn_ring.final(*token)

    values, queries = heads * HEAD_DIM, heads * FEAT
    return (
        layer_out.transpose(0, 2, 1),
        grad_input.transpose(0, 2, 1),
        gain_grads[0],
        gain_grads[1],
        attn_grad[:, values : values + queries],
        attn_grad[:, values + queries : columns],
        attn_grad[:, :values],
        attn_grad[:, columns:].T,
        gate_up_grad[:, :hidden_units],
        gate_up_grad[:, hidden_units:],
        down_grad.T,
    )


def solution(mesh):
    acts, rows, columns = P(None, "ctx", "wt"), P("ctx", "wt"), P("wt", "ctx")
    in_specs = (acts, P(), P("wt"), P("wt"), rows, rows, rows, columns, rows, rows, columns, acts)
    out_specs = (acts, acts, P("wt"), P("wt"), rows, rows, rows, columns, rows, rows, columns)
    return jax.shard_map(body, mesh=mesh, in_specs=in_specs, out_specs=out_specs, check_vma=False)
```

```python
import jax
import jax.numpy as jnp
from jax import lax
from jax.experimental import pallas as pl
from jax.experimental.pallas import tpu as pltpu
from jax.sharding import PartitionSpec as P


D = 1792
FEAT = 16
HEAD_DIM = 112
EXT = 128
PHI = 160
EPS = 1e-05
BF = jnp.bfloat16
F32 = jnp.float32
ANY = pl.BlockSpec(memory_space=pl.ANY)
WHOLE = pl.BlockSpec(memory_space=pltpu.VMEM)
SMEM = pl.BlockSpec(memory_space=pltpu.SMEM)
OFFSETS = (0, 1, 2, 3, 4, -1, -2, -3)
PLACE = {offset: 1 + k for k, offset in enumerate(OFFSETS)}
PLACE[-4] = PLACE[4]


def mm_nn(left, right):
    return lax.dot_general(left, right, (((1,), (0,)), ((), ())), preferred_element_type=F32)


def mm_tn(left, right):
    return lax.dot_general(left, right, (((0,), (0,)), ((), ())), preferred_element_type=F32)


def mm_nt(left, right):
    return lax.dot_general(left, right, (((1,), (1,)), ((), ())), preferred_element_type=F32)


def tie(value, *others):
    others = jax.tree.leaves(others)
    return lax.optimization_barrier((value, *others))[0] if others else value


def params(mib=24):
    return pltpu.CompilerParams(vmem_limit_bytes=mib << 20)


def cost(flops=0, moved=4 << 20):
    return pl.CostEstimate(flops=flops, bytes_accessed=moved, transcendentals=0)


def swap(value, bit):
    count = lax.axis_size("wt")
    return lax.ppermute(value, "wt", [(i, i ^ bit) for i in range(count)])


class Spread:
    def __init__(self, block):
        self.block, self.far, self.near = block, swap(block, 2), swap(block, 1)

    def cross(self, *others):
        self.far = tie(self.far, *others)
        self.both = swap(self.far, 1)

    def blocks(self):
        return self.block, self.near, self.far, self.both


def gathered(index, blocks, gains=None, column=0):
    seqs, rows, length = blocks[0].shape

    def kernel(index_ref, *refs):
        values = [ref[0] for ref in refs[:4]]
        out = refs[8 if gains is not None else 4]
        if gains is not None:
            values = [v.astype(F32) for v in values]
            total = sum(jnp.sum(v * v, 0, keepdims=True) for v in values)
            inverse = lax.rsqrt(total / D + EPS)
            refs[9][0] = inverse
            scaled = []
            for v, gain_ref in zip(values, refs[4:8]):
                gain = gain_ref[...][:, column : column + 1].astype(F32)
                scaled.append((v * inverse * gain).astype(BF))
            values = scaled
        me = index_ref[0]
        for bit in range(4):
            out[pl.ds(pl.multiple_of((me ^ bit) * rows, 16), rows), :] = values[bit]

    block = pl.BlockSpec((1, rows, length), lambda s, index_ref: (s, 0, 0))
    full = pl.BlockSpec((4 * rows, length), lambda s, index_ref: (0, s))
    row = pl.BlockSpec((1, 1, length), lambda s, index_ref: (s, 0, 0))
    gain = pl.BlockSpec((rows, 2), lambda s, index_ref: (0, 0))
    shape = jax.ShapeDtypeStruct((4 * rows, seqs * length), BF)
    inverse = jax.ShapeDtypeStruct((seqs, 1, length), F32)
    normed = gains is not None
    return pl.pallas_call(
        kernel,
        name="gather_norm" if normed else "gather",
        grid_spec=pltpu.PrefetchScalarGridSpec(
            num_scalar_prefetch=1,
            grid=(seqs,),
            in_specs=[block] * 4 + ([gain] * 4 if normed else []),
            out_specs=[full, row] if normed else full,
        ),
        out_shape=[shape, inverse] if normed else shape,
        compiler_params=params(),
        cost_estimate=cost(1 << 30),
    )(index, *blocks, *(gains if normed else ()))


def halves(value):
    high = value.astype(BF).astype(F32)
    place = lax.broadcasted_iota(jnp.int32, (8, value.shape[1]), 0)
    return jnp.where(place == 0, high, jnp.where(place == 1, value - high, 0.0)).astype(BF)


def projected(index, weights, rights, name, columns=None, row=None):
    rows = D // 4
    depth, width = rights[0].shape
    extra = 0 if row is None else 8
    start = 0 if columns is None else columns
    stacked = weights.ndim == 3

    def kernel(index_ref, weight_ref, *refs):
        right_refs = refs[: len(rights)]
        kept = refs[-1]
        total = 0.0
        for k, right in enumerate(right_refs):
            left = weight_ref[k] if stacked else weight_ref[...][:, start : start + depth]
            total += mm_nn(left, right[...])
        step = pl.program_id(0)
        total = total.astype(BF)

        def send(sent):
            sent[:rows] = total
            if row is not None:
                sent[rows:] = halves(refs[len(rights)][...])

        for place in range(2):
            pl.when(step == place)(lambda place=place: send(refs[place - 3]))

        @pl.when(step >= 2)
        def _():
            kept[0] = total

    def of(i, index_ref):
        core = index_ref[0] % 2
        return (i % 2) * 2 + jnp.where(i < 2, 1 - core, core)

    if stacked:
        left_spec = pl.BlockSpec((len(rights), rows, depth), lambda i, r: (0, of(i, r), 0))
    else:
        left_spec = pl.BlockSpec((rows, weights.shape[1]), lambda i, r: (of(i, r), 0))
    in_specs = [left_spec] + [pl.BlockSpec((depth, width), lambda i, r: (0, 0))] * len(rights)
    if row is not None:
        in_specs.append(pl.BlockSpec((1, width), lambda i, r: (0, 0)))
    return pl.pallas_call(
        kernel,
        name=name,
        grid_spec=pltpu.PrefetchScalarGridSpec(
            num_scalar_prefetch=1,
            grid=(4,),
            in_specs=in_specs,
            out_specs=[pl.BlockSpec((rows + extra, width), lambda i, r: (0, 0))] * 2
            + [pl.BlockSpec((1, rows, width), lambda i, r: (jnp.maximum(i - 2, 0), 0, 0))],
        ),
        out_shape=[jax.ShapeDtypeStruct((rows + extra, width), BF)] * 2
        + [jax.ShapeDtypeStruct((2, rows, width), BF)],
        compiler_params=params(32),
        cost_estimate=cost(2 * D * depth * len(rights) * width, 8 << 20),
    )(index, weights, *rights, *(() if row is None else (row,)))


class Reduce:
    def __init__(self, index, parts, row=None):
        self.index, self.row = index, row
        self.sent, self.kept = tuple(parts[:2]), parts[2]
        self.got = [swap(sent, 1) for sent in self.sent]
        self.here, self.there = [], []

    def cross(self, *others):
        rows, width = self.kept.shape[1:]
        extra = self.sent[0].shape[0] - rows
        length = width // 2

        def kernel(kept_ref, got_ref, *refs):
            out = refs[-1]
            out[:rows] = (kept_ref[0].astype(F32) + got_ref[:rows].astype(F32)).astype(BF)
            if extra:
                two = got_ref[rows:].astype(F32)
                out[rows:] = halves(refs[0][...] + two[:1] + two[1:2])

        for place in range(2):
            given = (self.kept, tie(self.got[place], *others))
            given += () if self.row is None else (self.row,)
            tall = pl.BlockSpec((rows + extra, length), lambda i: (0, i))
            kept = pl.BlockSpec((1, rows, length), lambda i, place=place: (place, 0, i))
            found = pl.pallas_call(
                kernel,
                name="core_sum",
                grid=(2,),
                in_specs=[kept, tall]
                + ([] if self.row is None else [pl.BlockSpec((1, length), lambda i: (0, i))]),
                out_specs=tall,
                out_shape=jax.ShapeDtypeStruct((rows + extra, width), BF),
                compiler_params=params(),
                cost_estimate=cost(1 << 28),
            )(*given)
            self.here.append(found)
            self.there.append(swap(found, 2))


class Scatter:
    def __init__(self, index, parts, seqs, row=None):
        self.index, self.row, self.seqs = index, row, seqs
        self.sent, self.kept = tuple(parts[:2]), parts[2]
        self.got = [swap(sent, 1) for sent in self.sent]

    def cross(self, *others):
        seqs, row = self.seqs, self.row
        rows, width = self.kept.shape[1:]
        length = width // seqs
        extra = self.sent[0].shape[0] - rows
        got = (tie(self.got[0], *others), self.got[1])

        def kernel(index_ref, kept_ref, first_ref, second_ref, *refs):
            far, mine = refs[-2:] if row is None else refs[-3:-1]
            chip = index_ref[0] // 2

            def pair(place):
                got = jnp.where(place == 0, first_ref[:rows], second_ref[:rows])
                return kept_ref[place].astype(F32) + got.astype(F32)

            far[0, :rows] = pair(1 - chip).astype(BF)
            mine[0] = pair(chip)
            if row is not None:
                two = first_ref[rows:].astype(F32)
                value = refs[0][...] + two[:1] + two[1:2]
                refs[-1][0] = value
                far[0, rows:] = halves(value)

        def spec(height):
            return pl.BlockSpec((1, height, length), lambda s, r: (s, 0, 0))

        out = [((seqs, rows + extra, length), BF), ((seqs, rows, length), F32)]
        out += [] if row is None else [((seqs, 1, length), F32)]
        in_specs = [pl.BlockSpec((2, rows, length), lambda s, r: (0, 0, s))]
        in_specs += [pl.BlockSpec((rows + extra, length), lambda s, r: (0, s))] * 2
        in_specs += [] if row is None else [pl.BlockSpec((1, length), lambda s, r: (0, s))]
        found = pl.pallas_call(
            kernel,
            name="pair_sum",
            grid_spec=pltpu.PrefetchScalarGridSpec(
                num_scalar_prefetch=1,
                grid=(seqs,),
                in_specs=in_specs,
                out_specs=[spec(shape[1]) for shape, _ in out],
            ),
            out_shape=[jax.ShapeDtypeStruct(*o) for o in out],
            compiler_params=params(),
            cost_estimate=cost(1 << 28),
        )(self.index, self.kept, *got, *(() if row is None else (row,)))
        self.sent_far, self.mine, self.rows = found[0], found[1], rows
        self.half = None if row is None else found[2]
        self.last = swap(self.sent_far, 2)

    def sums(self, *others):
        last = tie(self.last, *others)
        total = self.mine + last[:, : self.rows].astype(F32)
        if self.row is None:
            return total
        two = last[:, self.rows : self.rows + 2].astype(F32)
        return total, self.half + two[:, :1] + two[:, 1:]


def resid_added(index, reduce, own, far, *others):
    seqs, rows, length = own.shape
    width = seqs * length

    def kernel(index_ref, here_0, here_1, there_0, there_1, own_ref, far_ref, resid, both_0, both_1):
        chip = index_ref[0] // 2
        given = (here_0, there_0, both_0), (here_1, there_1, both_1)
        for place, (here, there, both) in enumerate(given):
            mine = chip == place
            base = jnp.where(mine, own_ref[0].astype(F32), far_ref[0].astype(F32))
            value = base + (here[...].astype(F32) + there[...].astype(F32))
            both[...] = value.astype(BF)

            @pl.when(mine)
            def _():
                resid[0] = value

    wide = pl.BlockSpec((rows, length), lambda s, r: (0, s))
    one = pl.BlockSpec((1, rows, length), lambda s, r: (s, 0, 0))
    resid, *both = pl.pallas_call(
        kernel,
        name="resid",
        grid_spec=pltpu.PrefetchScalarGridSpec(
            num_scalar_prefetch=1,
            grid=(seqs,),
            in_specs=[wide] * 4 + [one, one],
            out_specs=[one, wide, wide],
        ),
        out_shape=[jax.ShapeDtypeStruct((seqs, rows, length), F32)]
        + [jax.ShapeDtypeStruct((rows, width), BF)] * 2,
        compiler_params=params(),
        cost_estimate=cost(1 << 28),
    )(index, *reduce.here, tie(reduce.there[0], *others), reduce.there[1], own, far)
    return resid, both


def resid_back(index, reduce, grad_own, grad_far, resid, resid_both, inverse, gains, *others):
    seqs, rows, length = grad_own.shape
    width = seqs * length

    def kernel(index_ref, *refs):
        here, there, held_both, both = refs[:2], refs[2:4], refs[4:6], refs[-3:-1]
        own_ref, far_ref, resid_ref, inverse_ref, own_gain_ref, far_gain_ref, grad = refs[6:13]
        chip = index_ref[0] // 2
        tail = here[0][rows:].astype(F32) + there[0][rows:].astype(F32)
        inv = inverse_ref[0]
        scale = inv * inv * (tail[:1] + tail[1:2]) / D
        own_gain_column = own_gain_ref[...][:, 1:2].astype(F32)
        far_gain_column = far_gain_ref[...][:, 1:2].astype(F32)
        for place in range(2):
            mine = chip == place
            normed = here[place][:rows].astype(F32) + there[place][:rows].astype(F32)
            base = jnp.where(mine, own_ref[0].astype(F32), far_ref[0].astype(F32))
            gain = jnp.where(mine, own_gain_column, far_gain_column)
            most = base + inv * gain * normed
            both[place][...] = (most - held_both[place][...].astype(F32) * scale).astype(BF)

            @pl.when(mine)
            def _():
                held = resid_ref[0]
                grad[0] = most - held * scale
                refs[-1][0] = jnp.sum(held * inv * normed, 1, keepdims=True)

    wide = pl.BlockSpec((rows, length), lambda s, r: (0, s))
    more = pl.BlockSpec((rows + 8, length), lambda s, r: (0, s))
    one = pl.BlockSpec((1, rows, length), lambda s, r: (s, 0, 0))
    row = pl.BlockSpec((1, 1, length), lambda s, r: (s, 0, 0))
    gain = pl.BlockSpec((rows, 2), lambda s, r: (0, 0))
    grad, *both, gain_sum = pl.pallas_call(
        kernel,
        name="resid_back",
        grid_spec=pltpu.PrefetchScalarGridSpec(
            num_scalar_prefetch=1,
            grid=(seqs,),
            in_specs=[more] * 4 + [wide] * 2 + [one, one, one, row, gain, gain],
            out_specs=[one, wide, wide, pl.BlockSpec((1, rows, 1), lambda s, r: (s, 0, 0))],
        ),
        out_shape=[jax.ShapeDtypeStruct((seqs, rows, length), F32)]
        + [jax.ShapeDtypeStruct((rows, width), BF)] * 2
        + [jax.ShapeDtypeStruct((seqs, rows, 1), F32)],
        compiler_params=params(),
        cost_estimate=cost(1 << 28),
    )(
        index,
        *reduce.here,
        tie(reduce.there[0], *others),
        reduce.there[1],
        *resid_both,
        grad_own,
        grad_far,
        resid,
        inverse,
        *gains,
    )
    return grad, both, gain_sum


def gathered_pair(index, here, there, seqs, gains=None, column=0):
    rows, width = here[0].shape
    length = width // seqs
    normed = gains is not None

    def kernel(index_ref, *refs):
        me = index_ref[0]
        chip, core = me // 2, me % 2
        blocks = refs[:2], refs[2:4]
        out = refs[8 if normed else 4]
        if normed:
            total = 0.0
            for ref in refs[:4]:
                value = ref[...].astype(F32)
                total += jnp.sum(value * value, 0, keepdims=True)
            inverse = lax.rsqrt(total / D + EPS)
            refs[9][0] = inverse
            columns = [ref[...][:, column : column + 1].astype(F32) for ref in refs[4:8]]
        for other in range(2):
            for place in range(2):
                value = blocks[other][place][...]
                if normed:
                    gain = jnp.where(chip == place, columns[other], columns[2 + other])
                    value = (value.astype(F32) * inverse * gain).astype(BF)
                row = 2 * place + (core ^ other)
                out[pl.ds(pl.multiple_of(row * rows, 16), rows), :] = value

    wide = pl.BlockSpec((rows, length), lambda s, r: (0, s))
    full = pl.BlockSpec((4 * rows, length), lambda s, r: (0, s))
    row = pl.BlockSpec((1, 1, length), lambda s, r: (s, 0, 0))
    gain = pl.BlockSpec((rows, 2), lambda s, r: (0, 0))
    shape = jax.ShapeDtypeStruct((4 * rows, width), BF)
    inverse = jax.ShapeDtypeStruct((seqs, 1, length), F32)
    return pl.pallas_call(
        kernel,
        name="pair_norm" if normed else "pair",
        grid_spec=pltpu.PrefetchScalarGridSpec(
            num_scalar_prefetch=1,
            grid=(seqs,),
            in_specs=[wide] * 4 + ([gain] * 4 if normed else []),
            out_specs=[full, row] if normed else full,
        ),
        out_shape=[shape, inverse] if normed else shape,
        compiler_params=params(),
        cost_estimate=cost(1 << 30),
    )(index, *here, *there, *(gains if normed else ()))


def ring_order(count):
    half = count // 2
    return [2 * r for r in range(half)] + [2 * r + 1 for r in reversed(range(half))]


def ringed():
    return lax.axis_size("ctx") == 8


def hop(value, step):
    order = ring_order(lax.axis_size("ctx"))
    count = len(order)
    pairs = [(order[r], order[(r + step) % count]) for r in range(count)]
    return lax.ppermute(value, "ctx", pairs)


def places():
    count = lax.axis_size("ctx")
    order = ring_order(count)
    place = {device: r for r, device in enumerate(order)}
    table = [[0] + [order[(place[i] + offset) % count] for offset in OFFSETS] for i in range(count)]
    found = jnp.array(table, jnp.int32)[lax.axis_index("ctx")]
    return found + jnp.where(jnp.arange(len(OFFSETS) + 1) == 0, lax.axis_index("wt"), 0)


class Gather:
    def __init__(self, shard):
        self.shard, self.axis, self.sent = shard, shard.ndim - 2, ()
        self.right, self.left = [shard], [shard]

    def advance(self, *others):
        if not ringed():
            return
        right, left = self.right[-1], self.left[-1]
        if len(self.right) == 4:
            rows = right.shape[self.axis]
            right = lax.slice_in_dim(right, 0, rows // 2, axis=self.axis)
            left = lax.slice_in_dim(left, rows // 2, rows, axis=self.axis)
        others = jax.tree.leaves(others)
        if others:
            right, left = lax.optimization_barrier((right, left, *others))[:2]
        self.sent = right, left
        self.right.append(hop(right, 1))
        self.left.append(hop(left, -1))

    def here(self):
        return (self.right[-1], self.left[-1]) if ringed() else ()

    def full(self, index):
        if not ringed():
            return lax.all_gather(self.shard, "ctx", axis=self.axis, tiled=True)
        rows = self.shard.shape[self.axis]
        pieces = self.right + self.left[1:]
        offsets = (0, -1, -2, -3, 4, 1, 2, 3, 4)
        count = len(pieces)

        def kernel(index_ref, *refs):
            out, sems = refs[count], refs[count + 1]
            copies = []
            for k in range(count):
                first = index_ref[PLACE[offsets[k]]] * rows + (rows // 2 if k == 8 else 0)
                at = pl.ds(pl.multiple_of(first, 16), pieces[k].shape[-2])
                where = out.at[at, :] if len(out.shape) == 2 else out.at[:, at, :]
                copies.append(pltpu.make_async_copy(refs[k], where, sems.at[k]))
                copies[-1].start()
            for copy in copies:
                copy.wait()

        shape = self.shard.shape[:-2] + (rows * 8, self.shard.shape[-1])
        return pl.pallas_call(
            kernel,
            name="assemble",
            in_specs=[SMEM] + [ANY] * count,
            out_specs=WHOLE,
            out_shape=jax.ShapeDtypeStruct(shape, BF),
            scratch_shapes=[pltpu.SemaphoreType.DMA((count,))],
            compiler_params=params(),
            cost_estimate=cost(),
        )(index, *pieces)


def products(lefts, rights, name):
    rows, length = lefts[0].shape
    widths = [r.shape[0] for r in rights]
    used = lefts[:1] if all(left is lefts[0] for left in lefts) else lefts

    def kernel(*refs):
        out = refs[-1]
        first = 0
        for k, width in enumerate(widths):
            left = refs[k if len(used) > 1 else 0]
            out[:, pl.ds(first, width)] = mm_nt(left[...], refs[len(used) + k][...]).astype(BF)
            first += width

    return pl.pallas_call(
        kernel,
        name=name,
        grid=(4,),
        in_specs=[pl.BlockSpec((rows // 4, length), lambda i: (i, 0))] * len(used)
        + [pl.BlockSpec((width, length), lambda i: (0, 0)) for width in widths],
        out_specs=pl.BlockSpec((rows // 4, sum(widths)), lambda i: (i, 0)),
        out_shape=jax.ShapeDtypeStruct((rows, sum(widths)), BF),
        compiler_params=params(32),
        cost_estimate=cost(2 * rows * length * sum(widths), 2 * rows * sum(widths)),
    )(*used, *rights)


class Products:
    def __init__(self, index, full):
        self.index, self.full, self.step, self.sent = index, full, 4, ()
        if ringed():
            self.rows, self.width = full.shape[0] // 8, full.shape[1]
            self._send()

    def _send(self):
        half, step = self.rows // 2, self.step
        first, second = step == 4, step == 3

        def kernel(index_ref, *refs):
            row = pl.program_id(0)
            if first:
                own, right, left = refs

                @pl.when(row == 0)
                def _():
                    right[...] = own[...]

                @pl.when(row == 1)
                def _():
                    left[...] = own[...]

                return
            from_right, from_left, own_right, own_left, right, left = refs
            more_right, more_left = from_right[...].astype(F32), from_left[...].astype(F32)
            if second:
                more_right = jnp.where(row == 0, more_right, 0.0)
                more_left = jnp.where(row == 1, more_left, 0.0)
            right[...] = (own_right[...].astype(F32) + more_right).astype(BF)
            left[...] = (own_left[...].astype(F32) + more_left).astype(BF)

        def own(offset):
            return pl.BlockSpec((half, self.width), lambda i, r: (r[PLACE[offset]] * 2 + i, 0))

        still = pl.BlockSpec((half, self.width), lambda i, r: (0, 0))
        moving = pl.BlockSpec((half, self.width), lambda i, r: (i, 0))
        if first:
            in_specs, out_spec, given, rows = [own(4)], still, (self.full,), half
        else:
            in_specs = [still if second else moving] * 2 + [own(step), own(-step)]
            out_spec, given, rows = moving, (self.right, self.left, self.full, self.full), self.rows
        self.sent = pl.pallas_call(
            kernel,
            name="ring_sum",
            grid_spec=pltpu.PrefetchScalarGridSpec(
                num_scalar_prefetch=1, grid=(2,), in_specs=in_specs, out_specs=[out_spec] * 2
            ),
            out_shape=[jax.ShapeDtypeStruct((rows, self.width), BF)] * 2,
            compiler_params=params(),
            cost_estimate=cost(1 << 24),
        )(self.index, *given)
        self.right, self.left = hop(self.sent[0], 1), hop(self.sent[1], -1)

    def here(self):
        return (self.right, self.left) if ringed() else ()

    def advance(self, *others):
        if ringed():
            self.step -= 1
            self.right = tie(self.right, self.left, *others)
            self._send()

    def final(self, *others):
        if not ringed():
            return lax.psum_scatter(self.full, "ctx", scatter_dimension=0, tiled=True).astype(F32)
        right = tie(self.right, self.left, *others)

        def kernel(index_ref, own, right_ref, left_ref, out):
            out[...] = own[...].astype(F32) + right_ref[...].astype(F32) + left_ref[...].astype(F32)

        half = self.rows // 2
        moving = pl.BlockSpec((half, self.width), lambda i, r: (i, 0))
        own = pl.BlockSpec((half, self.width), lambda i, r: (r[PLACE[0]] * 2 + i, 0))
        return pl.pallas_call(
            kernel,
            name="ring_end",
            grid_spec=pltpu.PrefetchScalarGridSpec(
                num_scalar_prefetch=1, grid=(2,), in_specs=[own, moving, moving], out_specs=moving
            ),
            out_shape=jax.ShapeDtypeStruct((self.rows, self.width), F32),
            compiler_params=params(),
            cost_estimate=cost(1 << 24),
        )(self.index, self.full, right, self.left)


def shifted(value, by):
    count = lax.axis_size("ctx")
    pairs = [(i, i + by) for i in range(count) if 0 <= i + by < count]
    return lax.ppermute(value, "ctx", pairs)


class Before:
    def __init__(self, value, sign):
        self.value, self.sign = value, sign
        self.other = self.one = self.two = self.sent = ()
        if ringed():
            count = lax.axis_size("ctx")
            self.other = lax.ppermute(value, "ctx", [(i, i ^ 1) for i in range(count)])

    def first(self, *others):
        if ringed():
            other = tie(self.other, *others)
            self.total = (self.value.astype(F32) + other.astype(F32)).astype(BF)
            self.one = shifted(self.total, 2 * self.sign)

    def second(self, *others):
        if ringed():
            one = tie(self.one, *others)
            self.sent = (self.total.astype(F32) + one.astype(F32)).astype(BF)
            self.two = shifted(self.sent, 4 * self.sign)

    def result(self):
        count, index = lax.axis_size("ctx"), lax.axis_index("ctx")
        if not ringed():
            everything = lax.all_gather(self.value, "ctx").astype(F32)
            place = jnp.arange(count)
            keep = (place < index) if self.sign > 0 else (place > index)
            keep = keep.reshape((count,) + (1,) * self.value.ndim)
            return jnp.sum(jnp.where(keep, everything, 0.0), 0).astype(BF)
        behind = (index & 1) == (1 if self.sign > 0 else 0)
        result = self.one.astype(F32) + self.two.astype(F32)
        return (result + jnp.where(behind, self.other.astype(F32), 0.0)).astype(BF)


def ctx_total(value):
    if not ringed():
        return lax.psum(value, "ctx")
    for bit in (1, 2, 4):
        value = value + lax.ppermute(value, "ctx", [(i, i ^ bit) for i in range(8)])
    return value


def turned(rows, by):
    return jnp.concatenate([rows[by:], rows[:by]], 0)


def feature_rows(vectors, square, cross, linear):
    length = vectors.shape[1]
    half = FEAT // 2
    pieces = [vectors * vectors * square]
    pieces += [vectors * turned(vectors, by) * cross for by in range(1, half)]
    pieces += [vectors[:half] * vectors[half:] * cross]
    place = lax.broadcasted_iota(jnp.int32, (half, length), 0)
    pieces += [jnp.where(place == 0, 1.0, 0.0), vectors * linear]
    return jnp.concatenate(pieces, 0).astype(BF)


def feature_pull(grad, vectors, square, cross, linear):
    half = FEAT // 2
    total = 2.0 * square * grad[:FEAT] * vectors
    for by in range(1, half):
        part = grad[FEAT * by : FEAT * (by + 1)] * cross
        total += part * turned(vectors, by) + turned(part * vectors, FEAT - by)
    part = grad[FEAT * half : FEAT * half + half] * cross
    total += jnp.concatenate([part * vectors[half:], part * vectors[:half]], 0)
    return total + grad[PHI - FEAT :] * linear


QUERY_SCALE = (1.0 / 32.0, 1.0 / 16.0, 0.25)
KEY_SCALE = (1.0, 1.0, 1.0)


def extended(value, valid):
    place = lax.broadcasted_iota(jnp.int32, (EXT - HEAD_DIM, value.shape[1]), 0)
    tail = jnp.where(place == 0, jnp.broadcast_to(valid, place.shape), 0.0)
    return jnp.concatenate([(value.astype(F32) * valid).astype(BF), tail.astype(BF)], 0)


def causal_of(length):
    key_place = lax.broadcasted_iota(jnp.int32, (length, length), 0)
    query_place = lax.broadcasted_iota(jnp.int32, (length, length), 1)
    return key_place <= query_place


def state_kernel(key_ref, value_ref, valid_ref, state_ref):
    mapped = feature_rows(key_ref[...].astype(F32), *KEY_SCALE)
    state_ref[0, 0] = mm_nt(mapped, extended(value_ref[...], valid_ref[0])).astype(BF)


def attend_kernel(query_ref, key_ref, value_ref, valid_ref, state_ref, mixed_ref, denom_ref):
    query = query_ref[...]
    scores = mm_tn(key_ref[...], query) * 0.25
    weights = jnp.where(causal_of(query.shape[1]), 1.0 + scores + 0.5 * scores * scores, 0.0)
    total = mm_nn(extended(value_ref[...], valid_ref[0]), weights.astype(BF))
    mapped = feature_rows(query.astype(F32), *QUERY_SCALE)
    total += mm_tn(state_ref[0, 0], mapped)
    denom = total[HEAD_DIM : HEAD_DIM + 1]
    denom_ref[0, 0] = denom
    mixed_ref[...] = (total[:HEAD_DIM] / denom).astype(BF)


def spread_kernel(query_ref, grad_ref, mixed_ref, denom_ref, weighted_ref, state_ref):
    weighted = grad_ref[...].astype(F32) / denom_ref[0, 0]
    shift = jnp.sum(weighted * mixed_ref[...].astype(F32), 0, keepdims=True)
    place = lax.broadcasted_iota(jnp.int32, (EXT - HEAD_DIM, weighted.shape[1]), 0)
    tail = jnp.where(place == 0, -jnp.broadcast_to(shift, place.shape), 0.0)
    whole = jnp.concatenate([weighted, tail], 0).astype(BF)
    weighted_ref[0, 0] = whole
    mapped = feature_rows(query_ref[...].astype(F32), *QUERY_SCALE)
    state_ref[0, 0] = mm_nt(mapped, whole).astype(BF)


def local_kernel(
    query_ref, key_ref, value_ref, valid_ref, state_ref, weighted_ref, dq_ref, dk_ref, dv_ref
):
    query, key_in, weighted = query_ref[...], key_ref[...], weighted_ref[0, 0]
    causal = causal_of(query.shape[1])
    scores = mm_tn(key_in, query) * 0.25
    weights = jnp.where(causal, 1.0 + scores + 0.5 * scores * scores, 0.0).astype(BF)
    dv_ref[...] = mm_nt(weighted[:HEAD_DIM], weights) * valid_ref[0]
    slope = mm_tn(extended(value_ref[...], valid_ref[0]), weighted)
    slope = jnp.where(causal, slope * (1.0 + scores), 0.0).astype(BF)
    mapped = mm_nn(state_ref[0, 0], weighted)
    pulled = feature_pull(mapped, query.astype(F32), *QUERY_SCALE)
    dq_ref[...] = (mm_nn(key_in, slope) * 0.25 + pulled).astype(BF)
    dk_ref[...] = mm_nt(query, slope) * 0.25


def later_kernel(heads, key_ref, value_ref, valid_ref, state_ref, dq_in, dk_in, dv_in, out_ref):
    head = pl.program_id(1)
    key_in = key_ref[...].astype(F32)
    valid = valid_ref[0]
    mapped = mm_nn(state_ref[0, 0], extended(value_ref[...], valid))
    d_key = (dk_in[...] + feature_pull(mapped, key_in, *KEY_SCALE)).astype(BF)
    spread = mm_tn(state_ref[0, 0], feature_rows(key_in, *KEY_SCALE))
    d_value = (dv_in[...] + spread[:HEAD_DIM] * valid).astype(BF)
    values, queries = heads * HEAD_DIM, heads * FEAT
    out_ref[pl.ds(pl.multiple_of(head * HEAD_DIM, 16), HEAD_DIM), :] = d_value
    out_ref[pl.ds(pl.multiple_of(values + head * FEAT, 16), FEAT), :] = dq_in[...]
    out_ref[pl.ds(pl.multiple_of(values + queries + head * FEAT, 16), FEAT), :] = d_key


def head_call(kernel, name, seqs, heads, length, ins, outs, flops):
    first_query = heads * HEAD_DIM // FEAT
    columns = heads * (HEAD_DIM + 2 * FEAT)
    specs = {
        "value": pl.BlockSpec((HEAD_DIM, length), lambda s, h: (h, s)),
        "query": pl.BlockSpec((FEAT, length), lambda s, h: (first_query + h, s)),
        "key": pl.BlockSpec((FEAT, length), lambda s, h: (first_query + heads + h, s)),
        "all": pl.BlockSpec((columns, length), lambda s, h: (0, s)),
        "feat": pl.BlockSpec((FEAT, length), lambda s, h: (h, s)),
        "head": pl.BlockSpec((HEAD_DIM, length), lambda s, h: (h, s)),
        "valid": pl.BlockSpec((1, 1, length), lambda s, h: (s, 0, 0)),
        "state": pl.BlockSpec((1, 1, PHI, EXT), lambda s, h: (s, h, 0, 0)),
        "row": pl.BlockSpec((1, 1, 1, length), lambda s, h: (s, h, 0, 0)),
        "ext": pl.BlockSpec((1, 1, EXT, length), lambda s, h: (s, h, 0, 0)),
    }
    shapes = {
        "all": (columns, seqs * length),
        "feat": (heads * FEAT, seqs * length),
        "head": (heads * HEAD_DIM, seqs * length),
        "state": (seqs, heads, PHI, EXT),
        "row": (seqs, heads, 1, length),
        "ext": (seqs, heads, EXT, length),
    }
    return pl.pallas_call(
        kernel,
        name=name,
        grid=(seqs, heads),
        in_specs=[specs[i] for i in ins],
        out_specs=[specs[o] for o, _ in outs],
        out_shape=[jax.ShapeDtypeStruct(shapes[o], kind) for o, kind in outs],
        compiler_params=params(),
        cost_estimate=cost(flops),
    )


def body(
    hidden_in,
    lengths,
    gain_attn,
    gain_ffn,
    w_query,
    w_key,
    w_value,
    w_output,
    w_gate,
    w_up,
    w_down,
    cotangent,
):
    seqs, length, width = hidden_in.shape
    heads = w_value.shape[1] // HEAD_DIM
    hidden_units = w_gate.shape[1]
    columns = heads * (HEAD_DIM + 2 * FEAT)
    index = places()
    position = lax.axis_index("ctx") * length + jnp.arange(length, dtype=jnp.int32)
    valid = (position[None, :] < lengths[:, None]).astype(F32)[:, None, :]
    hidden = hidden_in.transpose(0, 2, 1)
    unit = seqs * heads * 2 * length * length * 256
    token = [jnp.zeros((8, 128), F32)]

    def call(kernel, name, ins, outs, share):
        return head_call(kernel, name, seqs, heads, length, ins, outs, int(unit * share))

    def turn(value, *others):
        return tie(value, token[0], *others)

    def fence(*values):
        token[0] = tie(token[0], *values)

    ring_attn = Gather(jnp.concatenate([w_value, w_query, w_key, w_output.T], 1))
    ring_down = Gather(w_down.T)
    ring_gate_up = Gather(jnp.stack([w_gate, w_up]))
    ring_attn.advance()
    spread_in = Spread(hidden)
    gains = Spread(jnp.stack([gain_attn, gain_ffn], 1))
    gains.cross()
    fence(ring_attn.here())
    ring_attn.advance(*token)
    fence(ring_attn.here(), ring_gate_up.shard)
    ring_attn.advance(*token)
    spread_in.cross(*token)
    grad_out = (cotangent.transpose(0, 2, 1).astype(F32) * valid).astype(BF)
    spread_out = Spread(tie(grad_out, spread_in.far))
    fence(ring_attn.here())
    ring_attn.advance(*token)
    ring_gate_up.advance(ring_attn.sent)
    fence(spread_in.near, spread_in.both)
    blocks = spread_in.blocks()
    normed_one, inv_one = gathered(index, (turn(blocks[0]),) + blocks[1:], gains.blocks(), 0)
    fence(normed_one)
    fence(ring_attn.here())
    w_attn = ring_attn.full(turn(index))

    qkv = mm_tn(w_attn[:, :columns], normed_one).astype(BF)
    (own,) = call(state_kernel, "state", ("key", "value", "valid"), (("state", BF),), 0.5)(
        qkv, qkv, valid
    )
    before = Before(own, 1)
    fence(own)
    fence(before.other)
    before.first(*token)
    fence(before.total if ringed() else ())
    fence(ring_gate_up.here())
    ring_gate_up.advance(*token)
    fence(before.one)
    before.second(*token)
    fence(before.sent)
    ring_down.advance(*token)
    spread_out.cross(*token)
    fence(ring_gate_up.here())
    ring_gate_up.advance(*token)

    state = before.result()
    mixed, denom = call(
        attend_kernel,
        "attend",
        ("query", "key", "value", "valid", "state"),
        (("head", BF), ("row", F32)),
        1,
    )(turn(qkv), qkv, qkv, valid, state)
    fence(ring_down.here())
    scatter_attn = Scatter(
        index, projected(index, w_attn, [turn(mixed)], "out_proj", columns), seqs
    )
    fence(scatter_attn.sent)
    fence(ring_gate_up.here())
    scatter_attn.cross(*token)
    fence(scatter_attn.sent_far)
    blocks = spread_out.blocks()
    grad_out_full = gathered(index, (turn(blocks[0]),) + blocks[1:])
    fence(grad_out_full)
    fence(ring_gate_up.here())
    ring_gate_up.advance(*token)
    ring_down.advance(*token)
    resid = hidden.astype(F32) + scatter_attn.sums(*token)
    spread_resid = Spread(resid.astype(BF))
    fence(spread_resid.block)
    fence(ring_gate_up.here(), ring_down.here())
    ring_down.advance(*token)
    gate_up = ring_gate_up.full(turn(index))
    fence(gate_up)
    fence(ring_down.here())
    ring_down.advance(*token)
    spread_resid.cross(*token)

    blocks = spread_resid.blocks()
    normed_two, inv_two = gathered(index, blocks, gains.blocks(), 1)
    fence(normed_two)
    gate = mm_tn(gate_up[0], turn(normed_two))
    up = mm_tn(gate_up[1], normed_two)
    act = (gate * jax.nn.sigmoid(gate) * up).astype(BF)
    fence(act)
    fence(ring_down.here())
    down_full = ring_down.full(turn(index))
    fence(down_full)

    sig = jax.nn.sigmoid(gate)
    d_act = mm_tn(down_full, turn(grad_out_full))
    g_gate = (d_act * up * sig * (1.0 + gate * (1.0 - sig))).astype(BF)
    g_up = (d_act * gate * sig).astype(BF)
    inner = jnp.sum(g_gate.astype(F32) * gate + g_up.astype(F32) * up, 0, keepdims=True)
    fence(g_gate, g_up)
    scatter_two = Scatter(
        index, projected(index, gate_up, [turn(g_gate), g_up], "ffn_back", row=inner), seqs, inner
    )
    fence(scatter_two.sent)
    down_ring = Products(index, products([turn(grad_out_full)], [act], "down_grad"))
    fence(down_ring.sent)
    scatter_two.cross(*token)
    fence(scatter_two.sent_far)
    gate_up_ring = Products(
        index, products([normed_two, normed_two], [turn(g_gate), g_up], "gate_up_grad")
    )
    fence(gate_up_ring.sent)
    fence(down_ring.here())
    down_ring.advance(*token)
    fence(down_ring.sent)

    gain_one, gain_two = gain_attn.astype(F32)[:, None], gain_ffn.astype(F32)[:, None]
    d_norm, inner = scatter_two.sums(*token)
    gain_two_part = jnp.sum(resid * inv_two * d_norm, (0, 2))
    d_resid = (
        grad_out.astype(F32)
        + inv_two * gain_two * d_norm
        - resid * (inv_two * inv_two * inner / D)
    )
    spread_grad = Spread(d_resid.astype(BF))
    fence(spread_grad.block)
    fence(gate_up_ring.here())
    gate_up_ring.advance(*token)
    fence(gate_up_ring.sent)
    ffn_out = projected(index, down_full, [turn(act)], "ffn_out")
    fence(ffn_out)
    fence(down_ring.here())
    down_ring.advance(*token)
    fence(down_ring.sent)
    spread_grad.cross(*token)
    blocks = spread_grad.blocks()
    resid_full = gathered(index, blocks)
    fence(resid_full)
    g_attn = mm_tn(w_attn[:, columns:], turn(resid_full)).astype(BF)
    weighted, spread = call(
        spread_kernel, "spread", ("query", "head", "head", "row"), (("ext", BF), ("state", BF)), 0.5
    )(turn(qkv), g_attn, mixed, denom)
    after = Before(spread, -1)
    fence(spread)
    fence(gate_up_ring.here())
    fence(after.other)
    after.first(*token)
    fence(after.total if ringed() else ())
    local = call(
        local_kernel,
        "local",
        ("query", "key", "value", "valid", "state", "ext"),
        (("feat", BF), ("feat", F32), ("head", F32)),
        2,
    )(turn(qkv), qkv, qkv, valid, state, weighted)
    fence(local)
    scatter_out = Scatter(index, [*lax.optimization_barrier((*ffn_out, *token))[:3]], seqs)
    fence(after.one)
    after.second(*token)
    fence(after.sent)
    gate_up_ring.advance(*token)
    fence(gate_up_ring.sent)

    fence(down_ring.here())
    down_ring.advance(*token)
    fence(down_ring.sent)

    def later(*refs):
        later_kernel(heads, *refs)

    (d_qkv,) = call(
        later,
        "later",
        ("key", "value", "valid", "state", "feat", "feat", "head"),
        (("all", BF),),
        0.5,
    )(turn(qkv), qkv, valid, after.result(), *local)
    inner = jnp.sum(d_qkv.astype(F32) * qkv.astype(F32), 0, keepdims=True)
    scatter_one = Scatter(
        index, projected(index, w_attn, [d_qkv], "qkv_back", row=inner), seqs, inner
    )
    fence(scatter_one.sent)
    attn_ring = Products(
        index, products([turn(normed_one), resid_full], [d_qkv, mixed], "attn_grad")
    )
    fence(attn_ring.sent)
    scatter_out.cross(*token)
    fence(scatter_out.sent_far)
    fence(gate_up_ring.here())
    gate_up_ring.advance(*token)
    fence(gate_up_ring.sent)
    scatter_one.cross(*token)
    fence(scatter_one.sent_far)
    fence(attn_ring.here())
    attn_ring.advance(*token)
    fence(attn_ring.sent)
    layer_out = (resid + scatter_out.sums(*token)).astype(BF)
    fence(layer_out)
    d_norm, inner = scatter_one.sums(*token)
    value = hidden.astype(F32)
    gain_one_part = jnp.sum(value * inv_one * d_norm, (0, 2))
    grad_input = (
        d_resid + inv_one * gain_one * d_norm - value * (inv_one * inv_one * inner / D)
    )
    fence(gain_one_part, grad_input)
    gain_grads = ctx_total(jnp.stack([gain_one_part, gain_two_part]) + token[0][:1, :1])
    fence(attn_ring.here())
    attn_ring.advance(*token)
    fence(attn_ring.sent)
    down_grad = down_ring.final(*token)
    fence(down_grad)
    fence(attn_ring.here())
    attn_ring.advance(*token)
    fence(attn_ring.sent)
    gate_up_grad = gate_up_ring.final(*token)
    fence(gate_up_grad)
    fence(gain_grads)
    attn_grad = attn_ring.final(*token)

    values, queries = heads * HEAD_DIM, heads * FEAT
    return (
        layer_out.transpose(0, 2, 1),
        grad_input.transpose(0, 2, 1),
        gain_grads[0],
        gain_grads[1],
        attn_grad[:, values : values + queries],
        attn_grad[:, values + queries : columns],
        attn_grad[:, :values],
        attn_grad[:, columns:].T,
        gate_up_grad[:, :hidden_units],
        gate_up_grad[:, hidden_units:],
        down_grad.T,
    )


def solution(mesh):
    acts, rows, columns = P(None, "ctx", "wt"), P("ctx", "wt"), P("wt", "ctx")
    in_specs = (acts, P(), P("wt"), P("wt"), rows, rows, rows, columns, rows, rows, columns, acts)
    out_specs = (acts, acts, P("wt"), P("wt"), rows, rows, rows, columns, rows, rows, columns)
    return jax.shard_map(body, mesh=mesh, in_specs=in_specs, out_specs=out_specs, check_vma=False)
```

```python
import jax
import jax.numpy as jnp
from jax import lax
from jax.experimental import pallas as pl
from jax.experimental.pallas import tpu as pltpu
from jax.sharding import PartitionSpec as P


D = 1792
FEAT = 16
HEAD_DIM = 112
EXT = 128
PHI = 160
EPS = 1e-05
BF = jnp.bfloat16
F32 = jnp.float32
ANY = pl.BlockSpec(memory_space=pl.ANY)
WHOLE = pl.BlockSpec(memory_space=pltpu.VMEM)
SMEM = pl.BlockSpec(memory_space=pltpu.SMEM)
OFFSETS = (0, 1, 2, 3, 4, -1, -2, -3)
PLACE = {offset: 1 + k for k, offset in enumerate(OFFSETS)}
PLACE[-4] = PLACE[4]


def mm_nn(left, right):
    return lax.dot_general(left, right, (((1,), (0,)), ((), ())), preferred_element_type=F32)


def mm_tn(left, right):
    return lax.dot_general(left, right, (((0,), (0,)), ((), ())), preferred_element_type=F32)


def mm_nt(left, right):
    return lax.dot_general(left, right, (((1,), (1,)), ((), ())), preferred_element_type=F32)


def tie(value, *others):
    others = jax.tree.leaves(others)
    return lax.optimization_barrier((value, *others))[0] if others else value


def params(mib=24):
    return pltpu.CompilerParams(vmem_limit_bytes=mib << 20)


def cost(flops=0, moved=4 << 20):
    return pl.CostEstimate(flops=flops, bytes_accessed=moved, transcendentals=0)


def swap(value, bit):
    count = lax.axis_size("wt")
    return lax.ppermute(value, "wt", [(i, i ^ bit) for i in range(count)])


class Spread:
    def __init__(self, block):
        self.block, self.far, self.near = block, swap(block, 2), swap(block, 1)

    def cross(self, *others):
        self.far = tie(self.far, *others)
        self.both = swap(self.far, 1)

    def blocks(self):
        return self.block, self.near, self.far, self.both


def gathered(index, blocks, gains=None, column=0):
    seqs, rows, length = blocks[0].shape

    def kernel(index_ref, *refs):
        values = [ref[0] for ref in refs[:4]]
        out = refs[8 if gains is not None else 4]
        if gains is not None:
            values = [v.astype(F32) for v in values]
            total = sum(jnp.sum(v * v, 0, keepdims=True) for v in values)
            inverse = lax.rsqrt(total / D + EPS)
            refs[9][0] = inverse
            scaled = []
            for v, gain_ref in zip(values, refs[4:8]):
                gain = gain_ref[...][:, column : column + 1].astype(F32)
                scaled.append((v * inverse * gain).astype(BF))
            values = scaled
        me = index_ref[0]
        for bit in range(4):
            out[pl.ds(pl.multiple_of((me ^ bit) * rows, 16), rows), :] = values[bit]

    block = pl.BlockSpec((1, rows, length), lambda s, index_ref: (s, 0, 0))
    full = pl.BlockSpec((4 * rows, length), lambda s, index_ref: (0, s))
    row = pl.BlockSpec((1, 1, length), lambda s, index_ref: (s, 0, 0))
    gain = pl.BlockSpec((rows, 2), lambda s, index_ref: (0, 0))
    shape = jax.ShapeDtypeStruct((4 * rows, seqs * length), BF)
    inverse = jax.ShapeDtypeStruct((seqs, 1, length), F32)
    normed = gains is not None
    return pl.pallas_call(
        kernel,
        name="gather_norm" if normed else "gather",
        grid_spec=pltpu.PrefetchScalarGridSpec(
            num_scalar_prefetch=1,
            grid=(seqs,),
            in_specs=[block] * 4 + ([gain] * 4 if normed else []),
            out_specs=[full, row] if normed else full,
        ),
        out_shape=[shape, inverse] if normed else shape,
        compiler_params=params(),
        cost_estimate=cost(1 << 30),
    )(index, *blocks, *(gains if normed else ()))


def halves(value):
    high = value.astype(BF).astype(F32)
    place = lax.broadcasted_iota(jnp.int32, (8, value.shape[1]), 0)
    return jnp.where(place == 0, high, jnp.where(place == 1, value - high, 0.0)).astype(BF)


def projected(index, weights, rights, name, columns=None, row=None):
    rows = D // 4
    depth, width = rights[0].shape
    extra = 0 if row is None else 8
    start = 0 if columns is None else columns
    stacked = weights.ndim == 3

    def kernel(index_ref, weight_ref, *refs):
        right_refs = refs[: len(rights)]
        kept = refs[-1]
        total = 0.0
        for k, right in enumerate(right_refs):
            left = weight_ref[k] if stacked else weight_ref[...][:, start : start + depth]
            total += mm_nn(left, right[...])
        step = pl.program_id(0)
        total = total.astype(BF)

        def send(sent):
            sent[:rows] = total
            if row is not None:
                sent[rows:] = halves(refs[len(rights)][...])

        for place in range(2):
            pl.when(step == place)(lambda place=place: send(refs[place - 3]))

        @pl.when(step >= 2)
        def _():
            kept[0] = total

    def of(i, index_ref):
        core = index_ref[0] % 2
        return (i % 2) * 2 + jnp.where(i < 2, 1 - core, core)

    if stacked:
        left_spec = pl.BlockSpec((len(rights), rows, depth), lambda i, r: (0, of(i, r), 0))
    else:
        left_spec = pl.BlockSpec((rows, weights.shape[1]), lambda i, r: (of(i, r), 0))
    in_specs = [left_spec] + [pl.BlockSpec((depth, width), lambda i, r: (0, 0))] * len(rights)
    if row is not None:
        in_specs.append(pl.BlockSpec((1, width), lambda i, r: (0, 0)))
    return pl.pallas_call(
        kernel,
        name=name,
        grid_spec=pltpu.PrefetchScalarGridSpec(
            num_scalar_prefetch=1,
            grid=(4,),
            in_specs=in_specs,
            out_specs=[pl.BlockSpec((rows + extra, width), lambda i, r: (0, 0))] * 2
            + [pl.BlockSpec((1, rows, width), lambda i, r: (jnp.maximum(i - 2, 0), 0, 0))],
        ),
        out_shape=[jax.ShapeDtypeStruct((rows + extra, width), BF)] * 2
        + [jax.ShapeDtypeStruct((2, rows, width), BF)],
        compiler_params=params(32),
        cost_estimate=cost(2 * D * depth * len(rights) * width, 8 << 20),
    )(index, weights, *rights, *(() if row is None else (row,)))


class Reduce:
    def __init__(self, index, parts, row=None):
        self.index, self.row = index, row
        self.sent, self.kept = tuple(parts[:2]), parts[2]
        self.got = [swap(sent, 1) for sent in self.sent]
        self.here, self.there = [], []

    def cross(self, *others):
        rows, width = self.kept.shape[1:]
        extra = self.sent[0].shape[0] - rows
        length = width // 2

        def kernel(kept_ref, got_ref, *refs):
            out = refs[-1]
            out[:rows] = (kept_ref[0].astype(F32) + got_ref[:rows].astype(F32)).astype(BF)
            if extra:
                two = got_ref[rows:].astype(F32)
                out[rows:] = halves(refs[0][...] + two[:1] + two[1:2])

        for place in range(2):
            given = (self.kept, tie(self.got[place], *others))
            given += () if self.row is None else (self.row,)
            tall = pl.BlockSpec((rows + extra, length), lambda i: (0, i))
            kept = pl.BlockSpec((1, rows, length), lambda i, place=place: (place, 0, i))
            found = pl.pallas_call(
                kernel,
                name="core_sum",
                grid=(2,),
                in_specs=[kept, tall]
                + ([] if self.row is None else [pl.BlockSpec((1, length), lambda i: (0, i))]),
                out_specs=tall,
                out_shape=jax.ShapeDtypeStruct((rows + extra, width), BF),
                compiler_params=params(),
                cost_estimate=cost(1 << 28),
            )(*given)
            self.here.append(found)
            self.there.append(swap(found, 2))


class Scatter:
    def __init__(self, index, parts, seqs, row=None):
        self.index, self.row, self.seqs = index, row, seqs
        self.sent, self.kept = tuple(parts[:2]), parts[2]
        self.got = [swap(sent, 1) for sent in self.sent]

    def cross(self, *others):
        seqs, row = self.seqs, self.row
        rows, width = self.kept.shape[1:]
        length = width // seqs
        extra = self.sent[0].shape[0] - rows
        got = (tie(self.got[0], *others), self.got[1])

        def kernel(index_ref, kept_ref, first_ref, second_ref, *refs):
            far, mine = refs[-2:] if row is None else refs[-3:-1]
            chip = index_ref[0] // 2

            def pair(place):
                got = jnp.where(place == 0, first_ref[:rows], second_ref[:rows])
                return kept_ref[place].astype(F32) + got.astype(F32)

            far[0, :rows] = pair(1 - chip).astype(BF)
            mine[0] = pair(chip)
            if row is not None:
                two = first_ref[rows:].astype(F32)
                value = refs[0][...] + two[:1] + two[1:2]
                refs[-1][0] = value
                far[0, rows:] = halves(value)

        def spec(height):
            return pl.BlockSpec((1, height, length), lambda s, r: (s, 0, 0))

        out = [((seqs, rows + extra, length), BF), ((seqs, rows, length), F32)]
        out += [] if row is None else [((seqs, 1, length), F32)]
        in_specs = [pl.BlockSpec((2, rows, length), lambda s, r: (0, 0, s))]
        in_specs += [pl.BlockSpec((rows + extra, length), lambda s, r: (0, s))] * 2
        in_specs += [] if row is None else [pl.BlockSpec((1, length), lambda s, r: (0, s))]
        found = pl.pallas_call(
            kernel,
            name="pair_sum",
            grid_spec=pltpu.PrefetchScalarGridSpec(
                num_scalar_prefetch=1,
                grid=(seqs,),
                in_specs=in_specs,
                out_specs=[spec(shape[1]) for shape, _ in out],
            ),
            out_shape=[jax.ShapeDtypeStruct(*o) for o in out],
            compiler_params=params(),
            cost_estimate=cost(1 << 28),
        )(self.index, self.kept, *got, *(() if row is None else (row,)))
        self.sent_far, self.mine, self.rows = found[0], found[1], rows
        self.half = None if row is None else found[2]
        self.last = swap(self.sent_far, 2)

    def sums(self, *others):
        last = tie(self.last, *others)
        total = self.mine + last[:, : self.rows].astype(F32)
        if self.row is None:
            return total
        two = last[:, self.rows : self.rows + 2].astype(F32)
        return total, self.half + two[:, :1] + two[:, 1:]


def resid_added(index, reduce, own, far, *others):
    seqs, rows, length = own.shape
    width = seqs * length

    def kernel(index_ref, here_0, here_1, there_0, there_1, own_ref, far_ref, resid, both_0, both_1):
        chip = index_ref[0] // 2
        given = (here_0, there_0, both_0), (here_1, there_1, both_1)
        for place, (here, there, both) in enumerate(given):
            mine = chip == place
            base = jnp.where(mine, own_ref[0].astype(F32), far_ref[0].astype(F32))
            value = base + (here[...].astype(F32) + there[...].astype(F32))
            both[...] = value.astype(BF)

            @pl.when(mine)
            def _():
                resid[0] = value

    wide = pl.BlockSpec((rows, length), lambda s, r: (0, s))
    one = pl.BlockSpec((1, rows, length), lambda s, r: (s, 0, 0))
    resid, *both = pl.pallas_call(
        kernel,
        name="resid",
        grid_spec=pltpu.PrefetchScalarGridSpec(
            num_scalar_prefetch=1,
            grid=(seqs,),
            in_specs=[wide] * 4 + [one, one],
            out_specs=[one, wide, wide],
        ),
        out_shape=[jax.ShapeDtypeStruct((seqs, rows, length), F32)]
        + [jax.ShapeDtypeStruct((rows, width), BF)] * 2,
        compiler_params=params(),
        cost_estimate=cost(1 << 28),
    )(index, *reduce.here, tie(reduce.there[0], *others), reduce.there[1], own, far)
    return resid, both


def resid_back(index, reduce, grad_own, grad_far, resid, resid_both, inverse, gains, *others):
    seqs, rows, length = grad_own.shape
    width = seqs * length

    def kernel(index_ref, *refs):
        here, there, held_both, both = refs[:2], refs[2:4], refs[4:6], refs[-3:-1]
        own_ref, far_ref, resid_ref, inverse_ref, own_gain_ref, far_gain_ref, grad = refs[6:13]
        chip = index_ref[0] // 2
        tail = here[0][rows:].astype(F32) + there[0][rows:].astype(F32)
        inv = inverse_ref[0]
        scale = inv * inv * (tail[:1] + tail[1:2]) / D
        own_gain_column = own_gain_ref[...][:, 1:2].astype(F32)
        far_gain_column = far_gain_ref[...][:, 1:2].astype(F32)
        for place in range(2):
            mine = chip == place
            normed = here[place][:rows].astype(F32) + there[place][:rows].astype(F32)
            base = jnp.where(mine, own_ref[0].astype(F32), far_ref[0].astype(F32))
            gain = jnp.where(mine, own_gain_column, far_gain_column)
            most = base + inv * gain * normed
            both[place][...] = (most - held_both[place][...].astype(F32) * scale).astype(BF)

            @pl.when(mine)
            def _():
                held = resid_ref[0]
                grad[0] = most - held * scale
                refs[-1][0] = jnp.sum(held * inv * normed, 1, keepdims=True)

    wide = pl.BlockSpec((rows, length), lambda s, r: (0, s))
    more = pl.BlockSpec((rows + 8, length), lambda s, r: (0, s))
    one = pl.BlockSpec((1, rows, length), lambda s, r: (s, 0, 0))
    row = pl.BlockSpec((1, 1, length), lambda s, r: (s, 0, 0))
    gain = pl.BlockSpec((rows, 2), lambda s, r: (0, 0))
    grad, *both, gain_sum = pl.pallas_call(
        kernel,
        name="resid_back",
        grid_spec=pltpu.PrefetchScalarGridSpec(
            num_scalar_prefetch=1,
            grid=(seqs,),
            in_specs=[more] * 4 + [wide] * 2 + [one, one, one, row, gain, gain],
            out_specs=[one, wide, wide, pl.BlockSpec((1, rows, 1), lambda s, r: (s, 0, 0))],
        ),
        out_shape=[jax.ShapeDtypeStruct((seqs, rows, length), F32)]
        + [jax.ShapeDtypeStruct((rows, width), BF)] * 2
        + [jax.ShapeDtypeStruct((seqs, rows, 1), F32)],
        compiler_params=params(),
        cost_estimate=cost(1 << 28),
    )(
        index,
        *reduce.here,
        tie(reduce.there[0], *others),
        reduce.there[1],
        *resid_both,
        grad_own,
        grad_far,
        resid,
        inverse,
        *gains,
    )
    return grad, both, gain_sum


def gathered_pair(index, here, there, seqs, gains=None, column=0):
    rows, width = here[0].shape
    length = width // seqs
    normed = gains is not None

    def kernel(index_ref, *refs):
        me = index_ref[0]
        chip, core = me // 2, me % 2
        blocks = refs[:2], refs[2:4]
        out = refs[8 if normed else 4]
        if normed:
            total = 0.0
            for ref in refs[:4]:
                value = ref[...].astype(F32)
                total += jnp.sum(value * value, 0, keepdims=True)
            inverse = lax.rsqrt(total / D + EPS)
            refs[9][0] = inverse
            columns = [ref[...][:, column : column + 1].astype(F32) for ref in refs[4:8]]
        for other in range(2):
            for place in range(2):
                value = blocks[other][place][...]
                if normed:
                    gain = jnp.where(chip == place, columns[other], columns[2 + other])
                    value = (value.astype(F32) * inverse * gain).astype(BF)
                row = 2 * place + (core ^ other)
                out[pl.ds(pl.multiple_of(row * rows, 16), rows), :] = value

    wide = pl.BlockSpec((rows, length), lambda s, r: (0, s))
    full = pl.BlockSpec((4 * rows, length), lambda s, r: (0, s))
    row = pl.BlockSpec((1, 1, length), lambda s, r: (s, 0, 0))
    gain = pl.BlockSpec((rows, 2), lambda s, r: (0, 0))
    shape = jax.ShapeDtypeStruct((4 * rows, width), BF)
    inverse = jax.ShapeDtypeStruct((seqs, 1, length), F32)
    return pl.pallas_call(
        kernel,
        name="pair_norm" if normed else "pair",
        grid_spec=pltpu.PrefetchScalarGridSpec(
            num_scalar_prefetch=1,
            grid=(seqs,),
            in_specs=[wide] * 4 + ([gain] * 4 if normed else []),
            out_specs=[full, row] if normed else full,
        ),
        out_shape=[shape, inverse] if normed else shape,
        compiler_params=params(),
        cost_estimate=cost(1 << 30),
    )(index, *here, *there, *(gains if normed else ()))


def ring_order(count):
    half = count // 2
    return [2 * r for r in range(half)] + [2 * r + 1 for r in reversed(range(half))]


def ringed():
    return lax.axis_size("ctx") == 8


def hop(value, step):
    order = ring_order(lax.axis_size("ctx"))
    count = len(order)
    pairs = [(order[r], order[(r + step) % count]) for r in range(count)]
    return lax.ppermute(value, "ctx", pairs)


def places():
    count = lax.axis_size("ctx")
    order = ring_order(count)
    place = {device: r for r, device in enumerate(order)}
    table = [[0] + [order[(place[i] + offset) % count] for offset in OFFSETS] for i in range(count)]
    found = jnp.array(table, jnp.int32)[lax.axis_index("ctx")]
    return found + jnp.where(jnp.arange(len(OFFSETS) + 1) == 0, lax.axis_index("wt"), 0)


class Gather:
    def __init__(self, shard):
        self.shard, self.axis, self.sent = shard, shard.ndim - 2, ()
        self.right, self.left = [shard], [shard]

    def advance(self, *others):
        if not ringed():
            return
        right, left = self.right[-1], self.left[-1]
        if len(self.right) == 4:
            rows = right.shape[self.axis]
            right = lax.slice_in_dim(right, 0, rows // 2, axis=self.axis)
            left = lax.slice_in_dim(left, rows // 2, rows, axis=self.axis)
        others = jax.tree.leaves(others)
        if others:
            right, left = lax.optimization_barrier((right, left, *others))[:2]
        self.sent = right, left
        self.right.append(hop(right, 1))
        self.left.append(hop(left, -1))

    def here(self):
        return (self.right[-1], self.left[-1]) if ringed() else ()

    def full(self, index):
        if not ringed():
            return lax.all_gather(self.shard, "ctx", axis=self.axis, tiled=True)
        rows = self.shard.shape[self.axis]
        pieces = self.right + self.left[1:]
        offsets = (0, -1, -2, -3, 4, 1, 2, 3, 4)
        count = len(pieces)

        def kernel(index_ref, *refs):
            out, sems = refs[count], refs[count + 1]
            copies = []
            for k in range(count):
                first = index_ref[PLACE[offsets[k]]] * rows + (rows // 2 if k == 8 else 0)
                at = pl.ds(pl.multiple_of(first, 16), pieces[k].shape[-2])
                where = out.at[at, :] if len(out.shape) == 2 else out.at[:, at, :]
                copies.append(pltpu.make_async_copy(refs[k], where, sems.at[k]))
                copies[-1].start()
            for copy in copies:
                copy.wait()

        shape = self.shard.shape[:-2] + (rows * 8, self.shard.shape[-1])
        return pl.pallas_call(
            kernel,
            name="assemble",
            in_specs=[SMEM] + [ANY] * count,
            out_specs=WHOLE,
            out_shape=jax.ShapeDtypeStruct(shape, BF),
            scratch_shapes=[pltpu.SemaphoreType.DMA((count,))],
            compiler_params=params(),
            cost_estimate=cost(),
        )(index, *pieces)


def products(lefts, rights, name):
    rows, length = lefts[0].shape
    widths = [r.shape[0] for r in rights]
    used = lefts[:1] if all(left is lefts[0] for left in lefts) else lefts

    def kernel(*refs):
        out = refs[-1]
        first = 0
        for k, width in enumerate(widths):
            left = refs[k if len(used) > 1 else 0]
            out[:, pl.ds(first, width)] = mm_nt(left[...], refs[len(used) + k][...]).astype(BF)
            first += width

    return pl.pallas_call(
        kernel,
        name=name,
        grid=(4,),
        in_specs=[pl.BlockSpec((rows // 4, length), lambda i: (i, 0))] * len(used)
        + [pl.BlockSpec((width, length), lambda i: (0, 0)) for width in widths],
        out_specs=pl.BlockSpec((rows // 4, sum(widths)), lambda i: (i, 0)),
        out_shape=jax.ShapeDtypeStruct((rows, sum(widths)), BF),
        compiler_params=params(32),
        cost_estimate=cost(2 * rows * length * sum(widths), 2 * rows * sum(widths)),
    )(*used, *rights)


class Products:
    def __init__(self, index, full):
        self.index, self.full, self.step, self.sent = index, full, 4, ()
        if ringed():
            self.rows, self.width = full.shape[0] // 8, full.shape[1]
            self._send()

    def _send(self):
        half, step = self.rows // 2, self.step
        first, second = step == 4, step == 3

        def kernel(index_ref, *refs):
            row = pl.program_id(0)
            if first:
                own, right, left = refs

                @pl.when(row == 0)
                def _():
                    right[...] = own[...]

                @pl.when(row == 1)
                def _():
                    left[...] = own[...]

                return
            from_right, from_left, own_right, own_left, right, left = refs
            more_right, more_left = from_right[...].astype(F32), from_left[...].astype(F32)
            if second:
                more_right = jnp.where(row == 0, more_right, 0.0)
                more_left = jnp.where(row == 1, more_left, 0.0)
            right[...] = (own_right[...].astype(F32) + more_right).astype(BF)
            left[...] = (own_left[...].astype(F32) + more_left).astype(BF)

        def own(offset):
            return pl.BlockSpec((half, self.width), lambda i, r: (r[PLACE[offset]] * 2 + i, 0))

        still = pl.BlockSpec((half, self.width), lambda i, r: (0, 0))
        moving = pl.BlockSpec((half, self.width), lambda i, r: (i, 0))
        if first:
            in_specs, out_spec, given, rows = [own(4)], still, (self.full,), half
        else:
            in_specs = [still if second else moving] * 2 + [own(step), own(-step)]
            out_spec, given, rows = moving, (self.right, self.left, self.full, self.full), self.rows
        self.sent = pl.pallas_call(
            kernel,
            name="ring_sum",
            grid_spec=pltpu.PrefetchScalarGridSpec(
                num_scalar_prefetch=1, grid=(2,), in_specs=in_specs, out_specs=[out_spec] * 2
            ),
            out_shape=[jax.ShapeDtypeStruct((rows, self.width), BF)] * 2,
            compiler_params=params(),
            cost_estimate=cost(1 << 24),
        )(self.index, *given)
        self.right, self.left = hop(self.sent[0], 1), hop(self.sent[1], -1)

    def here(self):
        return (self.right, self.left) if ringed() else ()

    def advance(self, *others):
        if ringed():
            self.step -= 1
            self.right = tie(self.right, self.left, *others)
            self._send()

    def final(self, *others):
        if not ringed():
            return lax.psum_scatter(self.full, "ctx", scatter_dimension=0, tiled=True).astype(F32)
        right = tie(self.right, self.left, *others)

        def kernel(index_ref, own, right_ref, left_ref, out):
            out[...] = own[...].astype(F32) + right_ref[...].astype(F32) + left_ref[...].astype(F32)

        half = self.rows // 2
        moving = pl.BlockSpec((half, self.width), lambda i, r: (i, 0))
        own = pl.BlockSpec((half, self.width), lambda i, r: (r[PLACE[0]] * 2 + i, 0))
        return pl.pallas_call(
            kernel,
            name="ring_end",
            grid_spec=pltpu.PrefetchScalarGridSpec(
                num_scalar_prefetch=1, grid=(2,), in_specs=[own, moving, moving], out_specs=moving
            ),
            out_shape=jax.ShapeDtypeStruct((self.rows, self.width), F32),
            compiler_params=params(),
            cost_estimate=cost(1 << 24),
        )(self.index, self.full, right, self.left)


def shifted(value, by):
    count = lax.axis_size("ctx")
    pairs = [(i, i + by) for i in range(count) if 0 <= i + by < count]
    return lax.ppermute(value, "ctx", pairs)


class Before:
    def __init__(self, value, sign):
        self.value, self.sign = value, sign
        self.other = self.one = self.two = self.sent = ()
        if ringed():
            count = lax.axis_size("ctx")
            self.other = lax.ppermute(value, "ctx", [(i, i ^ 1) for i in range(count)])

    def first(self, *others):
        if ringed():
            other = tie(self.other, *others)
            self.total = (self.value.astype(F32) + other.astype(F32)).astype(BF)
            self.one = shifted(self.total, 2 * self.sign)

    def second(self, *others):
        if ringed():
            one = tie(self.one, *others)
            self.sent = (self.total.astype(F32) + one.astype(F32)).astype(BF)
            self.two = shifted(self.sent, 4 * self.sign)

    def result(self):
        count, index = lax.axis_size("ctx"), lax.axis_index("ctx")
        if not ringed():
            everything = lax.all_gather(self.value, "ctx").astype(F32)
            place = jnp.arange(count)
            keep = (place < index) if self.sign > 0 else (place > index)
            keep = keep.reshape((count,) + (1,) * self.value.ndim)
            return jnp.sum(jnp.where(keep, everything, 0.0), 0).astype(BF)
        behind = (index & 1) == (1 if self.sign > 0 else 0)
        result = self.one.astype(F32) + self.two.astype(F32)
        return (result + jnp.where(behind, self.other.astype(F32), 0.0)).astype(BF)


def ctx_total(value):
    if not ringed():
        return lax.psum(value, "ctx")
    for bit in (1, 2, 4):
        value = value + lax.ppermute(value, "ctx", [(i, i ^ bit) for i in range(8)])
    return value


def turned(rows, by):
    return jnp.concatenate([rows[by:], rows[:by]], 0)


def feature_rows(vectors, square, cross, linear):
    length = vectors.shape[1]
    half = FEAT // 2
    pieces = [vectors * vectors * square]
    pieces += [vectors * turned(vectors, by) * cross for by in range(1, half)]
    pieces += [vectors[:half] * vectors[half:] * cross]
    place = lax.broadcasted_iota(jnp.int32, (half, length), 0)
    pieces += [jnp.where(place == 0, 1.0, 0.0), vectors * linear]
    return jnp.concatenate(pieces, 0).astype(BF)


def feature_pull(grad, vectors, square, cross, linear):
    half = FEAT // 2
    total = 2.0 * square * grad[:FEAT] * vectors
    for by in range(1, half):
        part = grad[FEAT * by : FEAT * (by + 1)] * cross
        total += part * turned(vectors, by) + turned(part * vectors, FEAT - by)
    part = grad[FEAT * half : FEAT * half + half] * cross
    total += jnp.concatenate([part * vectors[half:], part * vectors[:half]], 0)
    return total + grad[PHI - FEAT :] * linear


QUERY_SCALE = (1.0 / 32.0, 1.0 / 16.0, 0.25)
KEY_SCALE = (1.0, 1.0, 1.0)


def extended(value, valid):
    place = lax.broadcasted_iota(jnp.int32, (EXT - HEAD_DIM, value.shape[1]), 0)
    tail = jnp.where(place == 0, jnp.broadcast_to(valid, place.shape), 0.0)
    return jnp.concatenate([(value.astype(F32) * valid).astype(BF), tail.astype(BF)], 0)


def causal_of(length):
    key_place = lax.broadcasted_iota(jnp.int32, (length, length), 0)
    query_place = lax.broadcasted_iota(jnp.int32, (length, length), 1)
    return key_place <= query_place


def state_kernel(key_ref, value_ref, valid_ref, state_ref):
    mapped = feature_rows(key_ref[...].astype(F32), *KEY_SCALE)
    state_ref[0, 0] = mm_nt(mapped, extended(value_ref[...], valid_ref[0])).astype(BF)


def attend_kernel(query_ref, key_ref, value_ref, valid_ref, state_ref, mixed_ref, denom_ref):
    query = query_ref[...]
    scores = mm_tn(key_ref[...], query) * 0.25
    weights = jnp.where(causal_of(query.shape[1]), 1.0 + scores + 0.5 * scores * scores, 0.0)
    total = mm_nn(extended(value_ref[...], valid_ref[0]), weights.astype(BF))
    mapped = feature_rows(query.astype(F32), *QUERY_SCALE)
    total += mm_tn(state_ref[0, 0], mapped)
    denom = total[HEAD_DIM : HEAD_DIM + 1]
    denom_ref[0, 0] = denom
    mixed_ref[...] = (total[:HEAD_DIM] / denom).astype(BF)


def spread_kernel(query_ref, grad_ref, mixed_ref, denom_ref, weighted_ref, state_ref):
    weighted = grad_ref[...].astype(F32) / denom_ref[0, 0]
    shift = jnp.sum(weighted * mixed_ref[...].astype(F32), 0, keepdims=True)
    place = lax.broadcasted_iota(jnp.int32, (EXT - HEAD_DIM, weighted.shape[1]), 0)
    tail = jnp.where(place == 0, -jnp.broadcast_to(shift, place.shape), 0.0)
    whole = jnp.concatenate([weighted, tail], 0).astype(BF)
    weighted_ref[0, 0] = whole
    mapped = feature_rows(query_ref[...].astype(F32), *QUERY_SCALE)
    state_ref[0, 0] = mm_nt(mapped, whole).astype(BF)


def local_kernel(
    query_ref, key_ref, value_ref, valid_ref, state_ref, weighted_ref, dq_ref, dk_ref, dv_ref
):
    query, key_in, weighted = query_ref[...], key_ref[...], weighted_ref[0, 0]
    causal = causal_of(query.shape[1])
    scores = mm_tn(key_in, query) * 0.25
    weights = jnp.where(causal, 1.0 + scores + 0.5 * scores * scores, 0.0).astype(BF)
    dv_ref[...] = mm_nt(weighted[:HEAD_DIM], weights) * valid_ref[0]
    slope = mm_tn(extended(value_ref[...], valid_ref[0]), weighted)
    slope = jnp.where(causal, slope * (1.0 + scores), 0.0).astype(BF)
    mapped = mm_nn(state_ref[0, 0], weighted)
    pulled = feature_pull(mapped, query.astype(F32), *QUERY_SCALE)
    dq_ref[...] = (mm_nn(key_in, slope) * 0.25 + pulled).astype(BF)
    dk_ref[...] = mm_nt(query, slope) * 0.25


def later_kernel(heads, key_ref, value_ref, valid_ref, state_ref, dq_in, dk_in, dv_in, out_ref):
    head = pl.program_id(1)
    key_in = key_ref[...].astype(F32)
    valid = valid_ref[0]
    mapped = mm_nn(state_ref[0, 0], extended(value_ref[...], valid))
    d_key = (dk_in[...] + feature_pull(mapped, key_in, *KEY_SCALE)).astype(BF)
    spread = mm_tn(state_ref[0, 0], feature_rows(key_in, *KEY_SCALE))
    d_value = (dv_in[...] + spread[:HEAD_DIM] * valid).astype(BF)
    values, queries = heads * HEAD_DIM, heads * FEAT
    out_ref[pl.ds(pl.multiple_of(head * HEAD_DIM, 16), HEAD_DIM), :] = d_value
    out_ref[pl.ds(pl.multiple_of(values + head * FEAT, 16), FEAT), :] = dq_in[...]
    out_ref[pl.ds(pl.multiple_of(values + queries + head * FEAT, 16), FEAT), :] = d_key


def head_call(kernel, name, seqs, heads, length, ins, outs, flops):
    first_query = heads * HEAD_DIM // FEAT
    columns = heads * (HEAD_DIM + 2 * FEAT)
    specs = {
        "value": pl.BlockSpec((HEAD_DIM, length), lambda s, h: (h, s)),
        "query": pl.BlockSpec((FEAT, length), lambda s, h: (first_query + h, s)),
        "key": pl.BlockSpec((FEAT, length), lambda s, h: (first_query + heads + h, s)),
        "all": pl.BlockSpec((columns, length), lambda s, h: (0, s)),
        "feat": pl.BlockSpec((FEAT, length), lambda s, h: (h, s)),
        "head": pl.BlockSpec((HEAD_DIM, length), lambda s, h: (h, s)),
        "valid": pl.BlockSpec((1, 1, length), lambda s, h: (s, 0, 0)),
        "state": pl.BlockSpec((1, 1, PHI, EXT), lambda s, h: (s, h, 0, 0)),
        "row": pl.BlockSpec((1, 1, 1, length), lambda s, h: (s, h, 0, 0)),
        "ext": pl.BlockSpec((1, 1, EXT, length), lambda s, h: (s, h, 0, 0)),
    }
    shapes = {
        "all": (columns, seqs * length),
        "feat": (heads * FEAT, seqs * length),
        "head": (heads * HEAD_DIM, seqs * length),
        "state": (seqs, heads, PHI, EXT),
        "row": (seqs, heads, 1, length),
        "ext": (seqs, heads, EXT, length),
    }
    return pl.pallas_call(
        kernel,
        name=name,
        grid=(seqs, heads),
        in_specs=[specs[i] for i in ins],
        out_specs=[specs[o] for o, _ in outs],
        out_shape=[jax.ShapeDtypeStruct(shapes[o], kind) for o, kind in outs],
        compiler_params=params(),
        cost_estimate=cost(flops),
    )


def body(
    hidden_in,
    lengths,
    gain_attn,
    gain_ffn,
    w_query,
    w_key,
    w_value,
    w_output,
    w_gate,
    w_up,
    w_down,
    cotangent,
):
    seqs, length, width = hidden_in.shape
    heads = w_value.shape[1] // HEAD_DIM
    hidden_units = w_gate.shape[1]
    columns = heads * (HEAD_DIM + 2 * FEAT)
    index = places()
    position = lax.axis_index("ctx") * length + jnp.arange(length, dtype=jnp.int32)
    valid = (position[None, :] < lengths[:, None]).astype(F32)[:, None, :]
    hidden = hidden_in.transpose(0, 2, 1)
    unit = seqs * heads * 2 * length * length * 256
    token = [jnp.zeros((8, 128), F32)]

    def call(kernel, name, ins, outs, share):
        return head_call(kernel, name, seqs, heads, length, ins, outs, int(unit * share))

    def turn(value, *others):
        return tie(value, token[0], *others)

    def fence(*values):
        token[0] = tie(token[0], *values)

    ring_attn = Gather(jnp.concatenate([w_value, w_query, w_key, w_output.T], 1))
    ring_down = Gather(w_down.T)
    ring_gate_up = Gather(jnp.stack([w_gate, w_up]))
    ring_attn.advance()
    spread_in = Spread(hidden)
    gains = Spread(jnp.stack([gain_attn, gain_ffn], 1))
    gains.cross()
    fence(ring_attn.here())
    ring_attn.advance(*token)
    fence(ring_attn.here(), ring_gate_up.shard)
    ring_attn.advance(*token)
    spread_in.cross(*token)
    grad_out = (cotangent.transpose(0, 2, 1).astype(F32) * valid).astype(BF)
    spread_out = Spread(tie(grad_out, spread_in.far))
    fence(ring_attn.here())
    ring_attn.advance(*token)
    ring_gate_up.advance(ring_attn.sent)
    fence(spread_in.near, spread_in.both)
    blocks = spread_in.blocks()
    normed_one, inv_one = gathered(index, (turn(blocks[0]),) + blocks[1:], gains.blocks(), 0)
    fence(normed_one)
    fence(ring_attn.here())
    w_attn = ring_attn.full(turn(index))

    qkv = mm_tn(w_attn[:, :columns], normed_one).astype(BF)
    (own,) = call(state_kernel, "state", ("key", "value", "valid"), (("state", BF),), 0.5)(
        qkv, qkv, valid
    )
    before = Before(own, 1)
    fence(own)
    fence(before.other)
    before.first(*token)
    fence(before.total if ringed() else ())
    fence(ring_gate_up.here())
    ring_gate_up.advance(*token)
    fence(before.one)
    before.second(*token)
    fence(before.sent)
    ring_down.advance(*token)
    spread_out.cross(*token)
    fence(ring_gate_up.here())
    ring_gate_up.advance(*token)

    state = before.result()
    mixed, denom = call(
        attend_kernel,
        "attend",
        ("query", "key", "value", "valid", "state"),
        (("head", BF), ("row", F32)),
        1,
    )(turn(qkv), qkv, qkv, valid, state)
    fence(ring_down.here())
    scatter_attn = Scatter(
        index, projected(index, w_attn, [turn(mixed)], "out_proj", columns), seqs
    )
    fence(scatter_attn.sent)
    fence(ring_gate_up.here())
    scatter_attn.cross(*token)
    fence(scatter_attn.sent_far)
    blocks = spread_out.blocks()
    grad_out_full = gathered(index, (turn(blocks[0]),) + blocks[1:])
    fence(grad_out_full)
    fence(ring_gate_up.here())
    ring_gate_up.advance(*token)
    ring_down.advance(*token)
    resid = hidden.astype(F32) + scatter_attn.sums(*token)
    spread_resid = Spread(resid.astype(BF))
    fence(spread_resid.block)
    fence(ring_gate_up.here(), ring_down.here())
    ring_down.advance(*token)
    gate_up = ring_gate_up.full(turn(index))
    fence(gate_up)
    fence(ring_down.here())
    ring_down.advance(*token)
    spread_resid.cross(*token)

    blocks = spread_resid.blocks()
    normed_two, inv_two = gathered(index, blocks, gains.blocks(), 1)
    fence(normed_two)
    gate = mm_tn(gate_up[0], turn(normed_two))
    up = mm_tn(gate_up[1], normed_two)
    act = (gate * jax.nn.sigmoid(gate) * up).astype(BF)
    fence(act)
    fence(ring_down.here())
    down_full = ring_down.full(turn(index))
    fence(down_full)

    sig = jax.nn.sigmoid(gate)
    d_act = mm_tn(down_full, turn(grad_out_full))
    g_gate = (d_act * up * sig * (1.0 + gate * (1.0 - sig))).astype(BF)
    g_up = (d_act * gate * sig).astype(BF)
    inner = jnp.sum(g_gate.astype(F32) * gate + g_up.astype(F32) * up, 0, keepdims=True)
    fence(g_gate, g_up)
    scatter_two = Scatter(
        index, projected(index, gate_up, [turn(g_gate), g_up], "ffn_back", row=inner), seqs, inner
    )
    fence(scatter_two.sent)
    down_ring = Products(index, products([turn(grad_out_full)], [act], "down_grad"))
    fence(down_ring.sent)
    scatter_two.cross(*token)
    fence(scatter_two.sent_far)
    gate_up_ring = Products(
        index, products([normed_two, normed_two], [turn(g_gate), g_up], "gate_up_grad")
    )
    fence(gate_up_ring.sent)
    fence(down_ring.here())
    down_ring.advance(*token)
    fence(down_ring.sent)

    gain_one, gain_two = gain_attn.astype(F32)[:, None], gain_ffn.astype(F32)[:, None]
    d_norm, inner = scatter_two.sums(*token)
    gain_two_part = jnp.sum(resid * inv_two * d_norm, (0, 2))
    d_resid = (
        grad_out.astype(F32)
        + inv_two * gain_two * d_norm
        - resid * (inv_two * inv_two * inner / D)
    )
    spread_grad = Spread(d_resid.astype(BF))
    fence(spread_grad.block)
    fence(gate_up_ring.here())
    gate_up_ring.advance(*token)
    fence(gate_up_ring.sent)
    ffn_out = projected(index, down_full, [turn(act)], "ffn_out")
    fence(ffn_out)
    fence(down_ring.here())
    down_ring.advance(*token)
    fence(down_ring.sent)
    spread_grad.cross(*token)
    blocks = spread_grad.blocks()
    resid_full = gathered(index, blocks)
    fence(resid_full)
    g_attn = mm_tn(w_attn[:, columns:], turn(resid_full)).astype(BF)
    weighted, spread = call(
        spread_kernel, "spread", ("query", "head", "head", "row"), (("ext", BF), ("state", BF)), 0.5
    )(turn(qkv), g_attn, mixed, denom)
    after = Before(spread, -1)
    fence(spread)
    fence(gate_up_ring.here())
    fence(after.other)
    after.first(*token)
    fence(after.total if ringed() else ())
    local = call(
        local_kernel,
        "local",
        ("query", "key", "value", "valid", "state", "ext"),
        (("feat", BF), ("feat", F32), ("head", F32)),
        2,
    )(turn(qkv), qkv, qkv, valid, state, weighted)
    fence(local)
    scatter_out = Scatter(index, [*lax.optimization_barrier((*ffn_out, *token))[:3]], seqs)
    fence(after.one)
    after.second(*token)
    fence(after.sent)
    gate_up_ring.advance(*token)
    fence(gate_up_ring.sent)

    fence(down_ring.here())
    down_ring.advance(*token)
    fence(down_ring.sent)

    def later(*refs):
        later_kernel(heads, *refs)

    (d_qkv,) = call(
        later,
        "later",
        ("key", "value", "valid", "state", "feat", "feat", "head"),
        (("all", BF),),
        0.5,
    )(turn(qkv), qkv, valid, after.result(), *local)
    inner = jnp.sum(d_qkv.astype(F32) * qkv.astype(F32), 0, keepdims=True)
    scatter_one = Scatter(
        index, projected(index, w_attn, [d_qkv], "qkv_back", row=inner), seqs, inner
    )
    fence(scatter_one.sent)
    attn_ring = Products(
        index, products([turn(normed_one), resid_full], [d_qkv, mixed], "attn_grad")
    )
    fence(attn_ring.sent)
    scatter_out.cross(*token)
    fence(scatter_out.sent_far)
    fence(gate_up_ring.here())
    gate_up_ring.advance(*token)
    fence(gate_up_ring.sent)
    scatter_one.cross(*token)
    fence(scatter_one.sent_far)
    fence(attn_ring.here())
    attn_ring.advance(*token)
    fence(attn_ring.sent)
    d_norm, inner = scatter_one.sums(*token)
    value = hidden.astype(F32)
    gain_one_part = jnp.sum(value * inv_one * d_norm, (0, 2))
    grad_input = (
        d_resid + inv_one * gain_one * d_norm - value * (inv_one * inv_one * inner / D)
    )
    fence(gain_one_part, grad_input)
    layer_out = (resid + scatter_out.sums(*token)).astype(BF)
    fence(layer_out)
    gain_grads = ctx_total(jnp.stack([gain_one_part, gain_two_part]) + token[0][:1, :1])
    fence(attn_ring.here())
    attn_ring.advance(*token)
    fence(attn_ring.sent)
    down_grad = down_ring.final(*token)
    fence(down_grad)
    fence(attn_ring.here())
    attn_ring.advance(*token)
    fence(attn_ring.sent)
    gate_up_grad = gate_up_ring.final(*token)
    fence(gate_up_grad)
    fence(gain_grads)
    attn_grad = attn_ring.final(*token)

    values, queries = heads * HEAD_DIM, heads * FEAT
    return (
        layer_out.transpose(0, 2, 1),
        grad_input.transpose(0, 2, 1),
        gain_grads[0],
        gain_grads[1],
        attn_grad[:, values : values + queries],
        attn_grad[:, values + queries : columns],
        attn_grad[:, :values],
        attn_grad[:, columns:].T,
        gate_up_grad[:, :hidden_units],
        gate_up_grad[:, hidden_units:],
        down_grad.T,
    )


def solution(mesh):
    acts, rows, columns = P(None, "ctx", "wt"), P("ctx", "wt"), P("wt", "ctx")
    in_specs = (acts, P(), P("wt"), P("wt"), rows, rows, rows, columns, rows, rows, columns, acts)
    out_specs = (acts, acts, P("wt"), P("wt"), rows, rows, rows, columns, rows, rows, columns)
    return jax.shard_map(body, mesh=mesh, in_specs=in_specs, out_specs=out_specs, check_vma=False)
```
